32 devices in a mesh: sec: 2 (over core), lat: 8 (over z, y), head: 2 (over x).
Axes of the slice: x: 2, y: 2, z: 4, core: 2. Of those that a mesh axis runs over, the one named last changes fastest.
Arguments:
- fields: bfloat16 [2, 96, 96, 192], P(None, 'lat', ('sec', 'head')), may hold values from -6 to 6
- land_sea: int32 [96, 96], P('lat', ('sec', 'head')), may hold values 0 or 1
- land_embed: float32 [192], replicated, may hold values from -4 to 4
- bias_index: int32 [144, 144], replicated, may hold values from 0 to 3311
- fine_bias: float32 [2, 6, 3312], replicated, may hold values from -4 to 254
- fine_gains: float32 [2, 2, 192], replicated, may hold values from 0.1 to 1.9
- fine_query_key_value: bfloat16 [2, 192, 576], replicated, may hold values from -0.4375 to 0.4375
- fine_project: bfloat16 [2, 192, 192], replicated, may hold values from -0.4375 to 0.4375
- fine_widen: bfloat16 [2, 192, 768], replicated, may hold values from -0.4375 to 0.4375
- fine_narrow: bfloat16 [2, 768, 192], replicated, may hold values from -0.21875 to 0.21875
- merge_gain: float32 [768], replicated, may hold values from 0.1 to 1.9
- merge_weight: bfloat16 [768, 384], replicated, may hold values from -0.21875 to 0.21875
- coarse_bias: float32 [2, 12, 3312], replicated, may hold values from -4 to 254
- coarse_gains: float32 [2, 2, 384], replicated, may hold values from 0.1 to 1.9
- coarse_query_key_value: bfloat16 [2, 384, 1152], replicated, may hold values from -0.3125 to 0.3125
- coarse_project: bfloat16 [2, 384, 384], replicated, may hold values from -0.3125 to 0.3125
- coarse_widen: bfloat16 [2, 384, 1536], replicated, may hold values from -0.3125 to 0.3125
- coarse_narrow: bfloat16 [2, 1536, 384], replicated, may hold values from -0.15625 to 0.15625
- expand_weight: bfloat16 [384, 768], replicated, may hold values from -0.3125 to 0.3125
- expand_gain: float32 [192], replicated, may hold values from 0.1 to 1.9
Outputs:
- forecast: bfloat16 [2, 96, 96, 192], P(None, 'lat', ('sec', 'head'))
The draws below stay inside these ranges and needn't reach their ends.
All inputs are finite; a program needn't handle non-finite values. No bound on the sum of `land_sea` on one device may be relied on, other than what follows from the above.
Results may differ from the reference program's by a relative error of at most 0.019.
Values may be sent and summed in bfloat16 or wider, within the bound.
No kernel may reach another device: no remote copies, remote signals or barrier semaphores. Data moves between devices by JAX's collectives and lax.ppermute only.
A program may use at most 128 MiB of HBM per device.

```python
import jax
import jax.numpy as jnp
from jax import lax

C = 192
CC = 384
HF = 6
HC = 12
FFF = 768
FFC = 1536
LEVELS = 2
WIN_LAT = 6
WIN_LON = 12
WIN_TOK = 144
BIAS_LEN = 3312
NLAT = 96
NLON = 96


def bias_law(key, shape):
    pieces = jax.random.split(key, 1)
    return jnp.clip(jax.random.normal(pieces[0], shape, jnp.float32), -4.0, 4.0)


def draw_fine_bias(key, part):
    return bias_law(jax.random.fold_in(key, 11), (2, HF, BIAS_LEN))


def draw_coarse_bias(key, part):
    return bias_law(jax.random.fold_in(key, 23), (2, HC, BIAS_LEN))


def draw_bias_index(key, part):
    entry_count = WIN_TOK * WIN_TOK
    pieces = jax.random.split(jax.random.fold_in(key, 37), 3)
    entries = jax.random.randint(pieces[0], (entry_count,), 0, BIAS_LEN)
    low_place = jax.random.randint(pieces[1], (), 0, entry_count)
    high_place = (low_place + 1 + jax.random.randint(pieces[2], (), 0, entry_count - 1)) % entry_count
    entries = entries.at[low_place].set(0).at[high_place].set(BIAS_LEN - 1)
    return entries.reshape(WIN_TOK, WIN_TOK).astype(jnp.int32)


def plant(values, own_key, smallest, largest):
    place = [jax.random.randint(jax.random.fold_in(own_key, axis), (), 0, length) for axis, length in enumerate(values.shape)]
    main_axis = values.shape.index(max(values.shape))
    next_to = place[:main_axis] + [(place[main_axis] + 1) % values.shape[main_axis]] + place[main_axis + 1:]
    return values.at[tuple(place)].set(smallest).at[tuple(next_to)].set(largest)


def block_levels(stream_key, shape, shards, least, high):
    factor_of, own = 1.0, jax.random.fold_in(stream_key, 6)
    for dim, shards_of in shards:
        heights = jnp.exp(jax.random.uniform(jax.random.fold_in(own, dim), (shards_of,), jnp.float32, least / len(shards), high / len(shards)))
        factor_of = factor_of * jnp.repeat(heights, shape[dim] // shards_of).reshape([-1 if axis == dim else 1 for axis in range(len(shape))])
    return factor_of


def bell_draw(stream_key, dims, deviation, bound, cuts=(), held_as=jnp.bfloat16):
    values = jax.random.normal(stream_key, dims, jnp.float32) * deviation
    if len(cuts) > 0:
        values = block_levels(stream_key, dims, cuts, -0.22, 0.18) * values
    return jnp.clip(values, min=-bound, max=bound).astype(held_as)


def setup_inputs(seed: int = 0) -> dict:
    keys = jax.random.split(jax.random.key(seed), 21)
    fields = bell_draw(keys[0], (LEVELS, NLAT, NLON, C), 1.0, 6.0, ((1, 8), (2, 4)))
    land_sea = plant((jax.random.randint(keys[1], (NLAT, NLON), 0, 10) < 3).astype(jnp.int32), jax.random.fold_in(keys[1], 1), 0, 1)
    land_embed = bell_draw(keys[2], (C,), 1.0, 4.0, (), jnp.float32)
    bias_index = draw_bias_index(jax.random.fold_in(keys[20], 71), 0)
    fine_bias = draw_fine_bias(jax.random.fold_in(keys[20], 71), 0)
    fine_gains = jnp.clip(1.0 + 0.18 * jax.random.normal(keys[5], (2, 2, C), jnp.float32), 0.1, 1.9)
    fine_query_key_value = bell_draw(keys[6], (2, C, 3 * C), C ** -0.5, 0.4375)
    fine_project = bell_draw(keys[7], (2, C, C), C ** -0.5, 0.4375)
    fine_widen = bell_draw(keys[8], (2, C, FFF), C ** -0.5, 0.4375)
    fine_narrow = bell_draw(keys[9], (2, FFF, C), FFF ** -0.5, 0.21875)
    merge_gain = jnp.clip(1.0 + 0.18 * jax.random.normal(keys[10], (4 * C,), jnp.float32), 0.1, 1.9)
    merge_weight = bell_draw(keys[11], (4 * C, CC), (4 * C) ** -0.5, 0.21875)
    coarse_bias = draw_coarse_bias(jax.random.fold_in(keys[20], 71), 0)
    coarse_gains = jnp.clip(1.0 + 0.18 * jax.random.normal(keys[13], (2, 2, CC), jnp.float32), 0.1, 1.9)
    coarse_query_key_value = bell_draw(keys[14], (2, CC, 3 * CC), CC ** -0.5, 0.3125)
    coarse_project = bell_draw(keys[15], (2, CC, CC), CC ** -0.5, 0.3125)
    coarse_widen = bell_draw(keys[16], (2, CC, FFC), CC ** -0.5, 0.3125)
    coarse_narrow = bell_draw(keys[17], (2, FFC, CC), FFC ** -0.5, 0.15625)
    expand_weight = bell_draw(keys[18], (CC, 4 * C), CC ** -0.5, 0.3125)
    expand_gain = jnp.clip(1.0 + 0.18 * jax.random.normal(keys[19], (C,), jnp.float32), 0.1, 1.9)
    return {"fields": fields, "land_sea": land_sea, "land_embed": land_embed, "bias_index": bias_index, "fine_bias": fine_bias, "fine_gains": fine_gains, "fine_query_key_value": fine_query_key_value, "fine_project": fine_project, "fine_widen": fine_widen, "fine_narrow": fine_narrow, "merge_gain": merge_gain, "merge_weight": merge_weight, "coarse_bias": coarse_bias, "coarse_gains": coarse_gains, "coarse_query_key_value": coarse_query_key_value, "coarse_project": coarse_project, "coarse_widen": coarse_widen, "coarse_narrow": coarse_narrow, "expand_weight": expand_weight, "expand_gain": expand_gain}


def layer_norm(values, norm_gain):
    as_float = values.astype(jnp.float32)
    average = lax.optimization_barrier(jnp.mean(as_float, axis=-1, keepdims=True))
    centered = as_float - average
    variance = lax.optimization_barrier(jnp.mean(centered * centered, axis=-1, keepdims=True))
    return centered * lax.rsqrt(variance + 1e-05) * norm_gain

def attend(normed, w_triple, position_bias, region, head_count):
    level_count, row_count, col_count, channels = normed.shape
    head_size = channels // head_count
    lat_windows = row_count // WIN_LAT
    lon_windows = col_count // WIN_LON
    triple = jnp.dot(normed.reshape(-1, channels), w_triple, preferred_element_type=jnp.float32).astype(jnp.bfloat16)
    triple = triple.reshape(level_count, lat_windows, WIN_LAT, lon_windows, WIN_LON, 3, head_count, head_size)
    triple = triple.transpose(5, 1, 3, 6, 0, 2, 4, 7).reshape(3, lat_windows, lon_windows, head_count, WIN_TOK, head_size)
    triple = triple.astype(jnp.float32)
    scores = jnp.einsum('abhqd,abhkd->abhqk', triple[0], triple[1])
    scores = scores * head_size ** (-0.5) + position_bias
    if region is not None:
        token_region = jnp.broadcast_to(region.reshape(lat_windows, 1, WIN_LAT, 1), (lat_windows, level_count, WIN_LAT, WIN_LON)).reshape(lat_windows, WIN_TOK)
        same_region = token_region[:, :, None] == token_region[:, None, :]
        scores = jnp.where(same_region[:, None, None], scores, -1e+30)
    attention = jax.nn.softmax(scores, axis=-1).astype(jnp.bfloat16)
    context = jnp.einsum('abhqk,abhkd->abhqd', attention.astype(jnp.float32), triple[2]).astype(jnp.bfloat16)
    context = context.reshape(lat_windows, lon_windows, head_count, level_count, WIN_LAT, WIN_LON, head_size)
    return context.transpose(3, 0, 4, 1, 5, 2, 6).reshape(level_count, row_count, col_count, channels)

def finish(stream, context, norm_gains, w_project, w_widen, w_narrow):
    channels = stream.shape[-1]
    flat_stream = stream.reshape(-1, channels)
    projected = jnp.dot(context.reshape(-1, channels), w_project, preferred_element_type=jnp.float32)
    middle = lax.optimization_barrier((flat_stream.astype(jnp.float32) + projected).astype(jnp.bfloat16))
    normed = layer_norm(middle, norm_gains[1]).astype(jnp.bfloat16)
    hidden = jax.nn.gelu(jnp.dot(normed, w_widen, preferred_element_type=jnp.float32), approximate=False).astype(jnp.bfloat16)
    result = (middle.astype(jnp.float32) + jnp.dot(hidden, w_narrow, preferred_element_type=jnp.float32)).astype(jnp.bfloat16)
    return lax.optimization_barrier(result).reshape(stream.shape)

def reference_block(stream, shifted, position_bias, norm_gains, w_triple, w_project, w_widen, w_narrow, head_count):
    level_count, lat_total, lon_total, channels = stream.shape
    if shifted:
        stream = jnp.roll(stream, (-(WIN_LAT // 2), -(WIN_LON // 2)), axis=(1, 2))
    slab_count = lat_total // WIN_LAT
    slabs = stream.reshape(level_count, slab_count, WIN_LAT, lon_total, channels).transpose(1, 0, 2, 3, 4)

    def one_slab(inputs):
        slab_rows, slab_number = inputs
        region = None
        if shifted:
            global_row = slab_number * WIN_LAT + jnp.arange(WIN_LAT, dtype=jnp.int32) + WIN_LAT // 2
            region = (global_row >= lat_total).astype(jnp.int32)
        normed = layer_norm(slab_rows, norm_gains[0]).astype(jnp.bfloat16)
        context = attend(normed, w_triple, position_bias, region, head_count)
        return finish(slab_rows, context, norm_gains, w_project, w_widen, w_narrow)
    finished = lax.map(one_slab, (slabs, jnp.arange(slab_count, dtype=jnp.int32)))
    stream = finished.transpose(1, 0, 2, 3, 4).reshape(level_count, lat_total, lon_total, channels)
    if shifted:
        stream = jnp.roll(stream, (WIN_LAT // 2, WIN_LON // 2), axis=(1, 2))
    return stream

def merge_patches(stream, norm_gain, weight_matrix):
    level_count, row_count, col_count, channels = stream.shape
    grouped = stream.reshape(level_count, row_count // 2, 2, col_count // 2, 2, channels)
    grouped = grouped.transpose(0, 1, 3, 2, 4, 5).reshape(-1, 4 * channels)
    normed = layer_norm(grouped, norm_gain).astype(jnp.bfloat16)
    merged = jnp.dot(normed, weight_matrix, preferred_element_type=jnp.float32).astype(jnp.bfloat16)
    merged = lax.optimization_barrier(merged)
    return merged.reshape(level_count, row_count // 2, col_count // 2, -1)

def expand_patches(coarse, weight_matrix, norm_gain, skip_stream):
    level_count, row_count, col_count, channels = coarse.shape
    widened = jnp.dot(coarse.reshape(-1, channels), weight_matrix, preferred_element_type=jnp.float32)
    fine_channels = weight_matrix.shape[1] // 4
    shuffled = widened.reshape(level_count, row_count, col_count, 2, 2, fine_channels)
    shuffled = shuffled.transpose(0, 1, 3, 2, 4, 5).reshape(level_count, 2 * row_count, 2 * col_count, fine_channels)
    return (skip_stream.astype(jnp.float32) + layer_norm(shuffled, norm_gain)).astype(jnp.bfloat16)

def reference(fields, land_sea, land_embed, bias_index, fine_bias, fine_gains, fine_query_key_value, fine_project, fine_widen, fine_narrow, merge_gain, merge_weight, coarse_bias, coarse_gains, coarse_query_key_value, coarse_project, coarse_widen, coarse_narrow, expand_weight, expand_gain):
    stream = fields.astype(jnp.float32) + land_sea.astype(jnp.float32)[None, :, :, None] * land_embed
    stream = lax.optimization_barrier(stream.astype(jnp.bfloat16))
    for block_number in range(2):
        position_bias = jnp.take(fine_bias[block_number], bias_index, axis=1)
        stream = reference_block(stream, block_number == 1, position_bias, fine_gains[block_number], fine_query_key_value[block_number], fine_project[block_number], fine_widen[block_number], fine_narrow[block_number], HF)
    skip_stream = stream
    coarse = merge_patches(skip_stream, merge_gain, merge_weight)
    for block_number in range(2):
        position_bias = jnp.take(coarse_bias[block_number], bias_index, axis=1)
        coarse = reference_block(coarse, block_number == 1, position_bias, coarse_gains[block_number], coarse_query_key_value[block_number], coarse_project[block_number], coarse_widen[block_number], coarse_narrow[block_number], HC)
    return expand_patches(coarse, expand_weight, expand_gain, skip_stream)
```

```python
import functools

import jax
import jax.numpy as jnp
import numpy as np
from jax import lax
from jax.experimental import pallas as pl
from jax.experimental.pallas import tpu as pltpu
from jax.sharding import PartitionSpec as P

HF = 6
HC = 12
HEAD = 32
WIN_LAT = 6
WIN_LON = 12
WIN_TOK = 144
HALF_LAT = WIN_LAT // 2
HALF_LON = WIN_LON // 2
LEVELS = 2
QUAD = LEVELS * HALF_LAT * HALF_LON
QP = 40
WP = 4 * QP
LO_COUNT = 13
LOG2E = 1.4426950408889634
MASKED = -1e30
LON = ("sec", "head")
F32 = jnp.float32
BF16 = jnp.bfloat16


def quad_sources(row_count, col_count):
    slots = []
    for a in range(row_count // HALF_LAT):
        for b in range(col_count // HALF_LON):
            for s in range(QP):
                if s >= QUAD:
                    slots.append(None)
                    continue
                level, rest = divmod(s, HALF_LAT * HALF_LON)
                r, c = divmod(rest, HALF_LON)
                slots.append((level, a * HALF_LAT + r, b * HALF_LON + c))
    return slots


def one_hot(sources, width):
    table = np.zeros((len(sources), width), np.float32)
    for slot, source in enumerate(sources):
        if source is not None:
            table[slot, source] = 1.0
    return jnp.asarray(table.astype(jnp.bfloat16))


def fine_tables(rows, cols):
    slots = quad_sources(rows, cols)
    order = one_hot(
        [None if s is None else (s[0] * rows + s[1]) * cols + s[2] for s in slots],
        LEVELS * rows * cols,
    )
    of_row = one_hot([None if s is None else s[1] for s in slots], rows)
    of_col = one_hot([None if s is None else s[2] for s in slots], cols)
    return order, of_row, of_col


def merge_table(rows, cols):
    place = {s: n for n, s in enumerate(quad_sources(rows, cols)) if s is not None}
    sources = []
    for p in range(2):
        for q in range(2):
            for s in quad_sources(rows // 2, cols // 2):
                sources.append(
                    None if s is None else place[(s[0], 2 * s[1] + p, 2 * s[2] + q)]
                )
    return one_hot(sources, len(place) // QUAD * QP)


def expand_table(rows, cols):
    coarse = quad_sources(rows // 2, cols // 2)
    place = {s: n for n, s in enumerate(coarse) if s is not None}
    sources = []
    for level in range(LEVELS):
        for r in range(rows):
            for c in range(cols):
                part = (r % 2) * 2 + c % 2
                sources.append(part * len(coarse) + place[(level, r // 2, c // 2)])
    return one_hot(sources, 4 * len(coarse))


def dot(a, b):
    return jnp.dot(a, b, preferred_element_type=F32)


def dot_t(a, b):
    return lax.dot_general(a, b, (((1,), (1,)), ((), ())), preferred_element_type=F32)


def norm(x, gain):
    mean = jnp.mean(x, axis=-1, keepdims=True)
    centered = x - mean
    variance = jnp.mean(centered * centered, axis=-1, keepdims=True)
    return centered * lax.rsqrt(variance + 1e-05) * gain


def attend(q, k, v, bias_ref, first, heads, key_mask):
    n = q.shape[0]
    channels = q.shape[1]
    scale = HEAD**-0.5 * LOG2E
    outs = []
    for tile in range(0, channels, 128):
        width = min(128, channels - tile)
        count = width // HEAD
        qt = q[:, tile : tile + width]
        lane = lax.broadcasted_iota(jnp.int32, (n, width), 1) // HEAD
        masks = [lane == h for h in range(count)]
        stack = jnp.concatenate([jnp.where(m, qt, jnp.zeros_like(qt)) for m in masks], axis=0)
        scores = dot_t(stack, k[:, tile : tile + width])
        probs = []
        for h in range(count):
            head = tile // HEAD + h
            s = scores[h * n : (h + 1) * n] * scale + bias_ref[pl.ds(head * WP + first, n), :]
            if key_mask is not None:
                s = s + key_mask
            s = s - jnp.max(s, axis=-1, keepdims=True)
            probs.append(jnp.exp2(s).astype(BF16))
        probs = jnp.concatenate(probs, axis=0)
        vt = v[:, tile : tile + width]
        mixed = dot(probs, jnp.concatenate([vt, jnp.ones((WP, width), BF16)], axis=1))
        top = mixed[:n, :width]
        total = mixed[:n, width:]
        for h in range(1, count):
            top = jnp.where(masks[h], mixed[h * n : (h + 1) * n, :width], top)
            total = jnp.where(masks[h], mixed[h * n : (h + 1) * n, width:], total)
        outs.append(top / total)
    return outs[0] if len(outs) == 1 else jnp.concatenate(outs, axis=1)


def gelu(x):
    return 0.5 * x * (1.0 + lax.erf(x * np.float32(0.5**0.5)))


def finish(x, context, gain, w_project, w_widen, w_narrow):
    middle = (x + dot(context, w_project)).astype(BF16).astype(F32)
    second = norm(middle, gain).astype(BF16)
    hidden = gelu(dot(second, w_widen)).astype(BF16)
    return (middle + dot(hidden, w_narrow)).astype(BF16)


def bias_kernel(index_ref, spread_ref, table_ref, out_ref, table, index, *, heads, head_rows):
    spread = spread_ref[...]
    plain = index_ref[...]
    high = (plain >> 4).astype(F32).astype(BF16)
    low = (plain & 15).astype(F32).astype(BF16)

    def moved(part):
        return dot_t(dot(spread, part).astype(BF16), spread).astype(jnp.int32)

    spot = lax.broadcasted_iota(jnp.int32, (WP, WP), 1) % QP
    bias_len = table_ref.shape[-1]
    index[...] = jnp.where(spot < QUAD, moved(high) * 16 + moved(low), bias_len)

    wide = jnp.full((head_rows, LO_COUNT * 256), MASKED, F32)
    table[...] = wide
    table[:heads, :bias_len] = table_ref[...] * LOG2E
    values = table[...]
    big = values.astype(BF16)
    small = (values - big.astype(F32)).astype(BF16)
    left = jnp.concatenate(
        [p[:, i * 256 : (i + 1) * 256] for p in (big, small) for i in range(LO_COUNT)], axis=0
    )
    half = LO_COUNT * head_rows
    ladder = lax.broadcasted_iota(jnp.int32, (256, WP), 0).astype(F32).astype(BF16)

    def one(row, carry):
        entry = index[pl.ds(row, 1), :]
        near = (entry & 255).astype(F32).astype(BF16)
        picks = jnp.where(ladder == near, jnp.ones((), BF16), jnp.zeros((), BF16))
        both = dot(left, picks)
        far = entry >> 8
        total = jnp.zeros((head_rows, WP), F32)
        for i in range(LO_COUNT):
            at = i * head_rows
            total = jnp.where(
                far == i,
                both[at : at + head_rows] + both[half + at : half + at + head_rows],
                total,
            )
        for h in range(heads):
            out_ref[pl.ds(h * WP + row, 1), :] = total[h : h + 1]
        return carry

    lax.fori_loop(0, WP, one, 0, unroll=4)


def bias_of(tables, block, index, spread):
    heads = tables.shape[1]
    head_rows = -(-heads // 8) * 8
    flops = 2 * WP * 256 * WP * LO_COUNT * head_rows * 2
    return pl.pallas_call(
        functools.partial(bias_kernel, heads=heads, head_rows=head_rows),
        out_shape=jax.ShapeDtypeStruct((heads * WP, WP), F32),
        grid=(1,),
        in_specs=[
            pl.BlockSpec(memory_space=pltpu.VMEM),
            pl.BlockSpec(memory_space=pltpu.VMEM),
            pl.BlockSpec((None,) + tables.shape[1:], lambda _: (block, 0, 0)),
        ],
        out_specs=pl.BlockSpec(memory_space=pltpu.VMEM),
        scratch_shapes=[
            pltpu.VMEM((head_rows, LO_COUNT * 256), F32),
            pltpu.VMEM((WP, WP), jnp.int32),
        ],
        cost_estimate=pl.CostEstimate(flops=4 * flops, bytes_accessed=1 << 20, transcendentals=0),
        name="bias_table",
    )(index, spread, tables)


def first_kernel(
    fields_ref, land_ref, embed_ref, order_ref, of_row_ref, of_col_ref, bias_ref,
    gains_ref, w_triple_ref, w_project_ref, w_widen_ref, w_narrow_ref, out_ref, start_ref,
):
    channels = fields_ref.shape[1]
    land = land_ref[...].astype(F32).astype(BF16)
    on_row = dot(of_row_ref[...], land)
    on_land = jnp.sum(on_row * of_col_ref[...].astype(F32), axis=-1, keepdims=True)
    start = dot(order_ref[...], fields_ref[...]) + on_land * embed_ref[...]
    start_ref[...] = start.astype(BF16).astype(F32)
    rows = out_ref.shape[0]
    windows_down = 2
    pairs = rows // (QP * 4) // windows_down
    for a in range(windows_down):
        for b in range(pairs):
            top = (2 * a * 2 * pairs + 2 * b) * QP
            below = ((2 * a + 1) * 2 * pairs + 2 * b) * QP
            x = jnp.concatenate(
                [start_ref[top : top + 2 * QP], start_ref[below : below + 2 * QP]], axis=0
            )
            normed = norm(x, gains_ref[0:1]).astype(BF16)
            triple = dot(normed, w_triple_ref[...]).astype(BF16)
            context = attend(
                triple[:, :channels],
                triple[:, channels : 2 * channels],
                triple[:, 2 * channels :],
                bias_ref, 0, channels // HEAD, None,
            ).astype(BF16)
            done = finish(
                x, context, gains_ref[1:2], w_project_ref[...], w_widen_ref[...], w_narrow_ref[...]
            )
            out_ref[top : top + 2 * QP] = done[: 2 * QP]
            out_ref[below : below + 2 * QP] = done[2 * QP :]


def shifted_block(
    own_ref, north_ref, south_ref, west_ref, east_ref, edge_ref, bias_ref, gains_ref,
    w_triple_ref, w_project_ref, w_widen_ref, w_narrow_ref, query, key, value, context,
):
    channels = own_ref.shape[1]
    heads = channels // HEAD
    across = north_ref.shape[0] // QP
    down = own_ref.shape[0] // QP // across
    line = (across + 2) * QP
    inner = across * QP
    for i in range(down + 2):
        if i == 0:
            middle = north_ref[...]
        elif i == down + 1:
            middle = south_ref[...]
        else:
            middle = own_ref[(i - 1) * inner : i * inner]
        x = jnp.concatenate(
            [
                west_ref[i * QP : (i + 1) * QP].astype(F32),
                middle.astype(F32),
                east_ref[i * QP : (i + 1) * QP].astype(F32),
            ],
            axis=0,
        )
        normed = norm(x, gains_ref[0:1]).astype(BF16)
        triple = dot(normed, w_triple_ref[...])
        if 0 < i < down + 1:
            query[(i - 1) * line : i * line] = triple[:, :channels]
        key[i * line : (i + 1) * line] = triple[:, channels : 2 * channels].astype(BF16)
        value[i * line : (i + 1) * line] = triple[:, 2 * channels :].astype(BF16)
    lane = lax.broadcasted_iota(jnp.int32, (1, WP), 1)
    on_top = edge_ref[0]
    on_bottom = edge_ref[1]
    for wa in range(down // 2 + 1):
        mask = None
        if wa == 0:
            mask = jnp.where(lane < 2 * QP, on_top, 0.0)
        elif wa == down // 2:
            mask = jnp.where(lane < 2 * QP, 0.0, on_bottom)
        for wb in range(across // 2 + 1):
            at = [(2 * wa + r) * line + 2 * wb * QP for r in range(2)]
            k = jnp.concatenate([key[s : s + 2 * QP] for s in at], axis=0)
            v = jnp.concatenate([value[s : s + 2 * QP] for s in at], axis=0)
            rows = [r for r in range(2) if 0 < 2 * wa + r < down + 1]
            cols = [c for c in range(2) if 0 < 2 * wb + c < across + 1]
            size = len(cols) * QP
            qs = [
                query[
                    (2 * wa + r - 1) * line + (2 * wb + cols[0]) * QP :
                    (2 * wa + r - 1) * line + (2 * wb + cols[0]) * QP + size
                ]
                for r in rows
            ]
            if len(cols) == 2:
                groups = [(rows, jnp.concatenate(qs, axis=0) if len(qs) == 2 else qs[0])]
            else:
                groups = [([r], part) for r, part in zip(rows, qs)]
            for group, q in groups:
                out = attend(
                    q.astype(BF16), k, v, bias_ref, (2 * group[0] + cols[0]) * QP, heads, mask
                )
                for n, r in enumerate(group):
                    to = ((2 * wa + r - 1) * across + 2 * wb + cols[0] - 1) * QP
                    context[to : to + size] = out[n * size : (n + 1) * size]
    outs = []
    for at in range(0, own_ref.shape[0], WP):
        outs.append(
            finish(
                own_ref[at : at + WP].astype(F32),
                context[at : at + WP].astype(BF16),
                gains_ref[1:2],
                w_project_ref[...], w_widen_ref[...], w_narrow_ref[...],
            )
        )
    return outs


def middle_kernel(
    own_ref, north_ref, south_ref, west_ref, east_ref, edge_ref, bias_ref, gains_ref,
    w_triple_ref, w_project_ref, w_widen_ref, w_narrow_ref,
    merge_order_ref, merge_gain_ref, merge_weight_ref,
    coarse_bias_ref, coarse_gains_ref, c_triple_ref, c_project_ref, c_widen_ref, c_narrow_ref,
    parts_ref, coarse_ref, query, key, value, context,
):
    outs = shifted_block(
        own_ref, north_ref, south_ref, west_ref, east_ref, edge_ref, bias_ref, gains_ref,
        w_triple_ref, w_project_ref, w_widen_ref, w_narrow_ref, query, key, value, context,
    )
    channels = own_ref.shape[1]
    skip = jnp.concatenate(outs, axis=0)
    grouped = dot(merge_order_ref[...], skip)
    parts_ref[...] = grouped.astype(BF16)
    parts = [grouped[i * WP : (i + 1) * WP] for i in range(4)]
    width = 4 * channels
    mean = sum(jnp.sum(p, axis=-1, keepdims=True) for p in parts) / width
    parts = [p - mean for p in parts]
    variance = sum(jnp.sum(p * p, axis=-1, keepdims=True) for p in parts) / width
    factor = lax.rsqrt(variance + 1e-05)
    coarse = jnp.zeros((WP, merge_weight_ref.shape[1]), F32)
    for i, p in enumerate(parts):
        merged = (p * factor * merge_gain_ref[i : i + 1]).astype(BF16)
        coarse = coarse + dot(merged, merge_weight_ref[i * channels : (i + 1) * channels])
    x = coarse.astype(BF16).astype(F32)
    wide = x.shape[1]
    normed = norm(x, coarse_gains_ref[0:1]).astype(BF16)
    triple = dot(normed, c_triple_ref[...]).astype(BF16)
    mixed = attend(
        triple[:, :wide], triple[:, wide : 2 * wide], triple[:, 2 * wide :],
        coarse_bias_ref, 0, wide // HEAD, None,
    ).astype(BF16)
    coarse_ref[...] = finish(
        x, mixed, coarse_gains_ref[1:2], c_project_ref[...], c_widen_ref[...], c_narrow_ref[...]
    )


def last_kernel(
    own_ref, north_ref, south_ref, west_ref, east_ref, edge_ref, bias_ref, gains_ref,
    w_triple_ref, w_project_ref, w_widen_ref, w_narrow_ref,
    parts_ref, expand_weight_ref, expand_gain_ref, expand_order_ref,
    out_ref, query, key, value, context,
):
    (deep,) = shifted_block(
        own_ref, north_ref, south_ref, west_ref, east_ref, edge_ref, bias_ref, gains_ref,
        w_triple_ref, w_project_ref, w_widen_ref, w_narrow_ref, query, key, value, context,
    )
    channels = parts_ref.shape[1]
    widened = dot(deep, expand_weight_ref[...])
    outs = []
    for i in range(4):
        shuffled = widened[:, i * channels : (i + 1) * channels]
        skip = parts_ref[i * WP : (i + 1) * WP].astype(F32)
        outs.append((skip + norm(shuffled, expand_gain_ref[...])).astype(BF16))
    out_ref[...] = dot(expand_order_ref[...], jnp.concatenate(outs, axis=0)).astype(BF16)


WHOLE = pl.BlockSpec(memory_space=pltpu.VMEM)


def block_spec(array, block):
    return pl.BlockSpec((None,) + array.shape[1:], lambda _: (block,) + (0,) * (array.ndim - 1))


def halo(own):
    rows, cols, _, channels = own.shape
    lat = lax.axis_size("lat")
    lon = lax.axis_size(LON)
    down = [(i, (i + 1) % lat) for i in range(lat)]
    up = [((i + 1) % lat, i) for i in range(lat)]
    east = [(i, (i + 1) % lon) for i in range(lon)]
    west = [((i + 1) % lon, i) for i in range(lon)]
    north = lax.ppermute(own[rows - 1], "lat", down)
    south = lax.ppermute(own[0], "lat", up)

    def side(c):
        return jnp.concatenate([north[c : c + 1], own[:, c], south[c : c + 1]], axis=0)

    from_west = lax.ppermute(side(cols - 1), LON, east)
    from_east = lax.ppermute(side(0), LON, west)
    return [v.reshape(-1, channels) for v in (own, north, south, from_west, from_east)]


def shifted_scratch(rows, cols, channels):
    line = (cols + 2) * QP
    return [
        pltpu.VMEM((rows * line, channels), F32),
        pltpu.VMEM(((rows + 2) * line, channels), BF16),
        pltpu.VMEM(((rows + 2) * line, channels), BF16),
        pltpu.VMEM((rows * cols * QP, channels), F32),
    ]


def on_device(
    fields, land_sea, land_embed, bias_index, fine_bias, fine_gains, fine_query_key_value,
    fine_project, fine_widen, fine_narrow, merge_gain, merge_weight, coarse_bias, coarse_gains,
    coarse_query_key_value, coarse_project, coarse_widen, coarse_narrow, expand_weight, expand_gain,
):
    _, rows, cols, channels = fields.shape
    quad_rows, quad_cols = rows // HALF_LAT, cols // HALF_LON
    tokens = quad_rows * quad_cols * QP
    wide = merge_weight.shape[1]
    spread = one_hot(
        [None if s is None else (s[0] * WIN_LAT + s[1]) * WIN_LON + s[2]
         for s in quad_sources(WIN_LAT, WIN_LON)],
        WIN_TOK,
    )
    order, of_row, of_col = fine_tables(rows, cols)
    fine = [bias_of(fine_bias, n, bias_index, spread) for n in range(2)]
    deep = [bias_of(coarse_bias, n, bias_index, spread) for n in range(2)]
    fine_weights = (fine_gains, fine_query_key_value, fine_project, fine_widen, fine_narrow)
    coarse_weights = (
        coarse_gains, coarse_query_key_value, coarse_project, coarse_widen, coarse_narrow
    )
    params = pltpu.CompilerParams(vmem_limit_bytes=48 << 20)

    first = pl.pallas_call(
        first_kernel,
        out_shape=jax.ShapeDtypeStruct((tokens, channels), BF16),
        grid=(1,),
        in_specs=[WHOLE] * 7 + [block_spec(w, 0) for w in fine_weights],
        out_specs=WHOLE,
        scratch_shapes=[pltpu.VMEM((tokens, channels), F32)],
        compiler_params=params,
        name="fine_plain",
    )(
        fields.reshape(-1, channels), land_sea, land_embed[None], order, of_row, of_col, fine[0],
        *fine_weights,
    )

    place = lax.axis_index("lat")
    edge = jnp.stack(
        [
            jnp.where(place == 0, MASKED, 0.0),
            jnp.where(place == lax.axis_size("lat") - 1, MASKED, 0.0),
        ]
    ).astype(F32)
    smem = pl.BlockSpec(memory_space=pltpu.SMEM)

    parts, coarse = pl.pallas_call(
        middle_kernel,
        out_shape=[
            jax.ShapeDtypeStruct((tokens, channels), BF16),
            jax.ShapeDtypeStruct((tokens // 4, wide), BF16),
        ],
        grid=(1,),
        in_specs=[WHOLE] * 5 + [smem, WHOLE] + [block_spec(w, 1) for w in fine_weights]
        + [WHOLE] * 4 + [block_spec(w, 0) for w in coarse_weights],
        out_specs=[WHOLE] * 2,
        scratch_shapes=shifted_scratch(quad_rows, quad_cols, channels),
        compiler_params=params,
        name="fine_shifted_coarse_plain",
    )(
        *halo(first.reshape(quad_rows, quad_cols, QP, channels)), edge, fine[1], *fine_weights,
        merge_table(rows, cols), merge_gain.reshape(4, channels), merge_weight,
        deep[0], *coarse_weights,
    )

    out = pl.pallas_call(
        last_kernel,
        out_shape=jax.ShapeDtypeStruct((LEVELS * rows * cols, channels), BF16),
        grid=(1,),
        in_specs=[WHOLE] * 5 + [smem, WHOLE] + [block_spec(w, 1) for w in coarse_weights]
        + [WHOLE] * 4,
        out_specs=WHOLE,
        scratch_shapes=shifted_scratch(quad_rows // 2, quad_cols // 2, wide),
        compiler_params=params,
        name="coarse_shifted_expand",
    )(
        *halo(coarse.reshape(quad_rows // 2, quad_cols // 2, QP, wide)), edge, deep[1],
        *coarse_weights, parts, expand_weight, expand_gain[None], expand_table(rows, cols),
    )
    return out.reshape(fields.shape)


def solution(mesh):
    grid = P(None, "lat", LON, None)
    return jax.shard_map(
        on_device,
        mesh=mesh,
        in_specs=(grid, P("lat", LON)) + (P(),) * 18,
        out_specs=grid,
        check_vma=False,
    )
```

```python
import functools

import jax
import jax.numpy as jnp
import numpy as np
from jax import lax
from jax.experimental import pallas as pl
from jax.experimental.pallas import tpu as pltpu
from jax.sharding import PartitionSpec as P

HF = 6
HC = 12
HEAD = 32
WIN_LAT = 6
WIN_LON = 12
WIN_TOK = 144
HALF_LAT = WIN_LAT // 2
HALF_LON = WIN_LON // 2
LEVELS = 2
QUAD = LEVELS * HALF_LAT * HALF_LON
QP = 40
WP = 4 * QP
LO_COUNT = 13
LOG2E = 1.4426950408889634
MASKED = -1e30
LON = ("sec", "head")
F32 = jnp.float32
BF16 = jnp.bfloat16


def quad_sources(row_count, col_count):
    slots = []
    for a in range(row_count // HALF_LAT):
        for b in range(col_count // HALF_LON):
            for s in range(QP):
                if s >= QUAD:
                    slots.append(None)
                    continue
                level, rest = divmod(s, HALF_LAT * HALF_LON)
                r, c = divmod(rest, HALF_LON)
                slots.append((level, a * HALF_LAT + r, b * HALF_LON + c))
    return slots


def one_hot(sources, width):
    table = np.zeros((len(sources), width), np.float32)
    for slot, source in enumerate(sources):
        if source is not None:
            table[slot, source] = 1.0
    return jnp.asarray(table.astype(jnp.bfloat16))


def fine_tables(rows, cols):
    slots = quad_sources(rows, cols)
    order = one_hot(
        [None if s is None else (s[0] * rows + s[1]) * cols + s[2] for s in slots],
        LEVELS * rows * cols,
    )
    of_row = one_hot([None if s is None else s[1] for s in slots], rows)
    of_col = one_hot([None if s is None else s[2] for s in slots], cols)
    return order, of_row, of_col


def merge_table(rows, cols):
    place = {s: n for n, s in enumerate(quad_sources(rows, cols)) if s is not None}
    sources = []
    for p in range(2):
        for q in range(2):
            for s in quad_sources(rows // 2, cols // 2):
                sources.append(
                    None if s is None else place[(s[0], 2 * s[1] + p, 2 * s[2] + q)]
                )
    return one_hot(sources, len(place) // QUAD * QP)


def expand_table(rows, cols):
    coarse = quad_sources(rows // 2, cols // 2)
    place = {s: n for n, s in enumerate(coarse) if s is not None}
    sources = []
    for level in range(LEVELS):
        for r in range(rows):
            for c in range(cols):
                part = (r % 2) * 2 + c % 2
                sources.append(part * len(coarse) + place[(level, r // 2, c // 2)])
    return one_hot(sources, 4 * len(coarse))


def dot(a, b):
    return jnp.dot(a, b, preferred_element_type=F32)


def dot_t(a, b):
    return lax.dot_general(a, b, (((1,), (1,)), ((), ())), preferred_element_type=F32)


def norm(x, gain):
    mean = jnp.mean(x, axis=-1, keepdims=True)
    centered = x - mean
    variance = jnp.mean(centered * centered, axis=-1, keepdims=True)
    return centered * lax.rsqrt(variance + 1e-05) * gain


def attend(q, k, v, bias_ref, first, key_mask):
    n = q.shape[0]
    channels = q.shape[1]
    scale = HEAD**-0.5 * LOG2E
    outs = []
    for tile in range(0, channels, 128):
        width = min(128, channels - tile)
        count = width // HEAD
        qt = q[:, tile : tile + width]
        lane = lax.broadcasted_iota(jnp.int32, (n, width), 1) // HEAD
        masks = [lane == h for h in range(count)]
        stack = jnp.concatenate([jnp.where(m, qt, jnp.zeros_like(qt)) for m in masks], axis=0)
        scores = dot_t(stack, k[:, tile : tile + width])
        probs = []
        for h in range(count):
            head = tile // HEAD + h
            bias = jnp.concatenate(
                [
                    bias_ref[0, head, first : first + n, :],
                    bias_ref[1, head, first : first + n, : WP - 128],
                ],
                axis=1,
            )
            s = scores[h * n : (h + 1) * n] * scale + bias
            if key_mask is not None:
                s = s + key_mask
            s = s - jnp.max(s, axis=-1, keepdims=True)
            probs.append(jnp.exp2(s).astype(BF16))
        probs = jnp.concatenate(probs, axis=0)
        vt = v[:, tile : tile + width]
        mixed = dot(probs, jnp.concatenate([vt, jnp.ones((WP, width), BF16)], axis=1))
        top = mixed[:n, :width]
        total = mixed[:n, width:]
        for h in range(1, count):
            top = jnp.where(masks[h], mixed[h * n : (h + 1) * n, :width], top)
            total = jnp.where(masks[h], mixed[h * n : (h + 1) * n, width:], total)
        outs.append(top / total)
    return outs[0] if len(outs) == 1 else jnp.concatenate(outs, axis=1)


def gelu(x):
    return 0.5 * x * (1.0 + lax.erf(x * np.float32(0.5**0.5)))


def finish(x, context, gain, w_project, w_widen, w_narrow):
    middle = (x + dot(context, w_project)).astype(BF16).astype(F32)
    second = norm(middle, gain).astype(BF16)
    hidden = gelu(dot(second, w_widen)).astype(BF16)
    return (middle + dot(hidden, w_narrow)).astype(BF16)


def padded(heads):
    return -(-heads // 8) * 8


def bias_kernel(index_ref, spread_ref, *refs, picks):
    table_refs = refs[:-4]
    out_ref, table, index, left = refs[-4:]
    rows = table.shape[0]
    bias_len = table_refs[0].shape[-1]

    @pl.when(pl.program_id(0) == 0)
    def _():
        spread = spread_ref[...]
        plain = index_ref[...]
        high = (plain >> 4).astype(F32).astype(BF16)
        low = (plain & 15).astype(F32).astype(BF16)

        def moved(part):
            return dot_t(dot(spread, part).astype(BF16), spread).astype(jnp.int32)

        spot = lax.broadcasted_iota(jnp.int32, (WP, WP), 1) % QP
        index[...] = jnp.where(spot < QUAD, moved(high) * 16 + moved(low), bias_len)
        table[...] = jnp.full(table.shape, MASKED, F32)
        at = 0
        for table_ref, block in zip(table_refs, picks):
            heads = table_ref.shape[0]
            for h in range(heads):
                table[at + h : at + h + 1, :bias_len] = (
                    table_ref[h, block : block + 1, :] * LOG2E
                )
            at += padded(heads)
        values = table[...]
        big = values.astype(BF16)
        small = (values - big.astype(F32)).astype(BF16)
        for n, part in enumerate((big, small)):
            left[:, n * 256 : (n + 1) * 256] = jnp.concatenate(
                [part[:, i * 256 : (i + 1) * 256] for i in range(LO_COUNT)], axis=0
            )

    ladder = lax.broadcasted_iota(jnp.int32, (256, 256), 0).astype(F32).astype(BF16)
    lane = lax.broadcasted_iota(jnp.int32, (8, 256), 1) // 32
    sublane = lax.broadcasted_iota(jnp.int32, (8, 256), 0)
    span = out_ref.shape[1] // rows
    for group in range(span // 8):
        first = pl.multiple_of(pl.program_id(0) * span + group * 8, 8)
        entries = index[pl.ds(first, 8), :]
        rest = jnp.concatenate([entries[:, 128:]] * 8, axis=1)
        rest = jnp.sum(jnp.where(lane == sublane, rest, 0).astype(F32), axis=0, keepdims=True)
        pieces = [
            jnp.concatenate([entries[j : j + 1, :128], entries[j + 1 : j + 2, :128]], axis=1)
            for j in range(0, 8, 2)
        ] + [rest.astype(jnp.int32)]
        for t, entry in enumerate(pieces):
            near = (entry & 255).astype(F32).astype(BF16)
            far = entry >> 8
            chosen = jnp.where(ladder == near, jnp.ones((), BF16), jnp.zeros((), BF16))
            found = dot(left[...], jnp.concatenate([chosen, chosen], axis=0))
            total = found[:rows]
            for i in range(1, LO_COUNT):
                total = jnp.where(far == i, found[i * rows : (i + 1) * rows], total)
            for h in range(0, rows, 8):
                part = total[h : h + 8]
                at = h * span + group * 8
                if t < 4:
                    for j in range(2):
                        out_ref[0, pl.ds(at + 2 * t + j, 8, stride=span), :] = (
                            part[:, j * 128 : (j + 1) * 128]
                        )
                else:
                    for j in range(8):
                        moved_part = part[:, j // 4 * 128 : (j // 4 + 1) * 128]
                        if j % 4:
                            moved_part = pltpu.roll(moved_part, 128 - 32 * (j % 4), 1)
                        out_ref[1, pl.ds(at + j, 8, stride=span), :] = moved_part


def bias_of(picks, index, spread, span=32):
    tables = [t.transpose(1, 0, 2) for t, _ in picks]
    rows = sum(padded(t.shape[0]) for t in tables)
    flops = 2 * WP * 256 * WP * LO_COUNT * rows * 4
    steps = WP // span
    whole = pl.BlockSpec(memory_space=pltpu.VMEM)
    out = pl.pallas_call(
        functools.partial(bias_kernel, picks=tuple(b for _, b in picks)),
        out_shape=jax.ShapeDtypeStruct((2, steps * rows * span, 128), F32),
        grid=(steps,),
        in_specs=[whole] * (2 + len(tables)),
        out_specs=pl.BlockSpec((2, rows * span, 128), lambda i: (0, i, 0)),
        scratch_shapes=[
            pltpu.VMEM((rows, LO_COUNT * 256), F32),
            pltpu.VMEM((WP, WP), jnp.int32),
            pltpu.VMEM((rows * LO_COUNT, 512), BF16),
        ],
        compiler_params=pltpu.CompilerParams(vmem_limit_bytes=16 << 20),
        cost_estimate=pl.CostEstimate(flops=2 * flops, bytes_accessed=1 << 20, transcendentals=0),
        name="bias_table",
    )(index, spread, *tables)
    return out.reshape(2, steps, rows, span, 128)


def bias_copies(source_ref, bias, first, sems, at):
    steps, span, heads = source_ref.shape[1], source_ref.shape[3], bias.shape[1]
    return [
        pltpu.make_async_copy(
            source_ref.at[half, step, pl.ds(first, heads)],
            bias.at[half, :, pl.ds(step * span, span)],
            sems.at[at + half * steps + step],
        )
        for half in range(2)
        for step in range(steps)
    ]


class Fetched:
    def __init__(self, copies):
        self.copies = copies
        for group in copies:
            for copy in group:
                copy.start()

    def wait(self, *numbers):
        for n in numbers:
            for copy in self.copies[n]:
                copy.wait()


def first_kernel(
    fields_ref, land_ref, embed_ref, order_hbm, of_row_ref, of_col_ref, bias_hbm,
    gains_ref, triple_hbm, project_hbm, widen_hbm, narrow_hbm,
    out_ref, top_ref, bottom_ref,
    start_ref, order, bias, w_triple, w_project, w_widen, w_narrow, sems, bias_sems,
):
    channels = fields_ref.shape[1]
    fetched = Fetched(
        [[pltpu.make_async_copy(order_hbm, order, sems.at[0])],
         bias_copies(bias_hbm, bias, 0, bias_sems, 0)]
        + [
            [pltpu.make_async_copy(source.at[0], target, sems.at[1 + n])]
            for n, (source, target) in enumerate(
                [(triple_hbm, w_triple), (project_hbm, w_project),
                 (widen_hbm, w_widen), (narrow_hbm, w_narrow)]
            )
        ]
    )
    land = land_ref[...].astype(F32).astype(BF16)
    on_row = dot(of_row_ref[...], land)
    on_land = jnp.sum(on_row * of_col_ref[...].astype(F32), axis=-1, keepdims=True)
    fetched.wait(0)
    start = dot(order[...], fields_ref[...]) + on_land * embed_ref[...]
    start_ref[...] = start.astype(BF16).astype(F32)
    fetched.wait(1, 2, 3, 4, 5)
    rows = out_ref.shape[0]
    inner = top_ref.shape[0]
    down = rows // inner // 2
    for a in range(down):
        for b in range(inner // QP // 2):
            top = 2 * a * inner + 2 * b * QP
            below = top + inner
            x = jnp.concatenate(
                [start_ref[top : top + 2 * QP], start_ref[below : below + 2 * QP]], axis=0
            )
            normed = norm(x, gains_ref[0, 0:1]).astype(BF16)
            triple = dot(normed, w_triple[...]).astype(BF16)
            context = attend(
                triple[:, :channels],
                triple[:, channels : 2 * channels],
                triple[:, 2 * channels :],
                bias, 0, None,
            ).astype(BF16)
            done = finish(
                x, context, gains_ref[0, 1:2], w_project[...], w_widen[...], w_narrow[...]
            )
            out_ref[top : top + 2 * QP] = done[: 2 * QP]
            out_ref[below : below + 2 * QP] = done[2 * QP :]
    top_ref[...] = out_ref[:inner]
    bottom_ref[...] = out_ref[rows - inner :]


def shifted_block(
    own_ref, north_ref, south_ref, west_ref, east_ref, gains_ref, fetched,
    bias, w_triple, w_project, w_widen, w_narrow, query, key, value, context,
):
    channels = own_ref.shape[1]
    fetched.wait(1)
    across = north_ref.shape[0] // QP
    down = own_ref.shape[0] // QP // across
    line = (across + 2) * QP
    inner = across * QP
    for i in range(down + 2):
        if i == 0:
            middle = north_ref[...]
        elif i == down + 1:
            middle = south_ref[...]
        else:
            middle = own_ref[(i - 1) * inner : i * inner]
        x = jnp.concatenate(
            [
                west_ref[i * QP : (i + 1) * QP].astype(F32),
                middle.astype(F32),
                east_ref[i * QP : (i + 1) * QP].astype(F32),
            ],
            axis=0,
        )
        normed = norm(x, gains_ref[1, 0:1]).astype(BF16)
        triple = dot(normed, w_triple[...])
        if 0 < i < down + 1:
            query[(i - 1) * line : i * line] = triple[:, :channels]
        key[i * line : (i + 1) * line] = triple[:, channels : 2 * channels].astype(BF16)
        value[i * line : (i + 1) * line] = triple[:, 2 * channels :].astype(BF16)
    lane = lax.broadcasted_iota(jnp.int32, (1, WP), 1)
    place = lax.axis_index("lat")
    on_top = jnp.where(place == 0, MASKED, 0.0).astype(F32)
    on_bottom = jnp.where(place == lax.axis_size("lat") - 1, MASKED, 0.0).astype(F32)
    fetched.wait(0)
    for wa in range(down // 2 + 1):
        mask = None
        if wa == 0:
            mask = jnp.where(lane < 2 * QP, on_top, 0.0)
        elif wa == down // 2:
            mask = jnp.where(lane < 2 * QP, 0.0, on_bottom)
        for wb in range(across // 2 + 1):
            at = [(2 * wa + r) * line + 2 * wb * QP for r in range(2)]
            k = jnp.concatenate([key[s : s + 2 * QP] for s in at], axis=0)
            v = jnp.concatenate([value[s : s + 2 * QP] for s in at], axis=0)
            rows = [r for r in range(2) if 0 < 2 * wa + r < down + 1]
            cols = [c for c in range(2) if 0 < 2 * wb + c < across + 1]
            size = len(cols) * QP
            qs = [
                query[
                    (2 * wa + r - 1) * line + (2 * wb + cols[0]) * QP :
                    (2 * wa + r - 1) * line + (2 * wb + cols[0]) * QP + size
                ]
                for r in rows
            ]
            if len(cols) == 2:
                groups = [(rows, jnp.concatenate(qs, axis=0) if len(qs) == 2 else qs[0])]
            else:
                groups = [([r], part) for r, part in zip(rows, qs)]
            for group, q in groups:
                out = attend(
                    q.astype(BF16), k, v, bias, (2 * group[0] + cols[0]) * QP, mask
                )
                for n, r in enumerate(group):
                    to = ((2 * wa + r - 1) * across + 2 * wb + cols[0] - 1) * QP
                    context[to : to + size] = out[n * size : (n + 1) * size]
    fetched.wait(2, 3, 4)
    outs = []
    for at in range(0, own_ref.shape[0], WP):
        outs.append(
            finish(
                own_ref[at : at + WP].astype(F32),
                context[at : at + WP].astype(BF16),
                gains_ref[1, 1:2],
                w_project[...], w_widen[...], w_narrow[...],
            )
        )
    return outs


def block_copies(pairs, block, sems, at):
    return [
        [pltpu.make_async_copy(source.at[block], target, sems.at[at + n])]
        for n, (source, target) in enumerate(pairs)
    ]


def middle_kernel(
    own_ref, north_ref, south_ref, west_ref, east_ref, gains_ref, merge_gain_ref,
    coarse_gains_ref, bias_hbm, triple_hbm, project_hbm, widen_hbm, narrow_hbm,
    merge_order_hbm, merge_weight_hbm, c_triple_hbm, c_project_hbm, c_widen_hbm, c_narrow_hbm,
    parts_ref, coarse_ref, top_ref, bottom_ref,
    query, key, value, context, bias, c_bias, w_triple, w_project, w_widen, w_narrow,
    merge_order, merge_weight, c_triple, c_project, c_widen, c_narrow, sems, bias_sems,
):
    steps = bias_hbm.shape[1]
    heads = bias.shape[1]
    fetched = Fetched(
        [bias_copies(bias_hbm, bias, 0, bias_sems, 0)]
        + block_copies(
            [(triple_hbm, w_triple), (project_hbm, w_project),
             (widen_hbm, w_widen), (narrow_hbm, w_narrow)], 1, sems, 0,
        )
        + [
            [pltpu.make_async_copy(merge_order_hbm, merge_order, sems.at[4])],
            [pltpu.make_async_copy(merge_weight_hbm, merge_weight, sems.at[5])],
            bias_copies(bias_hbm, c_bias, padded(heads), bias_sems, 2 * steps),
        ]
        + block_copies(
            [(c_triple_hbm, c_triple), (c_project_hbm, c_project),
             (c_widen_hbm, c_widen), (c_narrow_hbm, c_narrow)], 0, sems, 6,
        )
    )
    outs = shifted_block(
        own_ref, north_ref, south_ref, west_ref, east_ref, gains_ref, fetched,
        bias, w_triple, w_project, w_widen, w_narrow, query, key, value, context,
    )
    channels = own_ref.shape[1]
    skip = jnp.concatenate(outs, axis=0)
    fetched.wait(*range(5, 12))
    grouped = dot(merge_order[...], skip)
    parts_ref[...] = grouped.astype(BF16)
    parts = [grouped[i * WP : (i + 1) * WP] for i in range(4)]
    width = 4 * channels
    mean = sum(jnp.sum(p, axis=-1, keepdims=True) for p in parts) / width
    parts = [p - mean for p in parts]
    variance = sum(jnp.sum(p * p, axis=-1, keepdims=True) for p in parts) / width
    factor = lax.rsqrt(variance + 1e-05)
    coarse = jnp.zeros((WP, merge_weight.shape[1]), F32)
    for i, p in enumerate(parts):
        merged = (p * factor * merge_gain_ref[i : i + 1]).astype(BF16)
        coarse = coarse + dot(merged, merge_weight[i * channels : (i + 1) * channels])
    x = coarse.astype(BF16).astype(F32)
    wide = x.shape[1]
    normed = norm(x, coarse_gains_ref[0, 0:1]).astype(BF16)
    triple = dot(normed, c_triple[...]).astype(BF16)
    mixed = attend(
        triple[:, :wide], triple[:, wide : 2 * wide], triple[:, 2 * wide :], c_bias, 0, None
    ).astype(BF16)
    done = finish(
        x, mixed, coarse_gains_ref[0, 1:2], c_project[...], c_widen[...], c_narrow[...]
    )
    coarse_ref[...] = done
    inner = top_ref.shape[0]
    top_ref[...] = done[:inner]
    bottom_ref[...] = done[WP - inner :]


def last_kernel(
    own_ref, north_ref, south_ref, west_ref, east_ref, gains_ref, parts_ref, expand_gain_ref,
    bias_hbm, triple_hbm, project_hbm, widen_hbm, narrow_hbm, expand_weight_hbm, expand_order_hbm,
    out_ref,
    query, key, value, context, bias, w_triple, w_project, w_widen, w_narrow,
    expand_weight, expand_order, sems, bias_sems,
):
    fetched = Fetched(
        [bias_copies(bias_hbm, bias, 0, bias_sems, 0)]
        + block_copies(
            [(triple_hbm, w_triple), (project_hbm, w_project),
             (widen_hbm, w_widen), (narrow_hbm, w_narrow)], 1, sems, 0,
        )
        + [
            [pltpu.make_async_copy(expand_weight_hbm, expand_weight, sems.at[4])],
            [pltpu.make_async_copy(expand_order_hbm, expand_order, sems.at[5])],
        ]
    )
    (deep,) = shifted_block(
        own_ref, north_ref, south_ref, west_ref, east_ref, gains_ref, fetched,
        bias, w_triple, w_project, w_widen, w_narrow, query, key, value, context,
    )
    channels = parts_ref.shape[1]
    fetched.wait(5, 6)
    widened = dot(deep, expand_weight[...])
    outs = []
    for i in range(4):
        shuffled = widened[:, i * channels : (i + 1) * channels]
        skip = parts_ref[i * WP : (i + 1) * WP].astype(F32)
        outs.append((skip + norm(shuffled, expand_gain_ref[...])).astype(BF16))
    out_ref[...] = dot(expand_order[...], jnp.concatenate(outs, axis=0)).astype(BF16)


WHOLE = pl.BlockSpec(memory_space=pltpu.VMEM)
APART = pl.BlockSpec(memory_space=pltpu.HBM)


def weight_scratch(weights):
    return [pltpu.VMEM(w.shape[1:], BF16) for w in weights]


def halo(own, top, bottom):
    rows, cols, _, channels = own.shape
    top = top.reshape(own.shape[1:])
    bottom = bottom.reshape(own.shape[1:])
    lat = lax.axis_size("lat")
    lon = lax.axis_size(LON)
    down = [(i, (i + 1) % lat) for i in range(lat)]
    up = [((i + 1) % lat, i) for i in range(lat)]
    east = [(i, (i + 1) % lon) for i in range(lon)]
    west = [((i + 1) % lon, i) for i in range(lon)]
    north = lax.ppermute(bottom, "lat", down)
    south = lax.ppermute(top, "lat", up)

    def side(c):
        return jnp.concatenate([north[c : c + 1], own[:, c], south[c : c + 1]], axis=0)

    from_west = lax.ppermute(side(cols - 1), LON, east)
    from_east = lax.ppermute(side(0), LON, west)
    return [v.reshape(-1, channels) for v in (own, north, south, from_west, from_east)]


def shifted_scratch(rows, cols, channels):
    line = (cols + 2) * QP
    return [
        pltpu.VMEM((rows * line, channels), F32),
        pltpu.VMEM(((rows + 2) * line, channels), BF16),
        pltpu.VMEM(((rows + 2) * line, channels), BF16),
        pltpu.VMEM((rows * cols * QP, channels), F32),
    ]


def on_device(
    fields, land_sea, land_embed, bias_index, fine_bias, fine_gains, fine_query_key_value,
    fine_project, fine_widen, fine_narrow, merge_gain, merge_weight, coarse_bias, coarse_gains,
    coarse_query_key_value, coarse_project, coarse_widen, coarse_narrow, expand_weight, expand_gain,
):
    _, rows, cols, channels = fields.shape
    quad_rows, quad_cols = rows // HALF_LAT, cols // HALF_LON
    tokens = quad_rows * quad_cols * QP
    wide = merge_weight.shape[1]
    spread = one_hot(
        [None if s is None else (s[0] * WIN_LAT + s[1]) * WIN_LON + s[2]
         for s in quad_sources(WIN_LAT, WIN_LON)],
        WIN_TOK,
    )
    order, of_row, of_col = fine_tables(rows, cols)
    bias_first = bias_of([(fine_bias, 0)], bias_index, spread)
    bias_middle = bias_of([(fine_bias, 1), (coarse_bias, 0)], bias_index, spread)
    bias_last = bias_of([(coarse_bias, 1)], bias_index, spread)
    fine_weights = (fine_query_key_value, fine_project, fine_widen, fine_narrow)
    coarse_weights = (coarse_query_key_value, coarse_project, coarse_widen, coarse_narrow)
    steps = bias_first.shape[1]
    dma = pltpu.SemaphoreType.DMA
    fine_scratch = pltpu.VMEM((2, HF, WP, 128), F32)
    coarse_scratch = pltpu.VMEM((2, HC, WP, 128), F32)
    line = quad_cols * QP

    first, top, bottom = pl.pallas_call(
        first_kernel,
        out_shape=[
            jax.ShapeDtypeStruct((tokens, channels), BF16),
            jax.ShapeDtypeStruct((line, channels), BF16),
            jax.ShapeDtypeStruct((line, channels), BF16),
        ],
        in_specs=[WHOLE] * 3 + [APART] + [WHOLE] * 2 + [APART, WHOLE] + [APART] * 4,
        out_specs=[WHOLE] * 3,
        scratch_shapes=[pltpu.VMEM((tokens, channels), F32), pltpu.VMEM(order.shape, BF16)]
        + [fine_scratch] + weight_scratch(fine_weights) + [dma((5,)), dma((2 * steps,))],
        compiler_params=pltpu.CompilerParams(vmem_limit_bytes=20 << 20),
        name="fine_plain",
    )(
        fields.reshape(-1, channels), land_sea, land_embed[None], order, of_row, of_col,
        bias_first, fine_gains, *fine_weights,
    )

    merge_order = merge_table(rows, cols)
    parts, coarse, top, bottom = pl.pallas_call(
        middle_kernel,
        out_shape=[
            jax.ShapeDtypeStruct((tokens, channels), BF16),
            jax.ShapeDtypeStruct((tokens // 4, wide), BF16),
            jax.ShapeDtypeStruct((line // 2, wide), BF16),
            jax.ShapeDtypeStruct((line // 2, wide), BF16),
        ],
        in_specs=[WHOLE] * 8 + [APART] * 11,
        out_specs=[WHOLE] * 4,
        scratch_shapes=shifted_scratch(quad_rows, quad_cols, channels)
        + [fine_scratch, coarse_scratch] + weight_scratch(fine_weights)
        + [pltpu.VMEM(merge_order.shape, BF16), pltpu.VMEM(merge_weight.shape, BF16)]
        + weight_scratch(coarse_weights) + [dma((10,)), dma((4 * steps,))],
        compiler_params=pltpu.CompilerParams(vmem_limit_bytes=32 << 20),
        name="fine_shifted_coarse_plain",
    )(
        *halo(first.reshape(quad_rows, quad_cols, QP, channels), top, bottom),
        fine_gains, merge_gain.reshape(4, channels), coarse_gains, bias_middle, *fine_weights,
        merge_order, merge_weight, *coarse_weights,
    )

    expand_order = expand_table(rows, cols)
    out = pl.pallas_call(
        last_kernel,
        out_shape=jax.ShapeDtypeStruct((LEVELS * rows * cols, channels), BF16),
        in_specs=[WHOLE] * 8 + [APART] * 7,
        out_specs=WHOLE,
        scratch_shapes=shifted_scratch(quad_rows // 2, quad_cols // 2, wide)
        + [coarse_scratch] + weight_scratch(coarse_weights)
        + [pltpu.VMEM(expand_weight.shape, BF16), pltpu.VMEM(expand_order.shape, BF16)]
        + [dma((6,)), dma((2 * steps,))],
        compiler_params=pltpu.CompilerParams(vmem_limit_bytes=28 << 20),
        name="coarse_shifted_expand",
    )(
        *halo(coarse.reshape(quad_rows // 2, quad_cols // 2, QP, wide), top, bottom),
        coarse_gains, parts, expand_gain[None], bias_last, *coarse_weights,
        expand_weight, expand_order,
    )
    return out.reshape(fields.shape)


def solution(mesh):
    grid = P(None, "lat", LON, None)
    return jax.shard_map(
        on_device,
        mesh=mesh,
        in_specs=(grid, P("lat", LON)) + (P(),) * 18,
        out_specs=grid,
        check_vma=False,
    )
```

```python
import functools

import jax
import jax.numpy as jnp
import numpy as np
from jax import lax
from jax.experimental import pallas as pl
from jax.experimental.pallas import tpu as pltpu
from jax.sharding import PartitionSpec as P

HF = 6
HC = 12
HEAD = 32
WIN_LAT = 6
WIN_LON = 12
WIN_TOK = 144
HALF_LAT = WIN_LAT // 2
HALF_LON = WIN_LON // 2
LEVELS = 2
QUAD = LEVELS * HALF_LAT * HALF_LON
QP = 40
WP = 4 * QP
LO_COUNT = 13
LOG2E = 1.4426950408889634
MASKED = -1e30
VMEM_LIMIT = 60 << 20
LON = ("sec", "head")
F32 = jnp.float32
BF16 = jnp.bfloat16


def quad_sources(row_count, col_count):
    slots = []
    for a in range(row_count // HALF_LAT):
        for b in range(col_count // HALF_LON):
            for s in range(QP):
                if s >= QUAD:
                    slots.append(None)
                    continue
                level, rest = divmod(s, HALF_LAT * HALF_LON)
                r, c = divmod(rest, HALF_LON)
                slots.append((level, a * HALF_LAT + r, b * HALF_LON + c))
    return slots


def one_hot(sources, width):
    table = np.zeros((len(sources), width), np.float32)
    for slot, source in enumerate(sources):
        if source is not None:
            table[slot, source] = 1.0
    return jnp.asarray(table.astype(jnp.bfloat16))


def target_row(targets):
    return jnp.asarray(np.array([-1 if t is None else t for t in targets], np.int32)[None])


def fine_tables(rows, cols):
    slots = quad_sources(rows, cols)
    place = {s: n for n, s in enumerate(slots) if s is not None}
    order = target_row(
        [place[(level, r, c)] for level in range(LEVELS) for r in range(rows) for c in range(cols)]
    )
    of_row = one_hot([None if s is None else s[1] for s in slots], rows)
    of_col = one_hot([None if s is None else s[2] for s in slots], cols)
    return order, of_row, of_col


def merge_table(rows, cols):
    coarse = quad_sources(rows // 2, cols // 2)
    place = {s: n for n, s in enumerate(coarse) if s is not None}
    return target_row(
        [
            None
            if s is None
            else ((s[1] % 2) * 2 + s[2] % 2) * len(coarse) + place[(s[0], s[1] // 2, s[2] // 2)]
            for s in quad_sources(rows, cols)
        ]
    )


def expand_table(rows, cols):
    return target_row(
        [
            None
            if s is None
            else (s[0] * rows + 2 * s[1] + p) * cols + 2 * s[2] + q
            for p in range(2)
            for q in range(2)
            for s in quad_sources(rows // 2, cols // 2)
        ]
    )


def sent_to(target_ref, count):
    width = target_ref.shape[1]
    slot = lax.broadcasted_iota(jnp.int32, (count, width), 0)
    return jnp.where(slot == target_ref[...], 1.0, 0.0).astype(BF16)


def dot(a, b):
    return jnp.dot(a, b, preferred_element_type=F32)


def dot_t(a, b):
    return lax.dot_general(a, b, (((1,), (1,)), ((), ())), preferred_element_type=F32)


def norm(x, gain):
    mean = jnp.mean(x, axis=-1, keepdims=True)
    centered = x - mean
    variance = jnp.mean(centered * centered, axis=-1, keepdims=True)
    return centered * lax.rsqrt(variance + 1e-05) * gain


def attend(q, k, v, bias_ref, first, key_mask):
    n = q.shape[0]
    channels = q.shape[1]
    scale = HEAD**-0.5 * LOG2E
    outs = []
    for tile in range(0, channels, 128):
        width = min(128, channels - tile)
        count = width // HEAD
        qt = q[:, tile : tile + width]
        lane = lax.broadcasted_iota(jnp.int32, (n, width), 1) // HEAD
        masks = [lane == h for h in range(count)]
        stack = jnp.concatenate([jnp.where(m, qt, jnp.zeros_like(qt)) for m in masks], axis=0)
        scores = dot_t(stack, k[:, tile : tile + width])
        probs = []
        for h in range(count):
            head = tile // HEAD + h
            bias = jnp.concatenate(
                [
                    bias_ref[0, head, first : first + n, :],
                    bias_ref[1, head, first : first + n, : WP - 128],
                ],
                axis=1,
            )
            s = scores[h * n : (h + 1) * n] * scale + bias
            if key_mask is not None:
                s = s + key_mask
            s = s - jnp.max(s, axis=-1, keepdims=True)
            probs.append(jnp.exp2(s).astype(BF16))
        probs = jnp.concatenate(probs, axis=0)
        vt = v[:, tile : tile + width]
        mixed = dot(probs, jnp.concatenate([vt, jnp.ones((WP, width), BF16)], axis=1))
        top = mixed[:n, :width]
        total = mixed[:n, width:]
        for h in range(1, count):
            top = jnp.where(masks[h], mixed[h * n : (h + 1) * n, :width], top)
            total = jnp.where(masks[h], mixed[h * n : (h + 1) * n, width:], total)
        outs.append(top / total)
    return outs[0] if len(outs) == 1 else jnp.concatenate(outs, axis=1)


def gelu(x):
    return 0.5 * x * (1.0 + lax.erf(x * np.float32(0.5**0.5)))


def finish(x, context, gain, w_project, w_widen, w_narrow):
    middle = (x + dot(context, w_project)).astype(BF16).astype(F32)
    second = norm(middle, gain).astype(BF16)
    hidden = gelu(dot(second, w_widen)).astype(BF16)
    narrow = dot if w_narrow.shape[0] > w_narrow.shape[1] else dot_t
    return (middle + narrow(hidden, w_narrow)).astype(BF16)


def padded(heads):
    return -(-heads // 8) * 8


def bias_kernel(index_ref, spread_ref, *refs, picks):
    table_refs = refs[:-4]
    out_ref, table, index, left = refs[-4:]
    rows = table.shape[0]
    bias_len = table_refs[0].shape[-1]

    @pl.when(pl.program_id(0) == 0)
    def _():
        spread = spread_ref[...]
        plain = index_ref[...]
        high = (plain >> 4).astype(F32).astype(BF16)
        low = (plain & 15).astype(F32).astype(BF16)

        def moved(part):
            return dot_t(dot(spread, part).astype(BF16), spread).astype(jnp.int32)

        spot = lax.broadcasted_iota(jnp.int32, (WP, WP), 1) % QP
        index[...] = jnp.where(spot < QUAD, moved(high) * 16 + moved(low), bias_len)
        table[...] = jnp.full(table.shape, MASKED, F32)
        at = 0
        for table_ref, block in zip(table_refs, picks):
            heads = table_ref.shape[0]
            for h in range(heads):
                table[at + h : at + h + 1, :bias_len] = (
                    table_ref[h, block : block + 1, :] * LOG2E
                )
            at += padded(heads)
        values = table[...]
        big = values.astype(BF16)
        small = (values - big.astype(F32)).astype(BF16)
        for n, part in enumerate((big, small)):
            left[:, n * 256 : (n + 1) * 256] = jnp.concatenate(
                [part[:, i * 256 : (i + 1) * 256] for i in range(LO_COUNT)], axis=0
            )

    ladder = lax.broadcasted_iota(jnp.int32, (256, 256), 0).astype(F32).astype(BF16)
    lane = lax.broadcasted_iota(jnp.int32, (8, 256), 1) // 32
    sublane = lax.broadcasted_iota(jnp.int32, (8, 256), 0)
    span = out_ref.shape[1] // rows
    for group in range(span // 8):
        first = pl.multiple_of(pl.program_id(0) * span + group * 8, 8)
        entries = index[pl.ds(first, 8), :]
        rest = jnp.concatenate([entries[:, 128:]] * 8, axis=1)
        rest = jnp.sum(jnp.where(lane == sublane, rest, 0).astype(F32), axis=0, keepdims=True)
        pieces = [
            jnp.concatenate([entries[j : j + 1, :128], entries[j + 1 : j + 2, :128]], axis=1)
            for j in range(0, 8, 2)
        ] + [rest.astype(jnp.int32)]
        for t, entry in enumerate(pieces):
            near = (entry & 255).astype(F32).astype(BF16)
            far = entry >> 8
            chosen = jnp.where(ladder == near, jnp.ones((), BF16), jnp.zeros((), BF16))
            found = dot(left[...], jnp.concatenate([chosen, chosen], axis=0))
            total = found[:rows]
            for i in range(1, LO_COUNT):
                total = jnp.where(far == i, found[i * rows : (i + 1) * rows], total)
            for h in range(0, rows, 8):
                part = total[h : h + 8]
                at = h * span + group * 8
                if t < 4:
                    for j in range(2):
                        out_ref[0, pl.ds(at + 2 * t + j, 8, stride=span), :] = (
                            part[:, j * 128 : (j + 1) * 128]
                        )
                else:
                    for j in range(8):
                        moved_part = part[:, j // 4 * 128 : (j // 4 + 1) * 128]
                        if j % 4:
                            moved_part = pltpu.roll(moved_part, 128 - 32 * (j % 4), 1)
                        out_ref[1, pl.ds(at + j, 8, stride=span), :] = moved_part


def bias_of(picks, index, spread, span=32):
    tables = [t.transpose(1, 0, 2) for t, _ in picks]
    rows = sum(padded(t.shape[0]) for t in tables)
    flops = 2 * WP * 256 * WP * LO_COUNT * rows * 4
    steps = WP // span
    whole = pl.BlockSpec(memory_space=pltpu.VMEM)
    out = pl.pallas_call(
        functools.partial(bias_kernel, picks=tuple(b for _, b in picks)),
        out_shape=jax.ShapeDtypeStruct((2, steps * rows * span, 128), F32),
        grid=(steps,),
        in_specs=[whole] * (2 + len(tables)),
        out_specs=pl.BlockSpec((2, rows * span, 128), lambda i: (0, i, 0)),
        scratch_shapes=[
            pltpu.VMEM((rows, LO_COUNT * 256), F32),
            pltpu.VMEM((WP, WP), jnp.int32),
            pltpu.VMEM((rows * LO_COUNT, 512), BF16),
        ],
        compiler_params=pltpu.CompilerParams(vmem_limit_bytes=VMEM_LIMIT),
        cost_estimate=pl.CostEstimate(flops=2 * flops, bytes_accessed=1 << 20, transcendentals=0),
        name="bias_table",
    )(index, spread, *tables)
    return out.reshape(2, steps, rows, span, 128)


def bias_copies(source_ref, bias, first, sems, at):
    steps, span, heads = source_ref.shape[1], source_ref.shape[3], bias.shape[1]
    return [
        pltpu.make_async_copy(
            source_ref.at[half, step, pl.ds(first, heads)],
            bias.at[half, :, pl.ds(step * span, span)],
            sems.at[at + half * steps + step],
        )
        for half in range(2)
        for step in range(steps)
    ]


class Fetched:
    def __init__(self, copies):
        self.copies = copies
        for group in copies:
            for copy in group:
                copy.start()

    def wait(self, *numbers):
        for n in numbers:
            for copy in self.copies[n]:
                copy.wait()


def first_kernel(
    fields_ref, land_ref, embed_ref, order_ref, of_row_ref, of_col_ref, gains_ref,
    bias_hbm, triple_hbm, project_hbm, widen_hbm, narrow_hbm,
    out_ref, top_ref, bottom_ref,
    context, bias, w_triple, w_project, w_widen, w_narrow, sems, bias_sems,
):
    channels = fields_ref.shape[1]
    fetched = Fetched(
        block_copies(
            [(triple_hbm, w_triple), (project_hbm, w_project),
             (widen_hbm, w_widen), (narrow_hbm, w_narrow)], 0, sems, 0,
        )
        + [bias_copies(bias_hbm, bias, 0, bias_sems, 0)]
    )
    land = land_ref[...].astype(F32).astype(BF16)
    on_row = dot(of_row_ref[...], land)
    on_land = jnp.sum(on_row * of_col_ref[...].astype(F32), axis=-1, keepdims=True)
    rows = out_ref.shape[0]
    start = dot(sent_to(order_ref, rows), fields_ref[...]) + on_land * embed_ref[...]
    x = start.astype(BF16).astype(F32)
    normed = norm(x, gains_ref[0, 0:1]).astype(BF16)
    fetched.wait(0)
    triple = dot(normed, w_triple[...]).astype(BF16)
    fetched.wait(4)
    inner = top_ref.shape[0]
    for a in range(rows // inner // 2):
        for b in range(inner // QP // 2):
            top = 2 * a * inner + 2 * b * QP
            below = top + inner
            window = jnp.concatenate(
                [triple[top : top + 2 * QP], triple[below : below + 2 * QP]], axis=0
            )
            mixed = attend(
                window[:, :channels],
                window[:, channels : 2 * channels],
                window[:, 2 * channels :],
                bias, 0, None,
            ).astype(BF16)
            context[top : top + 2 * QP] = mixed[: 2 * QP]
            context[below : below + 2 * QP] = mixed[2 * QP :]
    fetched.wait(1, 2, 3)
    done = finish(
        x, context[...], gains_ref[0, 1:2], w_project[...], w_widen[...], w_narrow[...]
    )
    out_ref[...] = done
    top_ref[...] = done[:inner]
    bottom_ref[...] = done[rows - inner :]


def shifted_block(
    own_ref, north_ref, south_ref, west_ref, east_ref, gains_ref, fetched,
    bias, w_triple, w_project, w_widen, w_narrow, query, key, value, context,
):
    channels = own_ref.shape[1]
    across = north_ref.shape[0] // QP
    down = own_ref.shape[0] // QP // across
    line = (across + 2) * QP
    inner = across * QP
    pieces = []
    for i in range(down + 2):
        if i == 0:
            middle = north_ref[...]
        elif i == down + 1:
            middle = south_ref[...]
        else:
            middle = own_ref[(i - 1) * inner : i * inner]
        pieces += [
            west_ref[i * QP : (i + 1) * QP].astype(F32),
            middle.astype(F32),
            east_ref[i * QP : (i + 1) * QP].astype(F32),
        ]
    normed = norm(jnp.concatenate(pieces, axis=0), gains_ref[1, 0:1]).astype(BF16)
    fetched.wait(1)
    query[...] = dot(normed[line : (down + 1) * line], w_triple[:, :channels])
    both = dot(normed, w_triple[:, channels:]).astype(BF16)
    key[...] = both[:, :channels]
    value[...] = both[:, channels:]
    lane = lax.broadcasted_iota(jnp.int32, (1, WP), 1)
    place = lax.axis_index("lat")
    on_top = jnp.where(place == 0, MASKED, 0.0).astype(F32)
    on_bottom = jnp.where(place == lax.axis_size("lat") - 1, MASKED, 0.0).astype(F32)
    fetched.wait(0)
    for wa in range(down // 2 + 1):
        mask = None
        if wa == 0:
            mask = jnp.where(lane < 2 * QP, on_top, 0.0)
        elif wa == down // 2:
            mask = jnp.where(lane < 2 * QP, 0.0, on_bottom)
        for wb in range(across // 2 + 1):
            at = [(2 * wa + r) * line + 2 * wb * QP for r in range(2)]
            k = jnp.concatenate([key[s : s + 2 * QP] for s in at], axis=0)
            v = jnp.concatenate([value[s : s + 2 * QP] for s in at], axis=0)
            rows = [r for r in range(2) if 0 < 2 * wa + r < down + 1]
            cols = [c for c in range(2) if 0 < 2 * wb + c < across + 1]
            size = len(cols) * QP
            qs = [
                query[
                    (2 * wa + r - 1) * line + (2 * wb + cols[0]) * QP :
                    (2 * wa + r - 1) * line + (2 * wb + cols[0]) * QP + size
                ]
                for r in rows
            ]
            if len(cols) == 2:
                groups = [(rows, jnp.concatenate(qs, axis=0) if len(qs) == 2 else qs[0])]
            else:
                groups = [([r], part) for r, part in zip(rows, qs)]
            for group, q in groups:
                out = attend(
                    q.astype(BF16), k, v, bias, (2 * group[0] + cols[0]) * QP, mask
                )
                for n, r in enumerate(group):
                    to = ((2 * wa + r - 1) * across + 2 * wb + cols[0] - 1) * QP
                    context[to : to + size] = out[n * size : (n + 1) * size]
    fetched.wait(2, 3, 4)
    return finish(
        own_ref[...].astype(F32), context[...].astype(BF16), gains_ref[1, 1:2],
        w_project[...], w_widen[...], w_narrow[...],
    )


def block_copies(pairs, block, sems, at):
    return [
        [pltpu.make_async_copy(source.at[block], target, sems.at[at + n])]
        for n, (source, target) in enumerate(pairs)
    ]


def middle_kernel(
    own_ref, north_ref, south_ref, west_ref, east_ref, gains_ref, merge_gain_ref,
    coarse_gains_ref, merge_order_ref, bias_hbm, triple_hbm, project_hbm, widen_hbm, narrow_hbm,
    merge_weight_hbm, c_triple_hbm, c_project_hbm, c_widen_hbm, c_narrow_hbm,
    parts_ref, coarse_ref, top_ref, bottom_ref,
    query, key, value, context, bias, c_bias, w_triple, w_project, w_widen, w_narrow,
    merge_weight, c_triple, c_project, c_widen, c_narrow, sems, bias_sems,
):
    steps = bias_hbm.shape[1]
    heads = bias.shape[1]
    fetched = Fetched(
        [bias_copies(bias_hbm, bias, 0, bias_sems, 0)]
        + block_copies(
            [(triple_hbm, w_triple), (project_hbm, w_project),
             (widen_hbm, w_widen), (narrow_hbm, w_narrow)], 1, sems, 0,
        )
        + [
            [pltpu.make_async_copy(merge_weight_hbm, merge_weight, sems.at[4])],
            bias_copies(bias_hbm, c_bias, padded(heads), bias_sems, 2 * steps),
        ]
        + block_copies(
            [(c_triple_hbm, c_triple), (c_project_hbm, c_project),
             (c_widen_hbm, c_widen), (c_narrow_hbm, c_narrow)], 0, sems, 5,
        )
    )
    skip = shifted_block(
        own_ref, north_ref, south_ref, west_ref, east_ref, gains_ref, fetched,
        bias, w_triple, w_project, w_widen, w_narrow, query, key, value, context,
    )
    channels = own_ref.shape[1]
    grouped = dot(sent_to(merge_order_ref, skip.shape[0]), skip)
    parts_ref[...] = grouped.astype(BF16)
    parts = [grouped[i * WP : (i + 1) * WP] for i in range(4)]
    width = 4 * channels
    mean = sum(jnp.sum(p, axis=-1, keepdims=True) for p in parts) / width
    parts = [p - mean for p in parts]
    variance = sum(jnp.sum(p * p, axis=-1, keepdims=True) for p in parts) / width
    factor = lax.rsqrt(variance + 1e-05)
    fetched.wait(5)
    coarse = jnp.zeros((WP, merge_weight.shape[1]), F32)
    for i, p in enumerate(parts):
        merged = (p * factor * merge_gain_ref[i : i + 1]).astype(BF16)
        coarse = coarse + dot(merged, merge_weight[i * channels : (i + 1) * channels])
    x = coarse.astype(BF16).astype(F32)
    wide = x.shape[1]
    normed = norm(x, coarse_gains_ref[0, 0:1]).astype(BF16)
    fetched.wait(6, 7)
    triple = dot(normed, c_triple[...]).astype(BF16)
    mixed = attend(
        triple[:, :wide], triple[:, wide : 2 * wide], triple[:, 2 * wide :], c_bias, 0, None
    ).astype(BF16)
    fetched.wait(8, 9, 10)
    done = finish(
        x, mixed, coarse_gains_ref[0, 1:2], c_project[...], c_widen[...], c_narrow[...]
    )
    coarse_ref[...] = done
    inner = top_ref.shape[0]
    top_ref[...] = done[:inner]
    bottom_ref[...] = done[WP - inner :]


def last_kernel(
    own_ref, north_ref, south_ref, west_ref, east_ref, gains_ref, parts_ref, expand_gain_ref,
    expand_order_ref, bias_hbm, triple_hbm, project_hbm, widen_hbm, narrow_hbm, expand_weight_hbm,
    out_ref,
    query, key, value, context, bias, w_triple, w_project, w_widen, w_narrow,
    expand_weight, sems, bias_sems,
):
    fetched = Fetched(
        [bias_copies(bias_hbm, bias, 0, bias_sems, 0)]
        + block_copies(
            [(triple_hbm, w_triple), (project_hbm, w_project),
             (widen_hbm, w_widen), (narrow_hbm, w_narrow)], 1, sems, 0,
        )
        + [[pltpu.make_async_copy(expand_weight_hbm, expand_weight, sems.at[4])]]
    )
    deep = shifted_block(
        own_ref, north_ref, south_ref, west_ref, east_ref, gains_ref, fetched,
        bias, w_triple, w_project, w_widen, w_narrow, query, key, value, context,
    )
    channels = parts_ref.shape[1]
    fetched.wait(5)
    widened = dot(deep, expand_weight[...])
    outs = []
    for i in range(4):
        shuffled = widened[:, i * channels : (i + 1) * channels]
        skip = parts_ref[i * WP : (i + 1) * WP].astype(F32)
        outs.append((skip + norm(shuffled, expand_gain_ref[...])).astype(BF16))
    moves = sent_to(expand_order_ref, out_ref.shape[0])
    out_ref[...] = dot(moves, jnp.concatenate(outs, axis=0)).astype(BF16)


WHOLE = pl.BlockSpec(memory_space=pltpu.VMEM)
APART = pl.BlockSpec(memory_space=pltpu.HBM)


def weight_scratch(weights):
    return [pltpu.VMEM(w.shape[1:], BF16) for w in weights]


def halo(own, top, bottom):
    rows, cols, _, channels = own.shape
    top = top.reshape(own.shape[1:])
    bottom = bottom.reshape(own.shape[1:])
    lat = lax.axis_size("lat")
    lon = lax.axis_size(LON)
    down = [(i, (i + 1) % lat) for i in range(lat)]
    up = [((i + 1) % lat, i) for i in range(lat)]
    east = [(i, (i + 1) % lon) for i in range(lon)]
    west = [((i + 1) % lon, i) for i in range(lon)]
    north = lax.ppermute(bottom, "lat", down)
    south = lax.ppermute(top, "lat", up)

    def side(c):
        return jnp.concatenate([north[c : c + 1], own[:, c], south[c : c + 1]], axis=0)

    from_west = lax.ppermute(side(cols - 1), LON, east)
    from_east = lax.ppermute(side(0), LON, west)
    return [v.reshape(-1, channels) for v in (own, north, south, from_west, from_east)]


def shifted_scratch(rows, cols, channels):
    line = (cols + 2) * QP
    return [
        pltpu.VMEM((rows * line, channels), F32),
        pltpu.VMEM(((rows + 2) * line, channels), BF16),
        pltpu.VMEM(((rows + 2) * line, channels), BF16),
        pltpu.VMEM((rows * cols * QP, channels), F32),
    ]


def on_device(
    fields, land_sea, land_embed, bias_index, fine_bias, fine_gains, fine_query_key_value,
    fine_project, fine_widen, fine_narrow, merge_gain, merge_weight, coarse_bias, coarse_gains,
    coarse_query_key_value, coarse_project, coarse_widen, coarse_narrow, expand_weight, expand_gain,
):
    _, rows, cols, channels = fields.shape
    quad_rows, quad_cols = rows // HALF_LAT, cols // HALF_LON
    tokens = quad_rows * quad_cols * QP
    wide = merge_weight.shape[1]
    spread = one_hot(
        [None if s is None else (s[0] * WIN_LAT + s[1]) * WIN_LON + s[2]
         for s in quad_sources(WIN_LAT, WIN_LON)],
        WIN_TOK,
    )
    order, of_row, of_col = fine_tables(rows, cols)
    bias_first = bias_of([(fine_bias, 0)], bias_index, spread)
    bias_middle = bias_of([(fine_bias, 1), (coarse_bias, 0)], bias_index, spread)
    bias_last = bias_of([(coarse_bias, 1)], bias_index, spread)
    fine_weights = (
        fine_query_key_value, fine_project, fine_widen, fine_narrow.transpose(0, 2, 1)
    )
    coarse_weights = (coarse_query_key_value, coarse_project, coarse_widen, coarse_narrow)
    steps = bias_first.shape[1]
    dma = pltpu.SemaphoreType.DMA
    fine_scratch = pltpu.VMEM((2, HF, WP, 128), F32)
    coarse_scratch = pltpu.VMEM((2, HC, WP, 128), F32)
    line = quad_cols * QP

    first, top, bottom = pl.pallas_call(
        first_kernel,
        out_shape=[
            jax.ShapeDtypeStruct((tokens, channels), BF16),
            jax.ShapeDtypeStruct((line, channels), BF16),
            jax.ShapeDtypeStruct((line, channels), BF16),
        ],
        in_specs=[WHOLE] * 7 + [APART] * 5,
        out_specs=[WHOLE] * 3,
        scratch_shapes=[pltpu.VMEM((tokens, channels), BF16), fine_scratch]
        + weight_scratch(fine_weights) + [dma((4,)), dma((2 * steps,))],
        compiler_params=pltpu.CompilerParams(vmem_limit_bytes=VMEM_LIMIT),
        name="fine_plain",
    )(
        fields.reshape(-1, channels), land_sea, land_embed[None], order, of_row, of_col,
        fine_gains, bias_first, *fine_weights,
    )

    parts, coarse, top, bottom = pl.pallas_call(
        middle_kernel,
        out_shape=[
            jax.ShapeDtypeStruct((tokens, channels), BF16),
            jax.ShapeDtypeStruct((tokens // 4, wide), BF16),
            jax.ShapeDtypeStruct((line // 2, wide), BF16),
            jax.ShapeDtypeStruct((line // 2, wide), BF16),
        ],
        in_specs=[WHOLE] * 9 + [APART] * 10,
        out_specs=[WHOLE] * 4,
        scratch_shapes=shifted_scratch(quad_rows, quad_cols, channels)
        + [fine_scratch, coarse_scratch] + weight_scratch(fine_weights)
        + [pltpu.VMEM(merge_weight.shape, BF16)]
        + weight_scratch(coarse_weights) + [dma((9,)), dma((4 * steps,))],
        compiler_params=pltpu.CompilerParams(vmem_limit_bytes=VMEM_LIMIT),
        name="fine_shifted_coarse_plain",
    )(
        *halo(first.reshape(quad_rows, quad_cols, QP, channels), top, bottom),
        fine_gains, merge_gain.reshape(4, channels), coarse_gains,
        merge_table(rows, cols), bias_middle, *fine_weights, merge_weight, *coarse_weights,
    )

    out = pl.pallas_call(
        last_kernel,
        out_shape=jax.ShapeDtypeStruct((LEVELS * rows * cols, channels), BF16),
        in_specs=[WHOLE] * 9 + [APART] * 6,
        out_specs=WHOLE,
        scratch_shapes=shifted_scratch(quad_rows // 2, quad_cols // 2, wide)
        + [coarse_scratch] + weight_scratch(coarse_weights)
        + [pltpu.VMEM(expand_weight.shape, BF16)]
        + [dma((5,)), dma((2 * steps,))],
        compiler_params=pltpu.CompilerParams(vmem_limit_bytes=VMEM_LIMIT),
        name="coarse_shifted_expand",
    )(
        *halo(coarse.reshape(quad_rows // 2, quad_cols // 2, QP, wide), top, bottom),
        coarse_gains, parts, expand_gain[None], expand_table(rows, cols),
        bias_last, *coarse_weights, expand_weight,
    )
    return out.reshape(fields.shape)


def solution(mesh):
    grid = P(None, "lat", LON, None)
    return jax.shard_map(
        on_device,
        mesh=mesh,
        in_specs=(grid, P("lat", LON)) + (P(),) * 18,
        out_specs=grid,
        check_vma=False,
    )
```

```python
import functools

import jax
import jax.numpy as jnp
import numpy as np
from jax import lax
from jax.experimental import pallas as pl
from jax.experimental.pallas import tpu as pltpu
from jax.sharding import PartitionSpec as P

HF = 6
HC = 12
HEAD = 32
WIN_LAT = 6
WIN_LON = 12
WIN_TOK = 144
HALF_LAT = WIN_LAT // 2
HALF_LON = WIN_LON // 2
LEVELS = 2
QUAD = LEVELS * HALF_LAT * HALF_LON
QP = 40
WP = 4 * QP
LO_COUNT = 13
LOG2E = 1.4426950408889634
MASKED = -1e30
LON = ("sec", "head")
F32 = jnp.float32
BF16 = jnp.bfloat16


def quad_sources(row_count, col_count):
    slots = []
    for a in range(row_count // HALF_LAT):
        for b in range(col_count // HALF_LON):
            for s in range(QP):
                if s >= QUAD:
                    slots.append(None)
                    continue
                level, rest = divmod(s, HALF_LAT * HALF_LON)
                r, c = divmod(rest, HALF_LON)
                slots.append((level, a * HALF_LAT + r, b * HALF_LON + c))
    return slots


def one_hot(sources, width):
    table = np.zeros((len(sources), width), np.float32)
    for slot, source in enumerate(sources):
        if source is not None:
            table[slot, source] = 1.0
    return jnp.asarray(table.astype(jnp.bfloat16))


def target_row(targets):
    return jnp.asarray(np.array([-1 if t is None else t for t in targets], np.int32)[None])


def fine_tables(rows, cols):
    slots = quad_sources(rows, cols)
    place = {s: n for n, s in enumerate(slots) if s is not None}
    order = target_row(
        [place[(level, r, c)] for level in range(LEVELS) for r in range(rows) for c in range(cols)]
    )
    of_row = one_hot([None if s is None else s[1] for s in slots], rows)
    of_col = one_hot([None if s is None else s[2] for s in slots], cols)
    return order, of_row, of_col


def merge_table(rows, cols):
    coarse = quad_sources(rows // 2, cols // 2)
    place = {s: n for n, s in enumerate(coarse) if s is not None}
    return target_row(
        [
            None
            if s is None
            else ((s[1] % 2) * 2 + s[2] % 2) * len(coarse) + place[(s[0], s[1] // 2, s[2] // 2)]
            for s in quad_sources(rows, cols)
        ]
    )


def expand_table(rows, cols):
    return target_row(
        [
            None
            if s is None
            else (s[0] * rows + 2 * s[1] + p) * cols + 2 * s[2] + q
            for p in range(2)
            for q in range(2)
            for s in quad_sources(rows // 2, cols // 2)
        ]
    )


def sent_to(target_ref, count):
    width = target_ref.shape[1]
    slot = lax.broadcasted_iota(jnp.int32, (count, width), 0)
    return jnp.where(slot == target_ref[...], 1.0, 0.0).astype(BF16)


def dot(a, b):
    return jnp.dot(a, b, preferred_element_type=F32)


def dot_t(a, b):
    return lax.dot_general(a, b, (((1,), (1,)), ((), ())), preferred_element_type=F32)


def norm(x, gain):
    mean = jnp.mean(x, axis=-1, keepdims=True)
    centered = x - mean
    variance = jnp.mean(centered * centered, axis=-1, keepdims=True)
    return centered * lax.rsqrt(variance + 1e-05) * gain


def attend(q, k, v, bias_ref, first, key_mask):
    n = q.shape[0]
    channels = q.shape[1]
    scale = HEAD**-0.5 * LOG2E
    outs = []
    for tile in range(0, channels, 128):
        width = min(128, channels - tile)
        count = width // HEAD
        qt = q[:, tile : tile + width]
        lane = lax.broadcasted_iota(jnp.int32, (n, width), 1) // HEAD
        masks = [lane == h for h in range(count)]
        stack = jnp.concatenate([jnp.where(m, qt, jnp.zeros_like(qt)) for m in masks], axis=0)
        scores = dot_t(stack, k[:, tile : tile + width])
        probs = []
        for h in range(count):
            head = tile // HEAD + h
            bias = jnp.concatenate(
                [
                    bias_ref[0, head, first : first + n, :],
                    bias_ref[1, head, first : first + n, : WP - 128],
                ],
                axis=1,
            )
            s = scores[h * n : (h + 1) * n] * scale + bias
            if key_mask is not None:
                s = s + key_mask
            s = s - jnp.max(s, axis=-1, keepdims=True)
            probs.append(jnp.exp2(s).astype(BF16))
        probs = jnp.concatenate(probs, axis=0)
        vt = v[:, tile : tile + width]
        mixed = dot(probs, jnp.concatenate([vt, jnp.ones((WP, width), BF16)], axis=1))
        top = mixed[:n, :width]
        total = mixed[:n, width:]
        for h in range(1, count):
            top = jnp.where(masks[h], mixed[h * n : (h + 1) * n, :width], top)
            total = jnp.where(masks[h], mixed[h * n : (h + 1) * n, width:], total)
        outs.append(top / total)
    return outs[0] if len(outs) == 1 else jnp.concatenate(outs, axis=1)


def gelu(x):
    return 0.5 * x * (1.0 + lax.erf(x * np.float32(0.5**0.5)))


def finish(x, context, gain, w_project, w_widen, w_narrow):
    middle = (x + dot(context, w_project)).astype(BF16).astype(F32)
    second = norm(middle, gain).astype(BF16)
    hidden = gelu(dot(second, w_widen)).astype(BF16)
    narrow = dot if w_narrow.shape[0] > w_narrow.shape[1] else dot_t
    return (middle + narrow(hidden, w_narrow)).astype(BF16)


def padded(heads):
    return -(-heads // 8) * 8


def bias_kernel(*refs, picks, fresh):
    if fresh:
        index_ref, spread_ref, *table_refs, out_ref, index, table, left = refs
    else:
        index, *table_refs, out_ref, table, left = refs
    rows = table.shape[0]
    bias_len = table_refs[0].shape[-1]

    @pl.when(pl.program_id(0) == 0)
    def _():
        if fresh:
            spread = spread_ref[...]
            plain = index_ref[...]
            high = (plain >> 4).astype(F32).astype(BF16)
            low = (plain & 15).astype(F32).astype(BF16)

            def moved(part):
                return dot_t(dot(spread, part).astype(BF16), spread).astype(jnp.int32)

            spot = lax.broadcasted_iota(jnp.int32, (WP, WP), 1) % QP
            index[...] = jnp.where(spot < QUAD, moved(high) * 16 + moved(low), bias_len)
        table[...] = jnp.full(table.shape, MASKED, F32)
        at = 0
        for table_ref, block in zip(table_refs, picks):
            heads = table_ref.shape[0]
            for h in range(heads):
                table[at + h : at + h + 1, :bias_len] = (
                    table_ref[h, block : block + 1, :] * LOG2E
                )
            at += padded(heads)
        values = table[...]
        big = values.astype(BF16)
        small = (values - big.astype(F32)).astype(BF16)
        for n, part in enumerate((big, small)):
            left[:, n * 256 : (n + 1) * 256] = jnp.concatenate(
                [part[:, i * 256 : (i + 1) * 256] for i in range(LO_COUNT)], axis=0
            )

    ladder = lax.broadcasted_iota(jnp.int32, (256, 256), 0).astype(F32).astype(BF16)
    lane = lax.broadcasted_iota(jnp.int32, (8, 256), 1) // 32
    sublane = lax.broadcasted_iota(jnp.int32, (8, 256), 0)
    span = out_ref.shape[1] // rows
    for group in range(span // 8):
        first = pl.multiple_of(pl.program_id(0) * span + group * 8, 8)
        entries = index[pl.ds(first, 8), :]
        rest = jnp.concatenate([entries[:, 128:]] * 8, axis=1)
        rest = jnp.sum(jnp.where(lane == sublane, rest, 0).astype(F32), axis=0, keepdims=True)
        pieces = [
            jnp.concatenate([entries[j : j + 1, :128], entries[j + 1 : j + 2, :128]], axis=1)
            for j in range(0, 8, 2)
        ] + [rest.astype(jnp.int32)]
        for t, entry in enumerate(pieces):
            near = (entry & 255).astype(F32).astype(BF16)
            far = entry >> 8
            chosen = jnp.where(ladder == near, jnp.ones((), BF16), jnp.zeros((), BF16))
            found = dot(left[...], jnp.concatenate([chosen, chosen], axis=0))
            total = found[:rows]
            for i in range(1, LO_COUNT):
                total = jnp.where(far == i, found[i * rows : (i + 1) * rows], total)
            for h in range(0, rows, 8):
                part = total[h : h + 8]
                at = h * span + group * 8
                if t < 4:
                    for j in range(2):
                        out_ref[0, pl.ds(at + 2 * t + j, 8, stride=span), :] = (
                            part[:, j * 128 : (j + 1) * 128]
                        )
                else:
                    for j in range(8):
                        moved_part = part[:, j // 4 * 128 : (j // 4 + 1) * 128]
                        if j % 4:
                            moved_part = pltpu.roll(moved_part, 128 - 32 * (j % 4), 1)
                        out_ref[1, pl.ds(at + j, 8, stride=span), :] = moved_part


def bias_of(picks, order, vmem, span=32):
    tables = [t.transpose(1, 0, 2) for t, _ in picks]
    rows = sum(padded(t.shape[0]) for t in tables)
    flops = 2 * WP * 256 * WP * LO_COUNT * rows * 4
    steps = WP // span
    fresh = len(order) == 2
    out_shape = [jax.ShapeDtypeStruct((2, steps * rows * span, 128), F32)]
    out_specs = [pl.BlockSpec((2, rows * span, 128), lambda i: (0, i, 0))]
    if fresh:
        out_shape.append(jax.ShapeDtypeStruct((WP, WP), jnp.int32))
        out_specs.append(pl.BlockSpec((WP, WP), lambda i: (0, 0)))
    out = pl.pallas_call(
        functools.partial(bias_kernel, picks=tuple(b for _, b in picks), fresh=fresh),
        out_shape=out_shape,
        grid=(steps,),
        in_specs=[pl.BlockSpec(memory_space=pltpu.VMEM)] * (len(order) + len(tables)),
        out_specs=out_specs,
        scratch_shapes=[
            pltpu.VMEM((rows, LO_COUNT * 256), F32),
            pltpu.VMEM((rows * LO_COUNT, 512), BF16),
        ],
        compiler_params=pltpu.CompilerParams(vmem_limit_bytes=vmem << 20),
        cost_estimate=pl.CostEstimate(flops=2 * flops, bytes_accessed=1 << 20, transcendentals=0),
        name="bias_table",
    )(*order, *tables)
    return [out[0].reshape(2, steps, rows, span, 128)] + list(out[1:])


def bias_copies(source_ref, bias, first, sems, at):
    steps, span, heads = source_ref.shape[1], source_ref.shape[3], bias.shape[1]
    return [
        pltpu.make_async_copy(
            source_ref.at[half, step, pl.ds(first, heads)],
            bias.at[half, :, pl.ds(step * span, span)],
            sems.at[at + half * steps + step],
        )
        for half in range(2)
        for step in range(steps)
    ]


class Fetched:
    def __init__(self, copies):
        self.copies = copies
        for group in copies[1:2] + copies[:1] + copies[2:]:
            for copy in group:
                copy.start()

    def wait(self, *numbers):
        for n in numbers:
            for copy in self.copies[n]:
                copy.wait()


def first_kernel(
    fields_ref, land_ref, embed_ref, order_ref, of_row_ref, of_col_ref, gains_ref,
    bias_hbm, triple_hbm, project_hbm, widen_hbm, narrow_hbm,
    out_ref, top_ref, bottom_ref,
    context, bias, w_triple, w_project, w_widen, w_narrow, sems, bias_sems,
):
    channels = fields_ref.shape[1]
    fetched = Fetched(
        [bias_copies(bias_hbm, bias, 0, bias_sems, 0)]
        + block_copies(
            [(triple_hbm, w_triple), (project_hbm, w_project),
             (widen_hbm, w_widen), (narrow_hbm, w_narrow)], 0, sems, 0,
        )
    )
    land = land_ref[...].astype(F32).astype(BF16)
    on_row = dot(of_row_ref[...], land)
    on_land = jnp.sum(on_row * of_col_ref[...].astype(F32), axis=-1, keepdims=True)
    rows = out_ref.shape[0]
    start = dot(sent_to(order_ref, rows), fields_ref[...]) + on_land * embed_ref[...]
    x = start.astype(BF16).astype(F32)
    normed = norm(x, gains_ref[0, 0:1]).astype(BF16)
    fetched.wait(1)
    triple = dot(normed, w_triple[...]).astype(BF16)
    fetched.wait(0)
    inner = top_ref.shape[0]
    for a in range(rows // inner // 2):
        for b in range(inner // QP // 2):
            top = 2 * a * inner + 2 * b * QP
            below = top + inner
            window = jnp.concatenate(
                [triple[top : top + 2 * QP], triple[below : below + 2 * QP]], axis=0
            )
            mixed = attend(
                window[:, :channels],
                window[:, channels : 2 * channels],
                window[:, 2 * channels :],
                bias, 0, None,
            ).astype(BF16)
            context[top : top + 2 * QP] = mixed[: 2 * QP]
            context[below : below + 2 * QP] = mixed[2 * QP :]
    fetched.wait(2, 3, 4)
    done = finish(
        x, context[...], gains_ref[0, 1:2], w_project[...], w_widen[...], w_narrow[...]
    )
    out_ref[...] = done
    top_ref[...] = done[:inner]
    bottom_ref[...] = done[rows - inner :]


def shifted_block(
    own_ref, north_ref, south_ref, west_ref, east_ref, gains_ref, fetched,
    bias, w_triple, w_project, w_widen, w_narrow, query, key, value, context,
):
    channels = own_ref.shape[1]
    across = north_ref.shape[0] // QP
    down = own_ref.shape[0] // QP // across
    line = (across + 2) * QP
    inner = across * QP
    pieces = []
    for i in range(down + 2):
        if i == 0:
            middle = north_ref[...]
        elif i == down + 1:
            middle = south_ref[...]
        else:
            middle = own_ref[(i - 1) * inner : i * inner]
        pieces += [
            west_ref[i * QP : (i + 1) * QP].astype(F32),
            middle.astype(F32),
            east_ref[i * QP : (i + 1) * QP].astype(F32),
        ]
    normed = norm(jnp.concatenate(pieces, axis=0), gains_ref[1, 0:1]).astype(BF16)
    fetched.wait(1)
    query[...] = dot(normed[line : (down + 1) * line], w_triple[:, :channels])
    both = dot(normed, w_triple[:, channels:]).astype(BF16)
    key[...] = both[:, :channels]
    value[...] = both[:, channels:]
    lane = lax.broadcasted_iota(jnp.int32, (1, WP), 1)
    place = lax.axis_index("lat")
    on_top = jnp.where(place == 0, MASKED, 0.0).astype(F32)
    on_bottom = jnp.where(place == lax.axis_size("lat") - 1, MASKED, 0.0).astype(F32)
    fetched.wait(0)
    for wa in range(down // 2 + 1):
        mask = None
        if wa == 0:
            mask = jnp.where(lane < 2 * QP, on_top, 0.0)
        elif wa == down // 2:
            mask = jnp.where(lane < 2 * QP, 0.0, on_bottom)
        for wb in range(across // 2 + 1):
            at = [(2 * wa + r) * line + 2 * wb * QP for r in range(2)]
            k = jnp.concatenate([key[s : s + 2 * QP] for s in at], axis=0)
            v = jnp.concatenate([value[s : s + 2 * QP] for s in at], axis=0)
            rows = [r for r in range(2) if 0 < 2 * wa + r < down + 1]
            cols = [c for c in range(2) if 0 < 2 * wb + c < across + 1]
            size = len(cols) * QP
            qs = [
                query[
                    (2 * wa + r - 1) * line + (2 * wb + cols[0]) * QP :
                    (2 * wa + r - 1) * line + (2 * wb + cols[0]) * QP + size
                ]
                for r in rows
            ]
            if len(cols) == 2:
                groups = [(rows, jnp.concatenate(qs, axis=0) if len(qs) == 2 else qs[0])]
            else:
                groups = [([r], part) for r, part in zip(rows, qs)]
            for group, q in groups:
                out = attend(
                    q.astype(BF16), k, v, bias, (2 * group[0] + cols[0]) * QP, mask
                )
                for n, r in enumerate(group):
                    to = ((2 * wa + r - 1) * across + 2 * wb + cols[0] - 1) * QP
                    context[to : to + size] = out[n * size : (n + 1) * size]
    fetched.wait(2, 3, 4)
    return finish(
        own_ref[...].astype(F32), context[...].astype(BF16), gains_ref[1, 1:2],
        w_project[...], w_widen[...], w_narrow[...],
    )


def block_copies(pairs, block, sems, at):
    return [
        [pltpu.make_async_copy(source.at[block], target, sems.at[at + n])]
        for n, (source, target) in enumerate(pairs)
    ]


def middle_kernel(
    own_ref, north_ref, south_ref, west_ref, east_ref, gains_ref, merge_gain_ref,
    coarse_gains_ref, merge_order_ref, bias_hbm, triple_hbm, project_hbm, widen_hbm, narrow_hbm,
    merge_weight_hbm, c_triple_hbm, c_project_hbm, c_widen_hbm, c_narrow_hbm,
    parts_ref, coarse_ref, top_ref, bottom_ref,
    query, key, value, context, bias, c_bias, w_triple, w_project, w_widen, w_narrow,
    merge_weight, c_triple, c_project, c_widen, c_narrow, sems, bias_sems,
):
    steps = bias_hbm.shape[1]
    heads = bias.shape[1]
    fetched = Fetched(
        [bias_copies(bias_hbm, bias, 0, bias_sems, 0)]
        + block_copies(
            [(triple_hbm, w_triple), (project_hbm, w_project),
             (widen_hbm, w_widen), (narrow_hbm, w_narrow)], 1, sems, 0,
        )
        + [
            [pltpu.make_async_copy(merge_weight_hbm, merge_weight, sems.at[4])],
            bias_copies(bias_hbm, c_bias, padded(heads), bias_sems, 2 * steps),
        ]
        + block_copies(
            [(c_triple_hbm, c_triple), (c_project_hbm, c_project),
             (c_widen_hbm, c_widen), (c_narrow_hbm, c_narrow)], 0, sems, 5,
        )
    )
    skip = shifted_block(
        own_ref, north_ref, south_ref, west_ref, east_ref, gains_ref, fetched,
        bias, w_triple, w_project, w_widen, w_narrow, query, key, value, context,
    )
    channels = own_ref.shape[1]
    grouped = dot(sent_to(merge_order_ref, skip.shape[0]), skip)
    parts_ref[...] = grouped.astype(BF16)
    parts = [grouped[i * WP : (i + 1) * WP] for i in range(4)]
    width = 4 * channels
    mean = sum(jnp.sum(p, axis=-1, keepdims=True) for p in parts) / width
    parts = [p - mean for p in parts]
    variance = sum(jnp.sum(p * p, axis=-1, keepdims=True) for p in parts) / width
    factor = lax.rsqrt(variance + 1e-05)
    merge_gain = merge_gain_ref[...].reshape(1, width)
    fetched.wait(5)
    coarse = jnp.zeros((WP, merge_weight.shape[1]), F32)
    for i, p in enumerate(parts):
        gain = merge_gain[:, i * channels : (i + 1) * channels]
        merged = (p * factor * gain).astype(BF16)
        coarse = coarse + dot(merged, merge_weight[i * channels : (i + 1) * channels])
    x = coarse.astype(BF16).astype(F32)
    wide = x.shape[1]
    normed = norm(x, coarse_gains_ref[0, 0:1]).astype(BF16)
    fetched.wait(6, 7)
    triple = dot(normed, c_triple[...]).astype(BF16)
    mixed = attend(
        triple[:, :wide], triple[:, wide : 2 * wide], triple[:, 2 * wide :], c_bias, 0, None
    ).astype(BF16)
    fetched.wait(8, 9, 10)
    done = finish(
        x, mixed, coarse_gains_ref[0, 1:2], c_project[...], c_widen[...], c_narrow[...]
    )
    coarse_ref[...] = done
    inner = top_ref.shape[0]
    top_ref[...] = done[:inner]
    bottom_ref[...] = done[WP - inner :]


def last_kernel(
    own_ref, north_ref, south_ref, west_ref, east_ref, gains_ref, parts_ref, expand_gain_ref,
    expand_order_ref, bias_hbm, triple_hbm, project_hbm, widen_hbm, narrow_hbm, expand_weight_hbm,
    out_ref,
    query, key, value, context, bias, w_triple, w_project, w_widen, w_narrow,
    expand_weight, sems, bias_sems,
):
    fetched = Fetched(
        [bias_copies(bias_hbm, bias, 0, bias_sems, 0)]
        + block_copies(
            [(triple_hbm, w_triple), (project_hbm, w_project),
             (widen_hbm, w_widen), (narrow_hbm, w_narrow)], 1, sems, 0,
        )
        + [[pltpu.make_async_copy(expand_weight_hbm, expand_weight, sems.at[4])]]
    )
    deep = shifted_block(
        own_ref, north_ref, south_ref, west_ref, east_ref, gains_ref, fetched,
        bias, w_triple, w_project, w_widen, w_narrow, query, key, value, context,
    )
    channels = parts_ref.shape[1]
    fetched.wait(5)
    widened = dot(deep, expand_weight[...])
    outs = []
    for i in range(4):
        shuffled = widened[:, i * channels : (i + 1) * channels]
        skip = parts_ref[i * WP : (i + 1) * WP].astype(F32)
        outs.append((skip + norm(shuffled, expand_gain_ref[...])).astype(BF16))
    moves = sent_to(expand_order_ref, out_ref.shape[0])
    out_ref[...] = dot(moves, jnp.concatenate(outs, axis=0)).astype(BF16)


WHOLE = pl.BlockSpec(memory_space=pltpu.VMEM)
APART = pl.BlockSpec(memory_space=pltpu.HBM)


def weight_scratch(weights):
    return [pltpu.VMEM(w.shape[1:], BF16) for w in weights]


def halo(own, top, bottom):
    rows, cols, _, channels = own.shape
    top = top.reshape(own.shape[1:])
    bottom = bottom.reshape(own.shape[1:])
    lat = lax.axis_size("lat")
    lon = lax.axis_size(LON)
    down = [(i, (i + 1) % lat) for i in range(lat)]
    up = [((i + 1) % lat, i) for i in range(lat)]
    east = [(i, (i + 1) % lon) for i in range(lon)]
    west = [((i + 1) % lon, i) for i in range(lon)]
    north = lax.ppermute(bottom, "lat", down)
    south = lax.ppermute(top, "lat", up)

    def side(c):
        return jnp.concatenate([north[c : c + 1], own[:, c], south[c : c + 1]], axis=0)

    from_west = lax.ppermute(side(cols - 1), LON, east)
    from_east = lax.ppermute(side(0), LON, west)
    return [v.reshape(-1, channels) for v in (own, north, south, from_west, from_east)]


def shifted_scratch(rows, cols, channels):
    line = (cols + 2) * QP
    return [
        pltpu.VMEM((rows * line, channels), F32),
        pltpu.VMEM(((rows + 2) * line, channels), BF16),
        pltpu.VMEM(((rows + 2) * line, channels), BF16),
        pltpu.VMEM((rows * cols * QP, channels), F32),
    ]


def on_device(
    fields, land_sea, land_embed, bias_index, fine_bias, fine_gains, fine_query_key_value,
    fine_project, fine_widen, fine_narrow, merge_gain, merge_weight, coarse_bias, coarse_gains,
    coarse_query_key_value, coarse_project, coarse_widen, coarse_narrow, expand_weight, expand_gain,
):
    _, rows, cols, channels = fields.shape
    quad_rows, quad_cols = rows // HALF_LAT, cols // HALF_LON
    tokens = quad_rows * quad_cols * QP
    wide = merge_weight.shape[1]
    spread = one_hot(
        [None if s is None else (s[0] * WIN_LAT + s[1]) * WIN_LON + s[2]
         for s in quad_sources(WIN_LAT, WIN_LON)],
        WIN_TOK,
    )
    order, of_row, of_col = fine_tables(rows, cols)
    bias_first, ordered = bias_of([(fine_bias, 0)], (bias_index, spread), 16)
    (bias_middle,) = bias_of([(fine_bias, 1), (coarse_bias, 0)], (ordered,), 16)
    (bias_last,) = bias_of([(coarse_bias, 1)], (ordered,), 16)
    fine_weights = (
        fine_query_key_value, fine_project, fine_widen, fine_narrow.transpose(0, 2, 1)
    )
    coarse_weights = (coarse_query_key_value, coarse_project, coarse_widen, coarse_narrow)
    steps = bias_first.shape[1]
    dma = pltpu.SemaphoreType.DMA
    fine_scratch = pltpu.VMEM((2, HF, WP, 128), F32)
    coarse_scratch = pltpu.VMEM((2, HC, WP, 128), F32)
    line = quad_cols * QP

    first, top, bottom = pl.pallas_call(
        first_kernel,
        out_shape=[
            jax.ShapeDtypeStruct((tokens, channels), BF16),
            jax.ShapeDtypeStruct((line, channels), BF16),
            jax.ShapeDtypeStruct((line, channels), BF16),
        ],
        in_specs=[WHOLE] * 7 + [APART] * 5,
        out_specs=[WHOLE] * 3,
        scratch_shapes=[pltpu.VMEM((tokens, channels), BF16), fine_scratch]
        + weight_scratch(fine_weights) + [dma((4,)), dma((2 * steps,))],
        compiler_params=pltpu.CompilerParams(vmem_limit_bytes=20 << 20),
        name="fine_plain",
    )(
        fields.reshape(-1, channels), land_sea, land_embed[None], order, of_row, of_col,
        fine_gains, bias_first, *fine_weights,
    )

    parts, coarse, top, bottom = pl.pallas_call(
        middle_kernel,
        out_shape=[
            jax.ShapeDtypeStruct((tokens, channels), BF16),
            jax.ShapeDtypeStruct((tokens // 4, wide), BF16),
            jax.ShapeDtypeStruct((line // 2, wide), BF16),
            jax.ShapeDtypeStruct((line // 2, wide), BF16),
        ],
        in_specs=[WHOLE] * 9 + [APART] * 10,
        out_specs=[WHOLE] * 4,
        scratch_shapes=shifted_scratch(quad_rows, quad_cols, channels)
        + [fine_scratch, coarse_scratch] + weight_scratch(fine_weights)
        + [pltpu.VMEM(merge_weight.shape, BF16)]
        + weight_scratch(coarse_weights) + [dma((9,)), dma((4 * steps,))],
        compiler_params=pltpu.CompilerParams(vmem_limit_bytes=60 << 20),
        name="fine_shifted_coarse_plain",
    )(
        *halo(first.reshape(quad_rows, quad_cols, QP, channels), top, bottom),
        fine_gains, merge_gain, coarse_gains,
        merge_table(rows, cols), bias_middle, *fine_weights, merge_weight, *coarse_weights,
    )

    out = pl.pallas_call(
        last_kernel,
        out_shape=jax.ShapeDtypeStruct((LEVELS * rows * cols, channels), BF16),
        in_specs=[WHOLE] * 9 + [APART] * 6,
        out_specs=WHOLE,
        scratch_shapes=shifted_scratch(quad_rows // 2, quad_cols // 2, wide)
        + [coarse_scratch] + weight_scratch(coarse_weights)
        + [pltpu.VMEM(expand_weight.shape, BF16)]
        + [dma((5,)), dma((2 * steps,))],
        compiler_params=pltpu.CompilerParams(vmem_limit_bytes=28 << 20),
        name="coarse_shifted_expand",
    )(
        *halo(coarse.reshape(quad_rows // 2, quad_cols // 2, QP, wide), top, bottom),
        coarse_gains, parts, expand_gain[None], expand_table(rows, cols),
        bias_last, *coarse_weights, expand_weight,
    )
    return out.reshape(fields.shape)


def solution(mesh):
    grid = P(None, "lat", LON, None)
    return jax.shard_map(
        on_device,
        mesh=mesh,
        in_specs=(grid, P("lat", LON)) + (P(),) * 18,
        out_specs=grid,
        check_vma=False,
    )
```

```python
import functools

import jax
import jax.numpy as jnp
import numpy as np
from jax import lax
from jax.experimental import pallas as pl
from jax.experimental.pallas import tpu as pltpu
from jax.sharding import PartitionSpec as P

HF = 6
HC = 12
HEAD = 32
WIN_LAT = 6
WIN_LON = 12
WIN_TOK = 144
HALF_LAT = WIN_LAT // 2
HALF_LON = WIN_LON // 2
LEVELS = 2
QUAD = LEVELS * HALF_LAT * HALF_LON
QP = 40
WP = 4 * QP
LO_COUNT = 13
LOG2E = 1.4426950408889634
MASKED = -1e30
LON = ("sec", "head")
F32 = jnp.float32
BF16 = jnp.bfloat16


def quad_sources(row_count, col_count):
    slots = []
    for a in range(row_count // HALF_LAT):
        for b in range(col_count // HALF_LON):
            for s in range(QP):
                if s >= QUAD:
                    slots.append(None)
                    continue
                level, rest = divmod(s, HALF_LAT * HALF_LON)
                r, c = divmod(rest, HALF_LON)
                slots.append((level, a * HALF_LAT + r, b * HALF_LON + c))
    return slots


def one_hot(sources, width):
    table = np.zeros((len(sources), width), np.float32)
    for slot, source in enumerate(sources):
        if source is not None:
            table[slot, source] = 1.0
    return jnp.asarray(table.astype(jnp.bfloat16))


def target_row(targets):
    return jnp.asarray(np.array([-1 if t is None else t for t in targets], np.int32)[None])


def fine_tables(rows, cols):
    slots = quad_sources(rows, cols)
    place = {s: n for n, s in enumerate(slots) if s is not None}
    order = target_row(
        [place[(level, r, c)] for level in range(LEVELS) for r in range(rows) for c in range(cols)]
    )
    of_row = one_hot([None if s is None else s[1] for s in slots], rows)
    of_col = one_hot([None if s is None else s[2] for s in slots], cols)
    return order, of_row, of_col


def merge_table(rows, cols):
    coarse = quad_sources(rows // 2, cols // 2)
    place = {s: n for n, s in enumerate(coarse) if s is not None}
    return target_row(
        [
            None
            if s is None
            else ((s[1] % 2) * 2 + s[2] % 2) * len(coarse) + place[(s[0], s[1] // 2, s[2] // 2)]
            for s in quad_sources(rows, cols)
        ]
    )


def expand_table(rows, cols):
    return target_row(
        [
            None
            if s is None
            else (s[0] * rows + 2 * s[1] + p) * cols + 2 * s[2] + q
            for p in range(2)
            for q in range(2)
            for s in quad_sources(rows // 2, cols // 2)
        ]
    )


def sent_to(target_ref, count):
    width = target_ref.shape[1]
    slot = lax.broadcasted_iota(jnp.int32, (count, width), 0)
    return jnp.where(slot == target_ref[...], 1.0, 0.0).astype(BF16)


def dot(a, b):
    return jnp.dot(a, b, preferred_element_type=F32)


def dot_t(a, b):
    return lax.dot_general(a, b, (((1,), (1,)), ((), ())), preferred_element_type=F32)


def norm(x, gain):
    mean = jnp.mean(x, axis=-1, keepdims=True)
    centered = x - mean
    variance = jnp.mean(centered * centered, axis=-1, keepdims=True)
    return centered * lax.rsqrt(variance + 1e-05) * gain


def attend(q, k, v, bias_ref, firsts, key_mask):
    n = q.shape[0]
    channels = q.shape[1]
    scale = HEAD**-0.5 * LOG2E
    outs = []
    for tile in range(0, channels, 128):
        width = min(128, channels - tile)
        count = width // HEAD
        qt = q[:, tile : tile + width]
        lane = lax.broadcasted_iota(jnp.int32, (n, width), 1) // HEAD
        masks = [lane == h for h in range(count)]
        stack = jnp.concatenate([jnp.where(m, qt, jnp.zeros_like(qt)) for m in masks], axis=0)
        scores = dot_t(stack, k[:, tile : tile + width])
        probs = []
        for h in range(count):
            head = tile // HEAD + h
            bias = jnp.concatenate(
                [
                    jnp.concatenate(
                        [bias_ref[half, head, f : f + n // len(firsts), :width] for f in firsts],
                        axis=0,
                    )
                    for half, width in ((0, 128), (1, WP - 128))
                ],
                axis=1,
            )
            s = scores[h * n : (h + 1) * n] * scale + bias
            if key_mask is not None:
                s = s + key_mask
            s = s - jnp.max(s, axis=-1, keepdims=True)
            probs.append(jnp.exp2(s).astype(BF16))
        probs = jnp.concatenate(probs, axis=0)
        vt = v[:, tile : tile + width]
        mixed = dot(probs, jnp.concatenate([vt, jnp.ones((WP, width), BF16)], axis=1))
        top = mixed[:n, :width]
        total = mixed[:n, width:]
        for h in range(1, count):
            top = jnp.where(masks[h], mixed[h * n : (h + 1) * n, :width], top)
            total = jnp.where(masks[h], mixed[h * n : (h + 1) * n, width:], total)
        outs.append(top / total)
    return outs[0] if len(outs) == 1 else jnp.concatenate(outs, axis=1)


def gelu(x):
    return 0.5 * x * (1.0 + lax.erf(x * np.float32(0.5**0.5)))


def finish(x, context, gain, w_project, w_widen, w_narrow):
    middle = (x + dot(context, w_project)).astype(BF16).astype(F32)
    second = norm(middle, gain).astype(BF16)
    hidden = gelu(dot(second, w_widen)).astype(BF16)
    narrow = dot if w_narrow.shape[0] > w_narrow.shape[1] else dot_t
    return (middle + narrow(hidden, w_narrow)).astype(BF16)


def padded(heads):
    return -(-heads // 8) * 8


def halved(heads):
    return heads % 8 == 4


def row_groups(head_counts):
    groups = []
    at = 0
    for heads in head_counts:
        count = padded(heads) // 8
        for g in range(count):
            groups.append((at + g * 8, 2 if halved(heads) and g == count - 1 else 1))
        at += padded(heads)
    return groups


def bias_kernel(*refs, picks, fresh):
    if fresh:
        index_ref, spread_ref, *table_refs, out_ref, index, table, left = refs
    else:
        index, *table_refs, out_ref, table, left = refs
    rows = table.shape[0]
    bias_len = table_refs[0].shape[-1]
    groups = row_groups([t.shape[0] for t in table_refs])

    @pl.when(pl.program_id(0) == 0)
    def _():
        if fresh:
            spread = spread_ref[...]
            plain = index_ref[...]
            high = (plain >> 4).astype(F32).astype(BF16)
            low = (plain & 15).astype(F32).astype(BF16)

            def moved(part):
                return dot_t(dot(spread, part).astype(BF16), spread).astype(jnp.int32)

            spot = lax.broadcasted_iota(jnp.int32, (WP, WP), 1) % QP
            index[...] = jnp.where(spot < QUAD, moved(high) * 16 + moved(low), bias_len)
        table[...] = jnp.full(table.shape, MASKED, F32)
        at = 0
        for table_ref, block in zip(table_refs, picks):
            heads = table_ref.shape[0]
            for h in range(heads):
                line = table_ref[h, block : block + 1, :] * LOG2E
                table[at + h : at + h + 1, :bias_len] = line
                if halved(heads) and h >= heads - 4:
                    table[at + h + 4 : at + h + 5, : bias_len - 256] = line[:, 256:]
            at += padded(heads)
        values = table[...]
        big = values.astype(BF16)
        small = (values - big.astype(F32)).astype(BF16)
        for n, part in enumerate((big, small)):
            left[:, n * 256 : (n + 1) * 256] = jnp.concatenate(
                [
                    part[row : row + 8, i * 256 : (i + 1) * 256]
                    for row, stride in groups
                    for i in range(0, LO_COUNT, stride)
                ],
                axis=0,
            )

    ladder = lax.broadcasted_iota(jnp.int32, (256, 256), 0).astype(F32).astype(BF16)
    lane = lax.broadcasted_iota(jnp.int32, (8, 256), 1) // 32
    sublane = lax.broadcasted_iota(jnp.int32, (8, 256), 0)
    low_half = lax.broadcasted_iota(jnp.int32, (8, 256), 0) // 4
    span = out_ref.shape[1] // rows
    for group in range(span // 8):
        first = pl.multiple_of(pl.program_id(0) * span + group * 8, 8)
        count = min(8, QUAD - group * 8)
        entries = index[pl.ds(first, 8), :]
        rest = jnp.concatenate([entries[:, 128:]] * 8, axis=1)
        rest = jnp.sum(jnp.where(lane == sublane, rest, 0).astype(F32), axis=0, keepdims=True)
        pieces = [
            jnp.concatenate([entries[j : j + 1, :128], entries[j + 1 : j + 2, :128]], axis=1)
            for j in range(0, count, 2)
        ] + [rest.astype(jnp.int32)]
        for t, entry in enumerate(pieces):
            near = (entry & 255).astype(F32).astype(BF16)
            far = entry >> 8
            chosen = jnp.where(ladder == near, jnp.ones((), BF16), jnp.zeros((), BF16))
            found = dot(left[...], jnp.concatenate([chosen, chosen], axis=0))
            shifted_far = far - low_half
            unit = 0
            for row, stride in groups:
                part = found[unit : unit + 8]
                unit += 8
                for i in range(stride, LO_COUNT, stride):
                    here = (far if stride == 1 else shifted_far) == i
                    part = jnp.where(here, found[unit : unit + 8], part)
                    unit += 8
                if stride == 2:
                    part = jnp.where((far & 1) == 0, part, pltpu.roll(part, 4, 0))
                at = row * span + group * 8
                if t < len(pieces) - 1:
                    for j in range(2):
                        out_ref[0, pl.ds(at + 2 * t + j, 8, stride=span), :] = (
                            part[:, j * 128 : (j + 1) * 128]
                        )
                else:
                    for j in range(count):
                        moved_part = part[:, j // 4 * 128 : (j // 4 + 1) * 128]
                        if j % 4:
                            moved_part = pltpu.roll(moved_part, 128 - 32 * (j % 4), 1)
                        out_ref[1, pl.ds(at + j, 8, stride=span), :] = moved_part
        for row, _ in groups:
            for j in range(count, 8):
                for half in range(2):
                    out_ref[half, pl.ds(row * span + group * 8 + j, 8, stride=span), :] = (
                        jnp.zeros((8, 128), F32)
                    )


def bias_of(picks, order, vmem, span=QP):
    tables = [t.transpose(1, 0, 2) for t, _ in picks]
    rows = sum(padded(t.shape[0]) for t in tables)
    units = sum(-(-LO_COUNT // stride) for _, stride in row_groups([t.shape[0] for t in tables]))
    flops = 2 * WP * 256 * WP * units * 8 * 4
    steps = WP // span
    fresh = len(order) == 2
    out_shape = [jax.ShapeDtypeStruct((2, steps * rows * span, 128), F32)]
    out_specs = [pl.BlockSpec((2, rows * span, 128), lambda i: (0, i, 0))]
    if fresh:
        out_shape.append(jax.ShapeDtypeStruct((WP, WP), jnp.int32))
        out_specs.append(pl.BlockSpec((WP, WP), lambda i: (0, 0)))
    out = pl.pallas_call(
        functools.partial(bias_kernel, picks=tuple(b for _, b in picks), fresh=fresh),
        out_shape=out_shape,
        grid=(steps,),
        in_specs=[pl.BlockSpec(memory_space=pltpu.VMEM)] * (len(order) + len(tables)),
        out_specs=out_specs,
        scratch_shapes=[
            pltpu.VMEM((rows, LO_COUNT * 256), F32),
            pltpu.VMEM((units * 8, 512), BF16),
        ],
        compiler_params=pltpu.CompilerParams(vmem_limit_bytes=vmem << 20),
        cost_estimate=pl.CostEstimate(flops=2 * flops, bytes_accessed=1 << 20, transcendentals=0),
        name="bias_table",
    )(*order, *tables)
    return [out[0].reshape(2, steps, rows, span, 128)] + list(out[1:])


def bias_copies(source_ref, bias, first, sems, at):
    steps, span, heads = source_ref.shape[1], source_ref.shape[3], bias.shape[1]
    return [
        pltpu.make_async_copy(
            source_ref.at[half, step, pl.ds(first, heads)],
            bias.at[half, :, pl.ds(step * span, span)],
            sems.at[at + half * steps + step],
        )
        for half in range(2)
        for step in range(steps)
    ]


class Fetched:
    def __init__(self, copies):
        self.copies = copies
        for group in copies[1:2] + copies[:1] + copies[2:]:
            for copy in group:
                copy.start()

    def wait(self, *numbers):
        for n in numbers:
            for copy in self.copies[n]:
                copy.wait()


def first_kernel(
    fields_ref, land_ref, embed_ref, order_ref, of_row_ref, of_col_ref, gains_ref,
    bias_hbm, triple_hbm, project_hbm, widen_hbm, narrow_hbm,
    out_ref, top_ref, bottom_ref,
    context, bias, w_triple, w_project, w_widen, w_narrow, sems, bias_sems,
):
    channels = fields_ref.shape[1]
    fetched = Fetched(
        [bias_copies(bias_hbm, bias, 0, bias_sems, 0)]
        + block_copies(
            [(triple_hbm, w_triple), (project_hbm, w_project),
             (widen_hbm, w_widen), (narrow_hbm, w_narrow)], 0, sems, 0,
        )
    )
    land = land_ref[...].astype(F32).astype(BF16)
    on_row = dot(of_row_ref[...], land)
    on_land = jnp.sum(on_row * of_col_ref[...].astype(F32), axis=-1, keepdims=True)
    rows = out_ref.shape[0]
    start = dot(sent_to(order_ref, rows), fields_ref[...]) + on_land * embed_ref[...]
    x = start.astype(BF16).astype(F32)
    normed = norm(x, gains_ref[0, 0:1]).astype(BF16)
    fetched.wait(1)
    triple = dot(normed, w_triple[...]).astype(BF16)
    fetched.wait(0)
    inner = top_ref.shape[0]
    for a in range(rows // inner // 2):
        for b in range(inner // QP // 2):
            top = 2 * a * inner + 2 * b * QP
            below = top + inner
            window = jnp.concatenate(
                [triple[top : top + 2 * QP], triple[below : below + 2 * QP]], axis=0
            )
            mixed = attend(
                window[:, :channels],
                window[:, channels : 2 * channels],
                window[:, 2 * channels :],
                bias, [0], None,
            ).astype(BF16)
            context[top : top + 2 * QP] = mixed[: 2 * QP]
            context[below : below + 2 * QP] = mixed[2 * QP :]
    fetched.wait(2, 3, 4)
    done = finish(
        x, context[...], gains_ref[0, 1:2], w_project[...], w_widen[...], w_narrow[...]
    )
    out_ref[...] = done
    top_ref[...] = done[:inner]
    bottom_ref[...] = done[rows - inner :]


def shifted_block(
    own_ref, north_ref, south_ref, west_ref, east_ref, gains_ref, fetched,
    bias, w_triple, w_project, w_widen, w_narrow, query, key, value, context,
):
    channels = own_ref.shape[1]
    across = north_ref.shape[0] // QP
    down = own_ref.shape[0] // QP // across
    line = (across + 2) * QP
    inner = across * QP
    pieces = []
    for i in range(down + 2):
        if i == 0:
            middle = north_ref[...]
        elif i == down + 1:
            middle = south_ref[...]
        else:
            middle = own_ref[(i - 1) * inner : i * inner]
        pieces += [
            west_ref[i * QP : (i + 1) * QP].astype(F32),
            middle.astype(F32),
            east_ref[i * QP : (i + 1) * QP].astype(F32),
        ]
    normed = norm(jnp.concatenate(pieces, axis=0), gains_ref[1, 0:1]).astype(BF16)
    fetched.wait(1)
    query[...] = dot(normed[line : (down + 1) * line], w_triple[:, :channels])
    both = dot(normed, w_triple[:, channels:]).astype(BF16)
    key[...] = both[:, :channels]
    value[...] = both[:, channels:]
    lane = lax.broadcasted_iota(jnp.int32, (1, WP), 1)
    place = lax.axis_index("lat")
    on_top = jnp.where(place == 0, MASKED, 0.0).astype(F32)
    on_bottom = jnp.where(place == lax.axis_size("lat") - 1, MASKED, 0.0).astype(F32)
    fetched.wait(0)
    for wa in range(down // 2 + 1):
        mask = None
        if wa == 0:
            mask = jnp.where(lane < 2 * QP, on_top, 0.0)
        elif wa == down // 2:
            mask = jnp.where(lane < 2 * QP, 0.0, on_bottom)
        for wb in range(across // 2 + 1):
            at = [(2 * wa + r) * line + 2 * wb * QP for r in range(2)]
            k = jnp.concatenate([key[s : s + 2 * QP] for s in at], axis=0)
            v = jnp.concatenate([value[s : s + 2 * QP] for s in at], axis=0)
            rows = [r for r in range(2) if 0 < 2 * wa + r < down + 1]
            cols = [c for c in range(2) if 0 < 2 * wb + c < across + 1]
            size = len(cols) * QP
            qs = [
                query[
                    (2 * wa + r - 1) * line + (2 * wb + cols[0]) * QP :
                    (2 * wa + r - 1) * line + (2 * wb + cols[0]) * QP + size
                ]
                for r in rows
            ]
            out = attend(
                jnp.concatenate(qs, axis=0).astype(BF16), k, v, bias,
                [(2 * r + cols[0]) * QP for r in rows], mask,
            )
            for n, r in enumerate(rows):
                to = ((2 * wa + r - 1) * across + 2 * wb + cols[0] - 1) * QP
                context[to : to + size] = out[n * size : (n + 1) * size]
    fetched.wait(2, 3, 4)
    return finish(
        own_ref[...].astype(F32), context[...].astype(BF16), gains_ref[1, 1:2],
        w_project[...], w_widen[...], w_narrow[...],
    )


def block_copies(pairs, block, sems, at):
    return [
        [pltpu.make_async_copy(source.at[block], target, sems.at[at + n])]
        for n, (source, target) in enumerate(pairs)
    ]


def middle_kernel(
    own_ref, north_ref, south_ref, west_ref, east_ref, gains_ref, merge_gain_ref,
    coarse_gains_ref, merge_order_ref, bias_hbm, triple_hbm, project_hbm, widen_hbm, narrow_hbm,
    merge_weight_hbm, c_triple_hbm, c_project_hbm, c_widen_hbm, c_narrow_hbm,
    parts_ref, coarse_ref, top_ref, bottom_ref,
    query, key, value, context, bias, c_bias, w_triple, w_project, w_widen, w_narrow,
    merge_weight, c_triple, c_project, c_widen, c_narrow, sems, bias_sems,
):
    steps = bias_hbm.shape[1]
    heads = bias.shape[1]
    fetched = Fetched(
        [bias_copies(bias_hbm, bias, 0, bias_sems, 0)]
        + block_copies(
            [(triple_hbm, w_triple), (project_hbm, w_project),
             (widen_hbm, w_widen), (narrow_hbm, w_narrow)], 1, sems, 0,
        )
        + [
            [pltpu.make_async_copy(merge_weight_hbm, merge_weight, sems.at[4])],
            bias_copies(bias_hbm, c_bias, padded(heads), bias_sems, 2 * steps),
        ]
        + block_copies(
            [(c_triple_hbm, c_triple), (c_project_hbm, c_project),
             (c_widen_hbm, c_widen), (c_narrow_hbm, c_narrow)], 0, sems, 5,
        )
    )
    skip = shifted_block(
        own_ref, north_ref, south_ref, west_ref, east_ref, gains_ref, fetched,
        bias, w_triple, w_project, w_widen, w_narrow, query, key, value, context,
    )
    channels = own_ref.shape[1]
    grouped = dot(sent_to(merge_order_ref, skip.shape[0]), skip)
    parts_ref[...] = grouped.astype(BF16)
    parts = [grouped[i * WP : (i + 1) * WP] for i in range(4)]
    width = 4 * channels
    mean = sum(jnp.sum(p, axis=-1, keepdims=True) for p in parts) / width
    parts = [p - mean for p in parts]
    variance = sum(jnp.sum(p * p, axis=-1, keepdims=True) for p in parts) / width
    factor = lax.rsqrt(variance + 1e-05)
    merge_gain = merge_gain_ref[...].reshape(1, width)
    fetched.wait(5)
    coarse = jnp.zeros((WP, merge_weight.shape[1]), F32)
    for i, p in enumerate(parts):
        gain = merge_gain[:, i * channels : (i + 1) * channels]
        merged = (p * factor * gain).astype(BF16)
        coarse = coarse + dot(merged, merge_weight[i * channels : (i + 1) * channels])
    x = coarse.astype(BF16).astype(F32)
    wide = x.shape[1]
    normed = norm(x, coarse_gains_ref[0, 0:1]).astype(BF16)
    fetched.wait(6, 7)
    triple = dot(normed, c_triple[...]).astype(BF16)
    mixed = attend(
        triple[:, :wide], triple[:, wide : 2 * wide], triple[:, 2 * wide :], c_bias, [0], None
    ).astype(BF16)
    fetched.wait(8, 9, 10)
    done = finish(
        x, mixed, coarse_gains_ref[0, 1:2], c_project[...], c_widen[...], c_narrow[...]
    )
    coarse_ref[...] = done
    inner = top_ref.shape[0]
    top_ref[...] = done[:inner]
    bottom_ref[...] = done[WP - inner :]


def last_kernel(
    own_ref, north_ref, south_ref, west_ref, east_ref, gains_ref, parts_ref, expand_gain_ref,
    expand_order_ref, bias_hbm, triple_hbm, project_hbm, widen_hbm, narrow_hbm, expand_weight_hbm,
    out_ref,
    query, key, value, context, bias, w_triple, w_project, w_widen, w_narrow,
    expand_weight, sems, bias_sems,
):
    fetched = Fetched(
        [bias_copies(bias_hbm, bias, 0, bias_sems, 0)]
        + block_copies(
            [(triple_hbm, w_triple), (project_hbm, w_project),
             (widen_hbm, w_widen), (narrow_hbm, w_narrow)], 1, sems, 0,
        )
        + [[pltpu.make_async_copy(expand_weight_hbm, expand_weight, sems.at[4])]]
    )
    deep = shifted_block(
        own_ref, north_ref, south_ref, west_ref, east_ref, gains_ref, fetched,
        bias, w_triple, w_project, w_widen, w_narrow, query, key, value, context,
    )
    channels = parts_ref.shape[1]
    fetched.wait(5)
    widened = dot(deep, expand_weight[...])
    outs = []
    for i in range(4):
        shuffled = widened[:, i * channels : (i + 1) * channels]
        skip = parts_ref[i * WP : (i + 1) * WP].astype(F32)
        outs.append((skip + norm(shuffled, expand_gain_ref[...])).astype(BF16))
    moves = sent_to(expand_order_ref, out_ref.shape[0])
    out_ref[...] = dot(moves, jnp.concatenate(outs, axis=0)).astype(BF16)


WHOLE = pl.BlockSpec(memory_space=pltpu.VMEM)
APART = pl.BlockSpec(memory_space=pltpu.HBM)


def weight_scratch(weights):
    return [pltpu.VMEM(w.shape[1:], BF16) for w in weights]


def halo(own, top, bottom):
    rows, cols, _, channels = own.shape
    top = top.reshape(own.shape[1:])
    bottom = bottom.reshape(own.shape[1:])
    lat = lax.axis_size("lat")
    lon = lax.axis_size(LON)
    down = [(i, (i + 1) % lat) for i in range(lat)]
    up = [((i + 1) % lat, i) for i in range(lat)]
    east = [(i, (i + 1) % lon) for i in range(lon)]
    west = [((i + 1) % lon, i) for i in range(lon)]
    north = lax.ppermute(bottom, "lat", down)
    south = lax.ppermute(top, "lat", up)

    def side(c):
        return jnp.concatenate([north[c : c + 1], own[:, c], south[c : c + 1]], axis=0)

    from_west = lax.ppermute(side(cols - 1), LON, east)
    from_east = lax.ppermute(side(0), LON, west)
    return [v.reshape(-1, channels) for v in (own, north, south, from_west, from_east)]


def shifted_scratch(rows, cols, channels):
    line = (cols + 2) * QP
    return [
        pltpu.VMEM((rows * line, channels), F32),
        pltpu.VMEM(((rows + 2) * line, channels), BF16),
        pltpu.VMEM(((rows + 2) * line, channels), BF16),
        pltpu.VMEM((rows * cols * QP, channels), F32),
    ]


def on_device(
    fields, land_sea, land_embed, bias_index, fine_bias, fine_gains, fine_query_key_value,
    fine_project, fine_widen, fine_narrow, merge_gain, merge_weight, coarse_bias, coarse_gains,
    coarse_query_key_value, coarse_project, coarse_widen, coarse_narrow, expand_weight, expand_gain,
):
    _, rows, cols, channels = fields.shape
    quad_rows, quad_cols = rows // HALF_LAT, cols // HALF_LON
    tokens = quad_rows * quad_cols * QP
    wide = merge_weight.shape[1]
    spread = one_hot(
        [None if s is None else (s[0] * WIN_LAT + s[1]) * WIN_LON + s[2]
         for s in quad_sources(WIN_LAT, WIN_LON)],
        WIN_TOK,
    )
    order, of_row, of_col = fine_tables(rows, cols)
    bias_first, ordered = bias_of([(fine_bias, 0)], (bias_index, spread), 16)
    (bias_middle,) = bias_of([(fine_bias, 1), (coarse_bias, 0)], (ordered,), 16)
    (bias_last,) = bias_of([(coarse_bias, 1)], (ordered,), 16)
    fine_weights = (
        fine_query_key_value, fine_project, fine_widen, fine_narrow.transpose(0, 2, 1)
    )
    coarse_weights = (coarse_query_key_value, coarse_project, coarse_widen, coarse_narrow)
    steps = bias_first.shape[1]
    dma = pltpu.SemaphoreType.DMA
    fine_scratch = pltpu.VMEM((2, HF, WP, 128), F32)
    coarse_scratch = pltpu.VMEM((2, HC, WP, 128), F32)
    line = quad_cols * QP

    first, top, bottom = pl.pallas_call(
        first_kernel,
        out_shape=[
            jax.ShapeDtypeStruct((tokens, channels), BF16),
            jax.ShapeDtypeStruct((line, channels), BF16),
            jax.ShapeDtypeStruct((line, channels), BF16),
        ],
        in_specs=[WHOLE] * 7 + [APART] * 5,
        out_specs=[WHOLE] * 3,
        scratch_shapes=[pltpu.VMEM((tokens, channels), BF16), fine_scratch]
        + weight_scratch(fine_weights) + [dma((4,)), dma((2 * steps,))],
        compiler_params=pltpu.CompilerParams(vmem_limit_bytes=20 << 20),
        name="fine_plain",
    )(
        fields.reshape(-1, channels), land_sea, land_embed[None], order, of_row, of_col,
        fine_gains, bias_first, *fine_weights,
    )

    parts, coarse, top, bottom = pl.pallas_call(
        middle_kernel,
        out_shape=[
            jax.ShapeDtypeStruct((tokens, channels), BF16),
            jax.ShapeDtypeStruct((tokens // 4, wide), BF16),
            jax.ShapeDtypeStruct((line // 2, wide), BF16),
            jax.ShapeDtypeStruct((line // 2, wide), BF16),
        ],
        in_specs=[WHOLE] * 9 + [APART] * 10,
        out_specs=[WHOLE] * 4,
        scratch_shapes=shifted_scratch(quad_rows, quad_cols, channels)
        + [fine_scratch, coarse_scratch] + weight_scratch(fine_weights)
        + [pltpu.VMEM(merge_weight.shape, BF16)]
        + weight_scratch(coarse_weights) + [dma((9,)), dma((4 * steps,))],
        compiler_params=pltpu.CompilerParams(vmem_limit_bytes=60 << 20),
        name="fine_shifted_coarse_plain",
    )(
        *halo(first.reshape(quad_rows, quad_cols, QP, channels), top, bottom),
        fine_gains, merge_gain, coarse_gains,
        merge_table(rows, cols), bias_middle, *fine_weights, merge_weight, *coarse_weights,
    )

    out = pl.pallas_call(
        last_kernel,
        out_shape=jax.ShapeDtypeStruct((LEVELS * rows * cols, channels), BF16),
        in_specs=[WHOLE] * 9 + [APART] * 6,
        out_specs=WHOLE,
        scratch_shapes=shifted_scratch(quad_rows // 2, quad_cols // 2, wide)
        + [coarse_scratch] + weight_scratch(coarse_weights)
        + [pltpu.VMEM(expand_weight.shape, BF16)]
        + [dma((5,)), dma((2 * steps,))],
        compiler_params=pltpu.CompilerParams(vmem_limit_bytes=28 << 20),
        name="coarse_shifted_expand",
    )(
        *halo(coarse.reshape(quad_rows // 2, quad_cols // 2, QP, wide), top, bottom),
        coarse_gains, parts, expand_gain[None], expand_table(rows, cols),
        bias_last, *coarse_weights, expand_weight,
    )
    return out.reshape(fields.shape)


def solution(mesh):
    grid = P(None, "lat", LON, None)
    return jax.shard_map(
        on_device,
        mesh=mesh,
        in_specs=(grid, P("lat", LON)) + (P(),) * 18,
        out_specs=grid,
        check_vma=False,
    )
```

```python
import functools

import jax
import jax.numpy as jnp
import numpy as np
from jax import lax
from jax.experimental import pallas as pl
from jax.experimental.pallas import tpu as pltpu
from jax.sharding import PartitionSpec as P

HF = 6
HC = 12
HEAD = 32
WIN_LAT = 6
WIN_LON = 12
WIN_TOK = 144
HALF_LAT = WIN_LAT // 2
HALF_LON = WIN_LON // 2
LEVELS = 2
QUAD = LEVELS * HALF_LAT * HALF_LON
QP = 40
WP = 4 * QP
LO_COUNT = 13
LOG2E = 1.4426950408889634
MASKED = -1e30
LON = ("sec", "head")
F32 = jnp.float32
BF16 = jnp.bfloat16


def quad_sources(row_count, col_count):
    slots = []
    for a in range(row_count // HALF_LAT):
        for b in range(col_count // HALF_LON):
            for s in range(QP):
                if s >= QUAD:
                    slots.append(None)
                    continue
                level, rest = divmod(s, HALF_LAT * HALF_LON)
                r, c = divmod(rest, HALF_LON)
                slots.append((level, a * HALF_LAT + r, b * HALF_LON + c))
    return slots


def one_hot(sources, width):
    table = np.zeros((len(sources), width), np.float32)
    for slot, source in enumerate(sources):
        if source is not None:
            table[slot, source] = 1.0
    return jnp.asarray(table.astype(jnp.bfloat16))


def target_row(targets):
    return jnp.asarray(np.array([-1 if t is None else t for t in targets], np.int32)[None])


def fine_tables(rows, cols):
    slots = quad_sources(rows, cols)
    place = {s: n for n, s in enumerate(slots) if s is not None}
    order = target_row(
        [place[(level, r, c)] for level in range(LEVELS) for r in range(rows) for c in range(cols)]
    )
    of_row = one_hot([None if s is None else s[1] for s in slots], rows)
    of_col = one_hot([None if s is None else s[2] for s in slots], cols)
    return order, of_row, of_col


def merge_table(rows, cols):
    coarse = quad_sources(rows // 2, cols // 2)
    place = {s: n for n, s in enumerate(coarse) if s is not None}
    return target_row(
        [
            None
            if s is None
            else ((s[1] % 2) * 2 + s[2] % 2) * len(coarse) + place[(s[0], s[1] // 2, s[2] // 2)]
            for s in quad_sources(rows, cols)
        ]
    )


def expand_table(rows, cols):
    return target_row(
        [
            None
            if s is None
            else (s[0] * rows + 2 * s[1] + p) * cols + 2 * s[2] + q
            for p in range(2)
            for q in range(2)
            for s in quad_sources(rows // 2, cols // 2)
        ]
    )


def sent_to(target_ref, count):
    width = target_ref.shape[1]
    slot = lax.broadcasted_iota(jnp.int32, (count, width), 0)
    return jnp.where(slot == target_ref[...], 1.0, 0.0).astype(BF16)


def dot(a, b):
    return jnp.dot(a, b, preferred_element_type=F32)


def dot_t(a, b):
    return lax.dot_general(a, b, (((1,), (1,)), ((), ())), preferred_element_type=F32)


def norm(x, gain):
    mean = jnp.mean(x, axis=-1, keepdims=True)
    centered = x - mean
    variance = jnp.mean(centered * centered, axis=-1, keepdims=True)
    return centered * lax.rsqrt(variance + 1e-05) * gain


def attend(q, k, v, bias_ref, firsts, key_mask):
    n = q.shape[0]
    channels = q.shape[1]
    scale = HEAD**-0.5 * LOG2E
    outs = []
    for tile in range(0, channels, 128):
        width = min(128, channels - tile)
        count = width // HEAD
        qt = q[:, tile : tile + width]
        lane = lax.broadcasted_iota(jnp.int32, (n, width), 1) // HEAD
        masks = [lane == h for h in range(count)]
        stack = jnp.concatenate([jnp.where(m, qt, jnp.zeros_like(qt)) for m in masks], axis=0)
        scores = dot_t(stack, k[:, tile : tile + width])
        probs = []
        for h in range(count):
            head = tile // HEAD + h
            bias = jnp.concatenate(
                [
                    jnp.concatenate(
                        [bias_ref[half, head, f : f + n // len(firsts), :width] for f in firsts],
                        axis=0,
                    )
                    for half, width in ((0, 128), (1, WP - 128))
                ],
                axis=1,
            )
            s = scores[h * n : (h + 1) * n] * scale + bias
            if key_mask is not None:
                s = s + key_mask
            s = s - jnp.max(s, axis=-1, keepdims=True)
            probs.append(jnp.exp2(s).astype(BF16))
        probs = jnp.concatenate(probs, axis=0)
        vt = v[:, tile : tile + width]
        mixed = dot(probs, jnp.concatenate([vt, jnp.ones((WP, width), BF16)], axis=1))
        top = mixed[:n, :width]
        total = mixed[:n, width:]
        for h in range(1, count):
            top = jnp.where(masks[h], mixed[h * n : (h + 1) * n, :width], top)
            total = jnp.where(masks[h], mixed[h * n : (h + 1) * n, width:], total)
        outs.append(top / total)
    return outs[0] if len(outs) == 1 else jnp.concatenate(outs, axis=1)


def gelu(x):
    return 0.5 * x * (1.0 + lax.erf(x * np.float32(0.5**0.5)))


def finish(x, context, gain, w_project, w_widen, w_narrow):
    middle = (x + dot(context, w_project)).astype(BF16).astype(F32)
    second = norm(middle, gain).astype(BF16)
    hidden = gelu(dot(second, w_widen)).astype(BF16)
    narrow = dot if w_narrow.shape[0] > w_narrow.shape[1] else dot_t
    return (middle + narrow(hidden, w_narrow)).astype(BF16)


def padded(heads):
    return -(-heads // 8) * 8


def window_order():
    token = lax.broadcasted_iota(jnp.int32, (WP, WIN_TOK), 1)
    level = jnp.where(token >= WIN_LAT * WIN_LON, 1, 0)
    token = token - level * (WIN_LAT * WIN_LON)
    row = sum(jnp.where(token >= WIN_LON * r, 1, 0) for r in range(1, WIN_LAT))
    col = token - row * WIN_LON
    down = jnp.where(row >= HALF_LAT, 1, 0)
    across = jnp.where(col >= HALF_LON, 1, 0)
    slot = (
        (2 * down + across) * QP
        + level * (HALF_LAT * HALF_LON)
        + (row - down * HALF_LAT) * HALF_LON
        + (col - across * HALF_LON)
    )
    place = lax.broadcasted_iota(jnp.int32, (WP, WIN_TOK), 0)
    return jnp.where(slot == place, 1.0, 0.0).astype(BF16)


def halved(heads):
    return heads % 8 == 4


def row_groups(head_counts):
    groups = []
    at = 0
    for heads in head_counts:
        count = padded(heads) // 8
        for g in range(count):
            groups.append((at + g * 8, 2 if halved(heads) and g == count - 1 else 1))
        at += padded(heads)
    return groups


def bias_kernel(*refs, picks, fresh):
    if fresh:
        index_ref, *table_refs, out_ref, index, table, left = refs
    else:
        index, *table_refs, out_ref, table, left = refs
    rows = table.shape[0]
    bias_len = table_refs[0].shape[-1]
    groups = row_groups([t.shape[0] for t in table_refs])

    @pl.when(pl.program_id(0) == 0)
    def _():
        if fresh:
            spread = window_order()
            plain = index_ref[...]
            high = (plain >> 4).astype(F32).astype(BF16)
            low = (plain & 15).astype(F32).astype(BF16)

            def moved(part):
                return dot_t(dot(spread, part).astype(BF16), spread).astype(jnp.int32)

            spot = lax.broadcasted_iota(jnp.int32, (WP, WP), 1) % QP
            index[...] = jnp.where(spot < QUAD, moved(high) * 16 + moved(low), bias_len)
        table[...] = jnp.full(table.shape, MASKED, F32)
        at = 0
        for table_ref, block in zip(table_refs, picks):
            heads = table_ref.shape[0]
            for h in range(heads):
                line = table_ref[h, block : block + 1, :] * LOG2E
                table[at + h : at + h + 1, :bias_len] = line
                if halved(heads) and h >= heads - 4:
                    table[at + h + 4 : at + h + 5, : bias_len - 256] = line[:, 256:]
            at += padded(heads)
        values = table[...]
        big = values.astype(BF16)
        small = (values - big.astype(F32)).astype(BF16)
        for n, part in enumerate((big, small)):
            left[:, n * 256 : (n + 1) * 256] = jnp.concatenate(
                [
                    part[row : row + 8, i * 256 : (i + 1) * 256]
                    for row, stride in groups
                    for i in range(0, LO_COUNT, stride)
                ],
                axis=0,
            )

    ladder = lax.broadcasted_iota(jnp.int32, (256, 256), 0).astype(F32).astype(BF16)
    lane = lax.broadcasted_iota(jnp.int32, (8, 256), 1) // 32
    sublane = lax.broadcasted_iota(jnp.int32, (8, 256), 0)
    low_half = lax.broadcasted_iota(jnp.int32, (8, 256), 0) // 4
    span = out_ref.shape[1] // rows
    for group in range(span // 8):
        first = pl.multiple_of(pl.program_id(0) * span + group * 8, 8)
        count = min(8, QUAD - group * 8)
        entries = index[pl.ds(first, 8), :]
        rest = jnp.concatenate([entries[:, 128:]] * 8, axis=1)
        rest = jnp.sum(jnp.where(lane == sublane, rest, 0).astype(F32), axis=0, keepdims=True)
        pieces = [
            jnp.concatenate([entries[j : j + 1, :128], entries[j + 1 : j + 2, :128]], axis=1)
            for j in range(0, count, 2)
        ] + [rest.astype(jnp.int32)]
        for t, entry in enumerate(pieces):
            near = (entry & 255).astype(F32).astype(BF16)
            far = entry >> 8
            chosen = jnp.where(ladder == near, jnp.ones((), BF16), jnp.zeros((), BF16))
            found = dot(left[...], jnp.concatenate([chosen, chosen], axis=0))
            shifted_far = far - low_half
            unit = 0
            for row, stride in groups:
                part = found[unit : unit + 8]
                unit += 8
                for i in range(stride, LO_COUNT, stride):
                    here = (far if stride == 1 else shifted_far) == i
                    part = jnp.where(here, found[unit : unit + 8], part)
                    unit += 8
                if stride == 2:
                    part = jnp.where((far & 1) == 0, part, pltpu.roll(part, 4, 0))
                at = row * span + group * 8
                if t < len(pieces) - 1:
                    for j in range(2):
                        out_ref[0, pl.ds(at + 2 * t + j, 8, stride=span), :] = (
                            part[:, j * 128 : (j + 1) * 128]
                        )
                else:
                    for j in range(count):
                        moved_part = part[:, j // 4 * 128 : (j // 4 + 1) * 128]
                        if j % 4:
                            moved_part = pltpu.roll(moved_part, 128 - 32 * (j % 4), 1)
                        out_ref[1, pl.ds(at + j, 8, stride=span), :] = moved_part
        for row, _ in groups:
            for j in range(count, 8):
                for half in range(2):
                    out_ref[half, pl.ds(row * span + group * 8 + j, 8, stride=span), :] = (
                        jnp.zeros((8, 128), F32)
                    )


def bias_of(picks, order, vmem, fresh=False, span=QP):
    tables = [t.transpose(1, 0, 2) for t, _ in picks]
    if fresh:
        order, tables = in_hbm(order), [in_hbm(t) for t in tables]
    rows = sum(padded(t.shape[0]) for t in tables)
    units = sum(-(-LO_COUNT // stride) for _, stride in row_groups([t.shape[0] for t in tables]))
    flops = 2 * WP * 256 * WP * units * 8 * 4
    steps = WP // span
    out_shape = [jax.ShapeDtypeStruct((2, steps * rows * span, 128), F32)]
    out_specs = [pl.BlockSpec((2, rows * span, 128), lambda i: (0, i, 0))]
    if fresh:
        out_shape.append(jax.ShapeDtypeStruct((WP, WP), jnp.int32))
        out_specs.append(pl.BlockSpec((WP, WP), lambda i: (0, 0)))
    out = pl.pallas_call(
        functools.partial(bias_kernel, picks=tuple(b for _, b in picks), fresh=fresh),
        out_shape=out_shape,
        grid=(steps,),
        in_specs=[pl.BlockSpec(memory_space=pltpu.VMEM)] * (1 + len(tables)),
        out_specs=out_specs,
        scratch_shapes=[
            pltpu.VMEM((rows, LO_COUNT * 256), F32),
            pltpu.VMEM((units * 8, 512), BF16),
        ],
        compiler_params=pltpu.CompilerParams(vmem_limit_bytes=vmem << 20),
        cost_estimate=pl.CostEstimate(flops=2 * flops, bytes_accessed=1 << 20, transcendentals=0),
        name="bias_table",
    )(order, *tables)
    return [out[0].reshape(2, steps, rows, span, 128)] + list(out[1:])


def bias_copies(source_ref, bias, first, sems, at):
    steps, span, heads = source_ref.shape[1], source_ref.shape[3], bias.shape[1]
    return [
        pltpu.make_async_copy(
            source_ref.at[half, step, pl.ds(first, heads)],
            bias.at[half, :, pl.ds(step * span, span)],
            sems.at[at + half * steps + step],
        )
        for half in range(2)
        for step in range(steps)
    ]


class Fetched:
    def __init__(self, copies):
        self.copies = copies
        for group in copies[1:2] + copies[:1] + copies[2:]:
            for copy in group:
                copy.start()

    def wait(self, *numbers):
        for n in numbers:
            for copy in self.copies[n]:
                copy.wait()


def first_kernel(
    fields_ref, land_ref, embed_ref, order_ref, of_row_ref, of_col_ref, gains_ref,
    bias_hbm, triple_hbm, project_hbm, widen_hbm, narrow_hbm,
    out_ref, top_ref, bottom_ref,
    context, bias, w_triple, w_project, w_widen, w_narrow, sems, bias_sems,
):
    channels = fields_ref.shape[1]
    fetched = Fetched(
        [bias_copies(bias_hbm, bias, 0, bias_sems, 0)]
        + block_copies(
            [(triple_hbm, w_triple), (project_hbm, w_project),
             (widen_hbm, w_widen), (narrow_hbm, w_narrow)], 0, sems, 0,
        )
    )
    land = land_ref[...].astype(F32).astype(BF16)
    on_row = dot(of_row_ref[...], land)
    on_land = jnp.sum(on_row * of_col_ref[...].astype(F32), axis=-1, keepdims=True)
    rows = out_ref.shape[0]
    start = dot(sent_to(order_ref, rows), fields_ref[...]) + on_land * embed_ref[...]
    x = start.astype(BF16).astype(F32)
    normed = norm(x, gains_ref[0, 0:1]).astype(BF16)
    fetched.wait(1)
    triple = dot(normed, w_triple[...]).astype(BF16)
    fetched.wait(0)
    inner = top_ref.shape[0]
    for a in range(rows // inner // 2):
        for b in range(inner // QP // 2):
            top = 2 * a * inner + 2 * b * QP
            below = top + inner
            window = jnp.concatenate(
                [triple[top : top + 2 * QP], triple[below : below + 2 * QP]], axis=0
            )
            mixed = attend(
                window[:, :channels],
                window[:, channels : 2 * channels],
                window[:, 2 * channels :],
                bias, [0], None,
            ).astype(BF16)
            context[top : top + 2 * QP] = mixed[: 2 * QP]
            context[below : below + 2 * QP] = mixed[2 * QP :]
    fetched.wait(2, 3, 4)
    done = finish(
        x, context[...], gains_ref[0, 1:2], w_project[...], w_widen[...], w_narrow[...]
    )
    out_ref[...] = done
    top_ref[...] = done[:inner]
    bottom_ref[...] = done[rows - inner :]


def shifted_block(
    own_ref, north_ref, south_ref, west_ref, east_ref, gains_ref, fetched,
    bias, w_triple, w_project, w_widen, w_narrow, query, key, value, context,
):
    channels = own_ref.shape[1]
    across = north_ref.shape[0] // QP
    down = own_ref.shape[0] // QP // across
    line = (across + 2) * QP
    inner = across * QP
    pieces = []
    for i in range(down + 2):
        if i == 0:
            middle = north_ref[...]
        elif i == down + 1:
            middle = south_ref[...]
        else:
            middle = own_ref[(i - 1) * inner : i * inner]
        pieces += [
            west_ref[i * QP : (i + 1) * QP].astype(F32),
            middle.astype(F32),
            east_ref[i * QP : (i + 1) * QP].astype(F32),
        ]
    normed = norm(jnp.concatenate(pieces, axis=0), gains_ref[1, 0:1]).astype(BF16)
    fetched.wait(1)
    query[...] = dot(normed[line : (down + 1) * line], w_triple[:, :channels])
    both = dot(normed, w_triple[:, channels:]).astype(BF16)
    key[...] = both[:, :channels]
    value[...] = both[:, channels:]
    lane = lax.broadcasted_iota(jnp.int32, (1, WP), 1)
    place = lax.axis_index("lat")
    on_top = jnp.where(place == 0, MASKED, 0.0).astype(F32)
    on_bottom = jnp.where(place == lax.axis_size("lat") - 1, MASKED, 0.0).astype(F32)
    fetched.wait(0)
    for wa in range(down // 2 + 1):
        mask = None
        if wa == 0:
            mask = jnp.where(lane < 2 * QP, on_top, 0.0)
        elif wa == down // 2:
            mask = jnp.where(lane < 2 * QP, 0.0, on_bottom)
        for wb in range(across // 2 + 1):
            at = [(2 * wa + r) * line + 2 * wb * QP for r in range(2)]
            k = jnp.concatenate([key[s : s + 2 * QP] for s in at], axis=0)
            v = jnp.concatenate([value[s : s + 2 * QP] for s in at], axis=0)
            rows = [r for r in range(2) if 0 < 2 * wa + r < down + 1]
            cols = [c for c in range(2) if 0 < 2 * wb + c < across + 1]
            size = len(cols) * QP
            qs = [
                query[
                    (2 * wa + r - 1) * line + (2 * wb + cols[0]) * QP :
                    (2 * wa + r - 1) * line + (2 * wb + cols[0]) * QP + size
                ]
                for r in rows
            ]
            out = attend(
                jnp.concatenate(qs, axis=0).astype(BF16), k, v, bias,
                [(2 * r + cols[0]) * QP for r in rows], mask,
            )
            for n, r in enumerate(rows):
                to = ((2 * wa + r - 1) * across + 2 * wb + cols[0] - 1) * QP
                context[to : to + size] = out[n * size : (n + 1) * size]
    fetched.wait(2, 3, 4)
    return finish(
        own_ref[...].astype(F32), context[...].astype(BF16), gains_ref[1, 1:2],
        w_project[...], w_widen[...], w_narrow[...],
    )


def block_copies(pairs, block, sems, at):
    return [
        [pltpu.make_async_copy(source.at[block], target, sems.at[at + n])]
        for n, (source, target) in enumerate(pairs)
    ]


def middle_kernel(
    own_ref, north_ref, south_ref, west_ref, east_ref, gains_ref, merge_gain_ref,
    coarse_gains_ref, merge_order_ref, bias_hbm, c_bias_hbm, triple_hbm, project_hbm, widen_hbm, narrow_hbm,
    merge_weight_hbm, c_triple_hbm, c_project_hbm, c_widen_hbm, c_narrow_hbm,
    parts_ref, coarse_ref, top_ref, bottom_ref,
    query, key, value, context, bias, c_bias, w_triple, w_project, w_widen, w_narrow,
    merge_weight, c_triple, c_project, c_widen, c_narrow, sems, bias_sems,
):
    steps = bias_hbm.shape[1]
    fetched = Fetched(
        [bias_copies(bias_hbm, bias, 0, bias_sems, 0)]
        + block_copies(
            [(triple_hbm, w_triple), (project_hbm, w_project),
             (widen_hbm, w_widen), (narrow_hbm, w_narrow)], 1, sems, 0,
        )
        + [
            [pltpu.make_async_copy(merge_weight_hbm, merge_weight, sems.at[4])],
            bias_copies(c_bias_hbm, c_bias, 0, bias_sems, 2 * steps),
        ]
        + block_copies(
            [(c_triple_hbm, c_triple), (c_project_hbm, c_project),
             (c_widen_hbm, c_widen), (c_narrow_hbm, c_narrow)], 0, sems, 5,
        )
    )
    skip = shifted_block(
        own_ref, north_ref, south_ref, west_ref, east_ref, gains_ref, fetched,
        bias, w_triple, w_project, w_widen, w_narrow, query, key, value, context,
    )
    channels = own_ref.shape[1]
    grouped = dot(sent_to(merge_order_ref, skip.shape[0]), skip)
    parts_ref[...] = grouped.astype(BF16)
    parts = [grouped[i * WP : (i + 1) * WP] for i in range(4)]
    width = 4 * channels
    mean = sum(jnp.sum(p, axis=-1, keepdims=True) for p in parts) / width
    parts = [p - mean for p in parts]
    variance = sum(jnp.sum(p * p, axis=-1, keepdims=True) for p in parts) / width
    factor = lax.rsqrt(variance + 1e-05)
    merge_gain = merge_gain_ref[...].reshape(1, width)
    fetched.wait(5)
    coarse = jnp.zeros((WP, merge_weight.shape[1]), F32)
    for i, p in enumerate(parts):
        gain = merge_gain[:, i * channels : (i + 1) * channels]
        merged = (p * factor * gain).astype(BF16)
        coarse = coarse + dot(merged, merge_weight[i * channels : (i + 1) * channels])
    x = coarse.astype(BF16).astype(F32)
    wide = x.shape[1]
    normed = norm(x, coarse_gains_ref[0, 0:1]).astype(BF16)
    fetched.wait(6, 7)
    triple = dot(normed, c_triple[...]).astype(BF16)
    mixed = attend(
        triple[:, :wide], triple[:, wide : 2 * wide], triple[:, 2 * wide :], c_bias, [0], None
    ).astype(BF16)
    fetched.wait(8, 9, 10)
    done = finish(
        x, mixed, coarse_gains_ref[0, 1:2], c_project[...], c_widen[...], c_narrow[...]
    )
    coarse_ref[...] = done
    inner = top_ref.shape[0]
    top_ref[...] = done[:inner]
    bottom_ref[...] = done[WP - inner :]


def last_kernel(
    own_ref, north_ref, south_ref, west_ref, east_ref, gains_ref, parts_ref, expand_gain_ref,
    expand_order_ref, bias_hbm, triple_hbm, project_hbm, widen_hbm, narrow_hbm, expand_weight_hbm,
    out_ref,
    query, key, value, context, bias, w_triple, w_project, w_widen, w_narrow,
    expand_weight, sems, bias_sems,
):
    fetched = Fetched(
        [bias_copies(bias_hbm, bias, 0, bias_sems, 0)]
        + block_copies(
            [(triple_hbm, w_triple), (project_hbm, w_project),
             (widen_hbm, w_widen), (narrow_hbm, w_narrow)], 1, sems, 0,
        )
        + [[pltpu.make_async_copy(expand_weight_hbm, expand_weight, sems.at[4])]]
    )
    deep = shifted_block(
        own_ref, north_ref, south_ref, west_ref, east_ref, gains_ref, fetched,
        bias, w_triple, w_project, w_widen, w_narrow, query, key, value, context,
    )
    channels = parts_ref.shape[1]
    fetched.wait(5)
    widened = dot(deep, expand_weight[...])
    outs = []
    for i in range(4):
        shuffled = widened[:, i * channels : (i + 1) * channels]
        skip = parts_ref[i * WP : (i + 1) * WP].astype(F32)
        outs.append((skip + norm(shuffled, expand_gain_ref[...])).astype(BF16))
    moves = sent_to(expand_order_ref, out_ref.shape[0])
    out_ref[...] = dot(moves, jnp.concatenate(outs, axis=0)).astype(BF16)


WHOLE = pl.BlockSpec(memory_space=pltpu.VMEM)
APART = pl.BlockSpec(memory_space=pltpu.HBM)


def in_hbm(array):
    return pltpu.with_memory_space_constraint(array, pltpu.HBM)


def weight_scratch(weights):
    return [pltpu.VMEM(w.shape[1:], BF16) for w in weights]


def halo(own, top, bottom, beside=None):
    rows, cols, _, channels = own.shape
    top = top.reshape(own.shape[1:])
    bottom = bottom.reshape(own.shape[1:])
    lat = lax.axis_size("lat")
    lon = lax.axis_size(LON)
    down = [(i, (i + 1) % lat) for i in range(lat)]
    up = [((i + 1) % lat, i) for i in range(lat)]
    east = [(i, (i + 1) % lon) for i in range(lon)]
    west = [((i + 1) % lon, i) for i in range(lon)]
    north = lax.ppermute(bottom, "lat", down)
    south = lax.ppermute(top, "lat", up)
    if beside is not None:
        north, south, beside = lax.optimization_barrier((north, south, beside))

    def side(c):
        return jnp.concatenate([north[c : c + 1], own[:, c], south[c : c + 1]], axis=0)

    from_west = lax.ppermute(side(cols - 1), LON, east)
    from_east = lax.ppermute(side(0), LON, west)
    halos = [v.reshape(-1, channels) for v in (own, north, south, from_west, from_east)]
    return halos if beside is None else (halos, beside)


def shifted_scratch(rows, cols, channels):
    line = (cols + 2) * QP
    return [
        pltpu.VMEM((rows * line, channels), F32),
        pltpu.VMEM(((rows + 2) * line, channels), BF16),
        pltpu.VMEM(((rows + 2) * line, channels), BF16),
        pltpu.VMEM((rows * cols * QP, channels), F32),
    ]


def on_device(
    fields, land_sea, land_embed, bias_index, fine_bias, fine_gains, fine_query_key_value,
    fine_project, fine_widen, fine_narrow, merge_gain, merge_weight, coarse_bias, coarse_gains,
    coarse_query_key_value, coarse_project, coarse_widen, coarse_narrow, expand_weight, expand_gain,
):
    _, rows, cols, channels = fields.shape
    quad_rows, quad_cols = rows // HALF_LAT, cols // HALF_LON
    tokens = quad_rows * quad_cols * QP
    wide = merge_weight.shape[1]
    order, of_row, of_col = fine_tables(rows, cols)
    bias_first, ordered = bias_of([(fine_bias, 0)], bias_index, 16, fresh=True)
    (bias_second,) = bias_of([(fine_bias, 1)], ordered, 16)
    (bias_third,) = bias_of([(coarse_bias, 0)], ordered, 16)
    (bias_last,) = bias_of([(coarse_bias, 1)], ordered, 16)
    fine_weights = (
        fine_query_key_value, fine_project, fine_widen, fine_narrow.transpose(0, 2, 1)
    )
    coarse_weights = (coarse_query_key_value, coarse_project, coarse_widen, coarse_narrow)
    steps = bias_first.shape[1]
    dma = pltpu.SemaphoreType.DMA
    fine_scratch = pltpu.VMEM((2, HF, WP, 128), F32)
    coarse_scratch = pltpu.VMEM((2, HC, WP, 128), F32)
    line = quad_cols * QP

    first, top, bottom = pl.pallas_call(
        first_kernel,
        out_shape=[
            jax.ShapeDtypeStruct((tokens, channels), BF16),
            jax.ShapeDtypeStruct((line, channels), BF16),
            jax.ShapeDtypeStruct((line, channels), BF16),
        ],
        in_specs=[WHOLE] * 7 + [APART] * 5,
        out_specs=[WHOLE] * 3,
        scratch_shapes=[pltpu.VMEM((tokens, channels), BF16), fine_scratch]
        + weight_scratch(fine_weights) + [dma((4,)), dma((2 * steps,))],
        compiler_params=pltpu.CompilerParams(vmem_limit_bytes=20 << 20),
        name="fine_plain",
    )(
        fields.reshape(-1, channels), land_sea, land_embed[None], order, of_row, of_col,
        fine_gains, bias_first, *fine_weights,
    )

    halos, bias_second = halo(
        first.reshape(quad_rows, quad_cols, QP, channels), top, bottom, bias_second
    )
    parts, coarse, top, bottom = pl.pallas_call(
        middle_kernel,
        out_shape=[
            jax.ShapeDtypeStruct((tokens, channels), BF16),
            jax.ShapeDtypeStruct((tokens // 4, wide), BF16),
            jax.ShapeDtypeStruct((line // 2, wide), BF16),
            jax.ShapeDtypeStruct((line // 2, wide), BF16),
        ],
        in_specs=[WHOLE] * 9 + [APART] * 11,
        out_specs=[WHOLE] * 4,
        scratch_shapes=shifted_scratch(quad_rows, quad_cols, channels)
        + [fine_scratch, coarse_scratch] + weight_scratch(fine_weights)
        + [pltpu.VMEM(merge_weight.shape, BF16)]
        + weight_scratch(coarse_weights) + [dma((9,)), dma((4 * steps,))],
        compiler_params=pltpu.CompilerParams(vmem_limit_bytes=36 << 20),
        name="fine_shifted_coarse_plain",
    )(
        *halos, fine_gains, merge_gain, coarse_gains,
        merge_table(rows, cols), bias_second, bias_third,
        *[in_hbm(w) for w in fine_weights], in_hbm(merge_weight),
        *[in_hbm(w) for w in coarse_weights],
    )

    out = pl.pallas_call(
        last_kernel,
        out_shape=jax.ShapeDtypeStruct((LEVELS * rows * cols, channels), BF16),
        in_specs=[WHOLE] * 9 + [APART] * 6,
        out_specs=WHOLE,
        scratch_shapes=shifted_scratch(quad_rows // 2, quad_cols // 2, wide)
        + [coarse_scratch] + weight_scratch(coarse_weights)
        + [pltpu.VMEM(expand_weight.shape, BF16)]
        + [dma((5,)), dma((2 * steps,))],
        compiler_params=pltpu.CompilerParams(vmem_limit_bytes=28 << 20),
        name="coarse_shifted_expand",
    )(
        *halo(coarse.reshape(quad_rows // 2, quad_cols // 2, QP, wide), top, bottom),
        coarse_gains, parts, expand_gain[None], expand_table(rows, cols),
        bias_last, *coarse_weights, expand_weight,
    )
    return out.reshape(fields.shape)


def solution(mesh):
    grid = P(None, "lat", LON, None)
    return jax.shard_map(
        on_device,
        mesh=mesh,
        in_specs=(grid, P("lat", LON)) + (P(),) * 18,
        out_specs=grid,
        check_vma=False,
    )
```

```python
import functools

import jax
import jax.numpy as jnp
import numpy as np
from jax import lax
from jax.experimental import pallas as pl
from jax.experimental.pallas import tpu as pltpu
from jax.sharding import PartitionSpec as P

HF = 6
HC = 12
HEAD = 32
WIN_LAT = 6
WIN_LON = 12
WIN_TOK = 144
HALF_LAT = WIN_LAT // 2
HALF_LON = WIN_LON // 2
LEVELS = 2
QUAD = LEVELS * HALF_LAT * HALF_LON
QP = 40
WP = 4 * QP
LO_COUNT = 13
LOG2E = 1.4426950408889634
MASKED = -1e30
LON = ("sec", "head")
F32 = jnp.float32
BF16 = jnp.bfloat16


def quad_sources(row_count, col_count):
    slots = []
    for a in range(row_count // HALF_LAT):
        for b in range(col_count // HALF_LON):
            for s in range(QP):
                if s >= QUAD:
                    slots.append(None)
                    continue
                level, rest = divmod(s, HALF_LAT * HALF_LON)
                r, c = divmod(rest, HALF_LON)
                slots.append((level, a * HALF_LAT + r, b * HALF_LON + c))
    return slots


def one_hot(sources, width):
    table = np.zeros((len(sources), width), np.float32)
    for slot, source in enumerate(sources):
        if source is not None:
            table[slot, source] = 1.0
    return jnp.asarray(table.astype(jnp.bfloat16))


def target_row(targets):
    return jnp.asarray(np.array([-1 if t is None else t for t in targets], np.int32)[None])


def fine_tables(rows, cols):
    slots = quad_sources(rows, cols)
    place = {s: n for n, s in enumerate(slots) if s is not None}
    order = target_row(
        [place[(level, r, c)] for level in range(LEVELS) for r in range(rows) for c in range(cols)]
    )
    of_row = one_hot([None if s is None else s[1] for s in slots], rows)
    of_col = one_hot([None if s is None else s[2] for s in slots], cols)
    return order, of_row, of_col


def merge_table(rows, cols):
    coarse = quad_sources(rows // 2, cols // 2)
    place = {s: n for n, s in enumerate(coarse) if s is not None}
    return target_row(
        [
            None
            if s is None
            else ((s[1] % 2) * 2 + s[2] % 2) * len(coarse) + place[(s[0], s[1] // 2, s[2] // 2)]
            for s in quad_sources(rows, cols)
        ]
    )


def expand_table(rows, cols):
    return target_row(
        [
            None
            if s is None
            else (s[0] * rows + 2 * s[1] + p) * cols + 2 * s[2] + q
            for p in range(2)
            for q in range(2)
            for s in quad_sources(rows // 2, cols // 2)
        ]
    )


def sent_to(target_ref, count):
    width = target_ref.shape[1]
    slot = lax.broadcasted_iota(jnp.int32, (count, width), 0)
    return jnp.where(slot == target_ref[...], 1.0, 0.0).astype(BF16)


def dot(a, b):
    return jnp.dot(a, b, preferred_element_type=F32)


def dot_t(a, b):
    return lax.dot_general(a, b, (((1,), (1,)), ((), ())), preferred_element_type=F32)


def norm(x, gain):
    mean = jnp.mean(x, axis=-1, keepdims=True)
    centered = x - mean
    variance = jnp.mean(centered * centered, axis=-1, keepdims=True)
    return centered * lax.rsqrt(variance + 1e-05) * gain


def attend(q, k, v, bias_ref, firsts, key_mask):
    n = q.shape[0]
    channels = q.shape[1]
    scale = HEAD**-0.5 * LOG2E
    outs = []
    for tile in range(0, channels, 128):
        width = min(128, channels - tile)
        count = width // HEAD
        qt = q[:, tile : tile + width]
        lane = lax.broadcasted_iota(jnp.int32, (n, width), 1) // HEAD
        masks = [lane == h for h in range(count)]
        stack = jnp.concatenate([jnp.where(m, qt, jnp.zeros_like(qt)) for m in masks], axis=0)
        scores = dot_t(stack, k[:, tile : tile + width])
        probs = []
        for h in range(count):
            head = tile // HEAD + h
            bias = jnp.concatenate(
                [
                    jnp.concatenate(
                        [
                            bias_ref[half, f // QP + i, head, :, :width]
                            for f in firsts
                            for i in range(n // len(firsts) // QP)
                        ],
                        axis=0,
                    )
                    for half, width in ((0, 128), (1, WP - 128))
                ],
                axis=1,
            )
            s = scores[h * n : (h + 1) * n] * scale + bias
            if key_mask is not None:
                s = s + key_mask
            s = s - jnp.max(s, axis=-1, keepdims=True)
            probs.append(jnp.exp2(s).astype(BF16))
        probs = jnp.concatenate(probs, axis=0)
        vt = v[:, tile : tile + width]
        mixed = dot(probs, jnp.concatenate([vt, jnp.ones((WP, width), BF16)], axis=1))
        top = mixed[:n, :width]
        total = mixed[:n, width:]
        for h in range(1, count):
            top = jnp.where(masks[h], mixed[h * n : (h + 1) * n, :width], top)
            total = jnp.where(masks[h], mixed[h * n : (h + 1) * n, width:], total)
        outs.append(top / total)
    return outs[0] if len(outs) == 1 else jnp.concatenate(outs, axis=1)


def gelu(x):
    return 0.5 * x * (1.0 + lax.erf(x * np.float32(0.5**0.5)))


def finish(x, context, gain, w_project, w_widen, w_narrow):
    middle = (x + dot(context, w_project)).astype(BF16).astype(F32)
    second = norm(middle, gain).astype(BF16)
    hidden = gelu(dot(second, w_widen)).astype(BF16)
    narrow = dot if w_narrow.shape[0] > w_narrow.shape[1] else dot_t
    return (middle + narrow(hidden, w_narrow)).astype(BF16)


def padded(heads):
    return -(-heads // 8) * 8


def window_order():
    token = lax.broadcasted_iota(jnp.int32, (WP, WIN_TOK), 1)
    level = jnp.where(token >= WIN_LAT * WIN_LON, 1, 0)
    token = token - level * (WIN_LAT * WIN_LON)
    row = sum(jnp.where(token >= WIN_LON * r, 1, 0) for r in range(1, WIN_LAT))
    col = token - row * WIN_LON
    down = jnp.where(row >= HALF_LAT, 1, 0)
    across = jnp.where(col >= HALF_LON, 1, 0)
    slot = (
        (2 * down + across) * QP
        + level * (HALF_LAT * HALF_LON)
        + (row - down * HALF_LAT) * HALF_LON
        + (col - across * HALF_LON)
    )
    place = lax.broadcasted_iota(jnp.int32, (WP, WIN_TOK), 0)
    return jnp.where(slot == place, 1.0, 0.0).astype(BF16)


def halved(heads):
    return heads % 8 == 4


def row_groups(head_counts):
    groups = []
    at = 0
    for heads in head_counts:
        count = padded(heads) // 8
        for g in range(count):
            groups.append((at + g * 8, 2 if halved(heads) and g == count - 1 else 1))
        at += padded(heads)
    return groups


def bias_kernel(*refs, picks, fresh):
    if fresh:
        index_ref, *table_refs, out_ref, index, table, left = refs
    else:
        index, *table_refs, out_ref, table, left = refs
    rows = table.shape[0]
    bias_len = table_refs[0].shape[-1]
    groups = row_groups([t.shape[0] for t in table_refs])

    @pl.when(pl.program_id(0) == 0)
    def _():
        if fresh:
            spread = window_order()
            plain = index_ref[...]
            high = (plain >> 4).astype(F32).astype(BF16)
            low = (plain & 15).astype(F32).astype(BF16)

            def moved(part):
                return dot_t(dot(spread, part).astype(BF16), spread).astype(jnp.int32)

            spot = lax.broadcasted_iota(jnp.int32, (WP, WP), 1) % QP
            index[...] = jnp.where(spot < QUAD, moved(high) * 16 + moved(low), bias_len)
        table[...] = jnp.full(table.shape, MASKED, F32)
        at = 0
        for table_ref, block in zip(table_refs, picks):
            heads = table_ref.shape[0]
            for h in range(heads):
                line = table_ref[h, block : block + 1, :] * LOG2E
                table[at + h : at + h + 1, :bias_len] = line
                if halved(heads) and h >= heads - 4:
                    table[at + h + 4 : at + h + 5, : bias_len - 256] = line[:, 256:]
            at += padded(heads)
        values = table[...]
        big = values.astype(BF16)
        small = (values - big.astype(F32)).astype(BF16)
        for n, part in enumerate((big, small)):
            left[:, n * 256 : (n + 1) * 256] = jnp.concatenate(
                [
                    part[row : row + 8, i * 256 : (i + 1) * 256]
                    for row, stride in groups
                    for i in range(0, LO_COUNT, stride)
                ],
                axis=0,
            )

    ladder = lax.broadcasted_iota(jnp.int32, (256, 256), 0).astype(F32).astype(BF16)
    lane = lax.broadcasted_iota(jnp.int32, (8, 256), 1) // 32
    sublane = lax.broadcasted_iota(jnp.int32, (8, 256), 0)
    low_half = lax.broadcasted_iota(jnp.int32, (8, 256), 0) // 4
    span = out_ref.shape[1] // rows
    for group in range(span // 8):
        first = pl.multiple_of(pl.program_id(0) * span + group * 8, 8)
        count = min(8, QUAD - group * 8)
        entries = index[pl.ds(first, 8), :]
        rest = jnp.concatenate([entries[:, 128:]] * 8, axis=1)
        rest = jnp.sum(jnp.where(lane == sublane, rest, 0).astype(F32), axis=0, keepdims=True)
        pieces = [
            jnp.concatenate([entries[j : j + 1, :128], entries[j + 1 : j + 2, :128]], axis=1)
            for j in range(0, count, 2)
        ] + [rest.astype(jnp.int32)]
        for t, entry in enumerate(pieces):
            near = (entry & 255).astype(F32).astype(BF16)
            far = entry >> 8
            chosen = jnp.where(ladder == near, jnp.ones((), BF16), jnp.zeros((), BF16))
            found = dot(left[...], jnp.concatenate([chosen, chosen], axis=0))
            shifted_far = far - low_half
            unit = 0
            for row, stride in groups:
                part = found[unit : unit + 8]
                unit += 8
                for i in range(stride, LO_COUNT, stride):
                    here = (far if stride == 1 else shifted_far) == i
                    part = jnp.where(here, found[unit : unit + 8], part)
                    unit += 8
                if stride == 2:
                    part = jnp.where((far & 1) == 0, part, pltpu.roll(part, 4, 0))
                at = row * span + group * 8
                if t < len(pieces) - 1:
                    for j in range(2):
                        out_ref[0, pl.ds(at + 2 * t + j, 8, stride=span), :] = (
                            part[:, j * 128 : (j + 1) * 128]
                        )
                else:
                    for j in range(count):
                        moved_part = part[:, j // 4 * 128 : (j // 4 + 1) * 128]
                        if j % 4:
                            moved_part = pltpu.roll(moved_part, 128 - 32 * (j % 4), 1)
                        out_ref[1, pl.ds(at + j, 8, stride=span), :] = moved_part
        for row, _ in groups:
            for j in range(count, 8):
                for half in range(2):
                    out_ref[half, pl.ds(row * span + group * 8 + j, 8, stride=span), :] = (
                        jnp.zeros((8, 128), F32)
                    )


def bias_of(picks, order, vmem, fresh=False, span=QP):
    tables = [t.transpose(1, 0, 2) for t, _ in picks]
    if fresh:
        order, tables = in_hbm(order), [in_hbm(t) for t in tables]
    rows = sum(padded(t.shape[0]) for t in tables)
    units = sum(-(-LO_COUNT // stride) for _, stride in row_groups([t.shape[0] for t in tables]))
    flops = 2 * WP * 256 * WP * units * 8 * 4
    steps = WP // span
    out_shape = [jax.ShapeDtypeStruct((2, steps * rows * span, 128), F32)]
    out_specs = [pl.BlockSpec((2, rows * span, 128), lambda i: (0, i, 0))]
    if fresh:
        out_shape.append(jax.ShapeDtypeStruct((WP, WP), jnp.int32))
        out_specs.append(pl.BlockSpec((WP, WP), lambda i: (0, 0)))
    out = pl.pallas_call(
        functools.partial(bias_kernel, picks=tuple(b for _, b in picks), fresh=fresh),
        out_shape=out_shape,
        grid=(steps,),
        in_specs=[pl.BlockSpec(memory_space=pltpu.VMEM)] * (1 + len(tables)),
        out_specs=out_specs,
        scratch_shapes=[
            pltpu.VMEM((rows, LO_COUNT * 256), F32),
            pltpu.VMEM((units * 8, 512), BF16),
        ],
        compiler_params=pltpu.CompilerParams(vmem_limit_bytes=vmem << 20),
        cost_estimate=pl.CostEstimate(flops=2 * flops, bytes_accessed=1 << 20, transcendentals=0),
        name="bias_table",
    )(order, *tables)
    return [out[0].reshape(2, steps, rows, span, 128)] + list(out[1:])


class Fetched:
    def __init__(self, copies):
        self.copies = copies
        for group in copies:
            for copy in group:
                copy.start()

    def wait(self, *numbers):
        for n in numbers:
            for copy in self.copies[n]:
                copy.wait()


def first_kernel(
    fields_ref, land_ref, embed_ref, order_ref, of_row_ref, of_col_ref, gains_ref,
    bias, triple_ref, project_ref, widen_ref, narrow_ref, out_ref, top_ref, bottom_ref, context,
):
    channels = fields_ref.shape[1]
    land = land_ref[...].astype(F32).astype(BF16)
    on_row = dot(of_row_ref[...], land)
    on_land = jnp.sum(on_row * of_col_ref[...].astype(F32), axis=-1, keepdims=True)
    rows = out_ref.shape[0]
    start = dot(sent_to(order_ref, rows), fields_ref[...]) + on_land * embed_ref[...]
    x = start.astype(BF16).astype(F32)
    normed = norm(x, gains_ref[0, 0:1]).astype(BF16)
    triple = dot(normed, triple_ref[0]).astype(BF16)
    inner = top_ref.shape[0]
    for a in range(rows // inner // 2):
        for b in range(inner // QP // 2):
            top = 2 * a * inner + 2 * b * QP
            below = top + inner
            window = jnp.concatenate(
                [triple[top : top + 2 * QP], triple[below : below + 2 * QP]], axis=0
            )
            mixed = attend(
                window[:, :channels],
                window[:, channels : 2 * channels],
                window[:, 2 * channels :],
                bias, [0], None,
            ).astype(BF16)
            context[top : top + 2 * QP] = mixed[: 2 * QP]
            context[below : below + 2 * QP] = mixed[2 * QP :]
    done = finish(
        x, context[...], gains_ref[0, 1:2], project_ref[0], widen_ref[0], narrow_ref[0]
    )
    out_ref[...] = done
    top_ref[...] = done[:inner]
    bottom_ref[...] = done[rows - inner :]


def shifted_block(
    own_ref, north_ref, south_ref, west_ref, east_ref, gains_ref, fetched,
    bias, w_triple, w_project, w_widen, w_narrow, query, key, value, context,
):
    channels = own_ref.shape[1]
    across = north_ref.shape[0] // QP
    down = own_ref.shape[0] // QP // across
    line = (across + 2) * QP
    inner = across * QP
    pieces = []
    for i in range(down + 2):
        if i == 0:
            middle = north_ref[...]
        elif i == down + 1:
            middle = south_ref[...]
        else:
            middle = own_ref[(i - 1) * inner : i * inner]
        pieces += [
            west_ref[i * QP : (i + 1) * QP].astype(F32),
            middle.astype(F32),
            east_ref[i * QP : (i + 1) * QP].astype(F32),
        ]
    normed = norm(jnp.concatenate(pieces, axis=0), gains_ref[1, 0:1]).astype(BF16)
    fetched.wait(0)
    query[...] = dot(normed[line : (down + 1) * line], w_triple[:, :channels])
    both = dot(normed, w_triple[:, channels:]).astype(BF16)
    key[...] = both[:, :channels]
    value[...] = both[:, channels:]
    lane = lax.broadcasted_iota(jnp.int32, (1, WP), 1)
    place = lax.axis_index("lat")
    on_top = jnp.where(place == 0, MASKED, 0.0).astype(F32)
    on_bottom = jnp.where(place == lax.axis_size("lat") - 1, MASKED, 0.0).astype(F32)
    for wa in range(down // 2 + 1):
        mask = None
        if wa == 0:
            mask = jnp.where(lane < 2 * QP, on_top, 0.0)
        elif wa == down // 2:
            mask = jnp.where(lane < 2 * QP, 0.0, on_bottom)
        for wb in range(across // 2 + 1):
            at = [(2 * wa + r) * line + 2 * wb * QP for r in range(2)]
            k = jnp.concatenate([key[s : s + 2 * QP] for s in at], axis=0)
            v = jnp.concatenate([value[s : s + 2 * QP] for s in at], axis=0)
            rows = [r for r in range(2) if 0 < 2 * wa + r < down + 1]
            cols = [c for c in range(2) if 0 < 2 * wb + c < across + 1]
            size = len(cols) * QP
            qs = [
                query[
                    (2 * wa + r - 1) * line + (2 * wb + cols[0]) * QP :
                    (2 * wa + r - 1) * line + (2 * wb + cols[0]) * QP + size
                ]
                for r in rows
            ]
            out = attend(
                jnp.concatenate(qs, axis=0).astype(BF16), k, v, bias,
                [(2 * r + cols[0]) * QP for r in rows], mask,
            )
            for n, r in enumerate(rows):
                to = ((2 * wa + r - 1) * across + 2 * wb + cols[0] - 1) * QP
                context[to : to + size] = out[n * size : (n + 1) * size]
    fetched.wait(1, 2, 3)
    return finish(
        own_ref[...].astype(F32), context[...].astype(BF16), gains_ref[1, 1:2],
        w_project[...], w_widen[...], w_narrow[...],
    )


def block_copies(pairs, block, sems, at):
    return [
        [pltpu.make_async_copy(source.at[block], target, sems.at[at + n])]
        for n, (source, target) in enumerate(pairs)
    ]


def middle_kernel(
    own_ref, north_ref, south_ref, west_ref, east_ref, gains_ref, merge_gain_ref,
    coarse_gains_ref, merge_order_ref, bias, c_bias, triple_hbm, project_hbm, widen_hbm, narrow_hbm,
    merge_weight_hbm, c_triple_hbm, c_project_hbm, c_widen_hbm, c_narrow_hbm,
    parts_ref, coarse_ref, top_ref, bottom_ref,
    query, key, value, context, w_triple, w_project, w_widen, w_narrow,
    merge_weight, c_triple, c_project, c_widen, c_narrow, sems,
):
    fetched = Fetched(
        block_copies(
            [(triple_hbm, w_triple), (project_hbm, w_project),
             (widen_hbm, w_widen), (narrow_hbm, w_narrow)], 1, sems, 0,
        )
        + [[pltpu.make_async_copy(merge_weight_hbm, merge_weight, sems.at[4])]]
        + block_copies(
            [(c_triple_hbm, c_triple), (c_project_hbm, c_project),
             (c_widen_hbm, c_widen), (c_narrow_hbm, c_narrow)], 0, sems, 5,
        )
    )
    skip = shifted_block(
        own_ref, north_ref, south_ref, west_ref, east_ref, gains_ref, fetched,
        bias, w_triple, w_project, w_widen, w_narrow, query, key, value, context,
    )
    channels = own_ref.shape[1]
    grouped = dot(sent_to(merge_order_ref, skip.shape[0]), skip)
    parts_ref[...] = grouped.astype(BF16)
    parts = [grouped[i * WP : (i + 1) * WP] for i in range(4)]
    width = 4 * channels
    mean = sum(jnp.sum(p, axis=-1, keepdims=True) for p in parts) / width
    parts = [p - mean for p in parts]
    variance = sum(jnp.sum(p * p, axis=-1, keepdims=True) for p in parts) / width
    factor = lax.rsqrt(variance + 1e-05)
    merge_gain = merge_gain_ref[...].reshape(1, width)
    fetched.wait(4)
    coarse = jnp.zeros((WP, merge_weight.shape[1]), F32)
    for i, p in enumerate(parts):
        gain = merge_gain[:, i * channels : (i + 1) * channels]
        merged = (p * factor * gain).astype(BF16)
        coarse = coarse + dot(merged, merge_weight[i * channels : (i + 1) * channels])
    x = coarse.astype(BF16).astype(F32)
    wide = x.shape[1]
    normed = norm(x, coarse_gains_ref[0, 0:1]).astype(BF16)
    fetched.wait(5)
    triple = dot(normed, c_triple[...]).astype(BF16)
    mixed = attend(
        triple[:, :wide], triple[:, wide : 2 * wide], triple[:, 2 * wide :], c_bias, [0], None
    ).astype(BF16)
    fetched.wait(6, 7, 8)
    done = finish(
        x, mixed, coarse_gains_ref[0, 1:2], c_project[...], c_widen[...], c_narrow[...]
    )
    coarse_ref[...] = done
    inner = top_ref.shape[0]
    top_ref[...] = done[:inner]
    bottom_ref[...] = done[WP - inner :]


def last_kernel(
    own_ref, north_ref, south_ref, west_ref, east_ref, gains_ref, parts_ref, expand_gain_ref,
    expand_order_ref, bias, triple_ref, project_ref, widen_ref, narrow_ref, expand_weight_ref,
    out_ref,
    query, key, value, context,
):
    fetched = Fetched([[]] * 4)
    w_triple, w_project, w_widen, w_narrow = (
        ref.at[1] for ref in (triple_ref, project_ref, widen_ref, narrow_ref)
    )
    deep = shifted_block(
        own_ref, north_ref, south_ref, west_ref, east_ref, gains_ref, fetched,
        bias, w_triple, w_project, w_widen, w_narrow, query, key, value, context,
    )
    channels = parts_ref.shape[1]
    widened = dot(deep, expand_weight_ref[...])
    outs = []
    for i in range(4):
        shuffled = widened[:, i * channels : (i + 1) * channels]
        skip = parts_ref[i * WP : (i + 1) * WP].astype(F32)
        outs.append((skip + norm(shuffled, expand_gain_ref[...])).astype(BF16))
    moves = sent_to(expand_order_ref, out_ref.shape[0])
    out_ref[...] = dot(moves, jnp.concatenate(outs, axis=0)).astype(BF16)


WHOLE = pl.BlockSpec(memory_space=pltpu.VMEM)
APART = pl.BlockSpec(memory_space=pltpu.HBM)


def in_hbm(array):
    return pltpu.with_memory_space_constraint(array, pltpu.HBM)


def weight_scratch(weights):
    return [pltpu.VMEM(w.shape[1:], BF16) for w in weights]


def halo(own, top, bottom, beside=None):
    rows, cols, _, channels = own.shape
    top = top.reshape(own.shape[1:])
    bottom = bottom.reshape(own.shape[1:])
    lat = lax.axis_size("lat")
    lon = lax.axis_size(LON)
    down = [(i, (i + 1) % lat) for i in range(lat)]
    up = [((i + 1) % lat, i) for i in range(lat)]
    east = [(i, (i + 1) % lon) for i in range(lon)]
    west = [((i + 1) % lon, i) for i in range(lon)]
    north = lax.ppermute(bottom, "lat", down)
    south = lax.ppermute(top, "lat", up)
    if beside is not None:
        north, south, beside = lax.optimization_barrier((north, south, beside))

    def side(c):
        return jnp.concatenate([north[c : c + 1], own[:, c], south[c : c + 1]], axis=0)

    from_west = lax.ppermute(side(cols - 1), LON, east)
    from_east = lax.ppermute(side(0), LON, west)
    halos = [v.reshape(-1, channels) for v in (own, north, south, from_west, from_east)]
    return halos if beside is None else (halos, beside)


def shifted_scratch(rows, cols, channels):
    line = (cols + 2) * QP
    return [
        pltpu.VMEM((rows * line, channels), F32),
        pltpu.VMEM(((rows + 2) * line, channels), BF16),
        pltpu.VMEM(((rows + 2) * line, channels), BF16),
        pltpu.VMEM((rows * cols * QP, channels), F32),
    ]


def on_device(
    fields, land_sea, land_embed, bias_index, fine_bias, fine_gains, fine_query_key_value,
    fine_project, fine_widen, fine_narrow, merge_gain, merge_weight, coarse_bias, coarse_gains,
    coarse_query_key_value, coarse_project, coarse_widen, coarse_narrow, expand_weight, expand_gain,
):
    _, rows, cols, channels = fields.shape
    quad_rows, quad_cols = rows // HALF_LAT, cols // HALF_LON
    tokens = quad_rows * quad_cols * QP
    wide = merge_weight.shape[1]
    order, of_row, of_col = fine_tables(rows, cols)
    bias_first, ordered = bias_of([(fine_bias, 0)], bias_index, 16, fresh=True)
    (bias_second,) = bias_of([(fine_bias, 1)], ordered, 16)
    (bias_third,) = bias_of([(coarse_bias, 0)], ordered, 16)
    (bias_last,) = bias_of([(coarse_bias, 1)], ordered, 16)
    fine_weights = (
        fine_query_key_value, fine_project, fine_widen, fine_narrow.transpose(0, 2, 1)
    )
    coarse_weights = (coarse_query_key_value, coarse_project, coarse_widen, coarse_narrow)
    dma = pltpu.SemaphoreType.DMA
    line = quad_cols * QP

    first, top, bottom = pl.pallas_call(
        first_kernel,
        out_shape=[
            jax.ShapeDtypeStruct((tokens, channels), BF16),
            jax.ShapeDtypeStruct((line, channels), BF16),
            jax.ShapeDtypeStruct((line, channels), BF16),
        ],
        in_specs=[WHOLE] * 12,
        out_specs=[WHOLE] * 3,
        scratch_shapes=[pltpu.VMEM((tokens, channels), BF16)],
        compiler_params=pltpu.CompilerParams(vmem_limit_bytes=20 << 20),
        name="fine_plain",
    )(
        fields.reshape(-1, channels), land_sea, land_embed[None], order, of_row, of_col,
        fine_gains, bias_first, *fine_weights,
    )

    halos, bias_second = halo(
        first.reshape(quad_rows, quad_cols, QP, channels), top, bottom, bias_second
    )
    parts, coarse, top, bottom = pl.pallas_call(
        middle_kernel,
        out_shape=[
            jax.ShapeDtypeStruct((tokens, channels), BF16),
            jax.ShapeDtypeStruct((tokens // 4, wide), BF16),
            jax.ShapeDtypeStruct((line // 2, wide), BF16),
            jax.ShapeDtypeStruct((line // 2, wide), BF16),
        ],
        in_specs=[WHOLE] * 11 + [APART] * 9,
        out_specs=[WHOLE] * 4,
        scratch_shapes=shifted_scratch(quad_rows, quad_cols, channels)
        + weight_scratch(fine_weights)
        + [pltpu.VMEM(merge_weight.shape, BF16)]
        + weight_scratch(coarse_weights) + [dma((9,))],
        compiler_params=pltpu.CompilerParams(vmem_limit_bytes=36 << 20),
        name="fine_shifted_coarse_plain",
    )(
        *halos, fine_gains, merge_gain, coarse_gains,
        merge_table(rows, cols), bias_second, bias_third,
        *[in_hbm(w) for w in fine_weights], in_hbm(merge_weight),
        *[in_hbm(w) for w in coarse_weights],
    )

    out = pl.pallas_call(
        last_kernel,
        out_shape=jax.ShapeDtypeStruct((LEVELS * rows * cols, channels), BF16),
        in_specs=[WHOLE] * 15,
        out_specs=WHOLE,
        scratch_shapes=shifted_scratch(quad_rows // 2, quad_cols // 2, wide),
        compiler_params=pltpu.CompilerParams(vmem_limit_bytes=28 << 20),
        name="coarse_shifted_expand",
    )(
        *halo(coarse.reshape(quad_rows // 2, quad_cols // 2, QP, wide), top, bottom),
        coarse_gains, parts, expand_gain[None], expand_table(rows, cols),
        bias_last, *coarse_weights, expand_weight,
    )
    return out.reshape(fields.shape)


def solution(mesh):
    grid = P(None, "lat", LON, None)
    return jax.shard_map(
        on_device,
        mesh=mesh,
        in_specs=(grid, P("lat", LON)) + (P(),) * 18,
        out_specs=grid,
        check_vma=False,
    )
```

```python
import functools

import jax
import jax.numpy as jnp
import numpy as np
from jax import lax
from jax.experimental import pallas as pl
from jax.experimental.pallas import tpu as pltpu
from jax.sharding import PartitionSpec as P

HF = 6
HC = 12
HEAD = 32
WIN_LAT = 6
WIN_LON = 12
WIN_TOK = 144
HALF_LAT = WIN_LAT // 2
HALF_LON = WIN_LON // 2
LEVELS = 2
QUAD = LEVELS * HALF_LAT * HALF_LON
QP = 40
WP = 4 * QP
LO_COUNT = 13
LOG2E = 1.4426950408889634
MASKED = -1e30
LON = ("sec", "head")
F32 = jnp.float32
BF16 = jnp.bfloat16


def quad_sources(row_count, col_count):
    slots = []
    for a in range(row_count // HALF_LAT):
        for b in range(col_count // HALF_LON):
            for s in range(QP):
                if s >= QUAD:
                    slots.append(None)
                    continue
                level, rest = divmod(s, HALF_LAT * HALF_LON)
                r, c = divmod(rest, HALF_LON)
                slots.append((level, a * HALF_LAT + r, b * HALF_LON + c))
    return slots


def one_hot(sources, width):
    table = np.zeros((len(sources), width), np.float32)
    for slot, source in enumerate(sources):
        if source is not None:
            table[slot, source] = 1.0
    return jnp.asarray(table.astype(jnp.bfloat16))


def target_row(targets):
    return jnp.asarray(np.array([-1 if t is None else t for t in targets], np.int32)[None])


def fine_tables(rows, cols):
    slots = quad_sources(rows, cols)
    place = {s: n for n, s in enumerate(slots) if s is not None}
    order = target_row(
        [place[(level, r, c)] for level in range(LEVELS) for r in range(rows) for c in range(cols)]
    )
    of_row = one_hot([None if s is None else s[1] for s in slots], rows)
    of_col = one_hot([None if s is None else s[2] for s in slots], cols)
    return order, of_row, of_col


def merge_table(rows, cols):
    coarse = quad_sources(rows // 2, cols // 2)
    place = {s: n for n, s in enumerate(coarse) if s is not None}
    return target_row(
        [
            None
            if s is None
            else ((s[1] % 2) * 2 + s[2] % 2) * len(coarse) + place[(s[0], s[1] // 2, s[2] // 2)]
            for s in quad_sources(rows, cols)
        ]
    )


def expand_table(rows, cols):
    return target_row(
        [
            None
            if s is None
            else (s[0] * rows + 2 * s[1] + p) * cols + 2 * s[2] + q
            for p in range(2)
            for q in range(2)
            for s in quad_sources(rows // 2, cols // 2)
        ]
    )


def sent_to(target_ref, count):
    width = target_ref.shape[1]
    slot = lax.broadcasted_iota(jnp.int32, (count, width), 0)
    return jnp.where(slot == target_ref[...], 1.0, 0.0).astype(BF16)


def dot(a, b):
    return jnp.dot(a, b, preferred_element_type=F32)


def dot_t(a, b):
    return lax.dot_general(a, b, (((1,), (1,)), ((), ())), preferred_element_type=F32)


def norm(x, gain):
    mean = jnp.mean(x, axis=-1, keepdims=True)
    centered = x - mean
    variance = jnp.mean(centered * centered, axis=-1, keepdims=True)
    return centered * lax.rsqrt(variance + 1e-05) * gain


def attend(q, k, v, bias_ref, firsts, key_mask):
    n = q.shape[0]
    channels = q.shape[1]
    scale = HEAD**-0.5 * LOG2E
    outs = []
    for tile in range(0, channels, 128):
        width = min(128, channels - tile)
        count = width // HEAD
        qt = q[:, tile : tile + width]
        lane = lax.broadcasted_iota(jnp.int32, (n, width), 1) // HEAD
        masks = [lane == h for h in range(count)]
        stack = jnp.concatenate([jnp.where(m, qt, jnp.zeros_like(qt)) for m in masks], axis=0)
        scores = dot_t(stack, k[:, tile : tile + width])
        probs = []
        for h in range(count):
            head = tile // HEAD + h
            bias = jnp.concatenate(
                [
                    jnp.concatenate(
                        [
                            bias_ref[half, f // QP + i, head, :, :width]
                            for f in firsts
                            for i in range(n // len(firsts) // QP)
                        ],
                        axis=0,
                    )
                    for half, width in ((0, 128), (1, WP - 128))
                ],
                axis=1,
            )
            s = scores[h * n : (h + 1) * n] * scale + bias
            if key_mask is not None:
                s = s + key_mask
            s = s - jnp.max(s, axis=-1, keepdims=True)
            probs.append(jnp.exp2(s).astype(BF16))
        probs = jnp.concatenate(probs, axis=0)
        vt = v[:, tile : tile + width]
        mixed = dot(probs, jnp.concatenate([vt, jnp.ones((WP, width), BF16)], axis=1))
        top = mixed[:n, :width]
        total = mixed[:n, width:]
        for h in range(1, count):
            top = jnp.where(masks[h], mixed[h * n : (h + 1) * n, :width], top)
            total = jnp.where(masks[h], mixed[h * n : (h + 1) * n, width:], total)
        outs.append(top / total)
    return outs[0] if len(outs) == 1 else jnp.concatenate(outs, axis=1)


def gelu(x):
    return 0.5 * x * (1.0 + lax.erf(x * np.float32(0.5**0.5)))


def finish(x, context, gain, w_project, w_widen, w_narrow):
    middle = (x + dot(context, w_project)).astype(BF16).astype(F32)
    second = norm(middle, gain).astype(BF16)
    hidden = gelu(dot(second, w_widen)).astype(BF16)
    narrow = dot if w_narrow.shape[0] > w_narrow.shape[1] else dot_t
    return (middle + narrow(hidden, w_narrow)).astype(BF16)


def padded(heads):
    return -(-heads // 8) * 8


def window_order():
    token = lax.broadcasted_iota(jnp.int32, (WP, WIN_TOK), 1)
    level = jnp.where(token >= WIN_LAT * WIN_LON, 1, 0)
    token = token - level * (WIN_LAT * WIN_LON)
    row = sum(jnp.where(token >= WIN_LON * r, 1, 0) for r in range(1, WIN_LAT))
    col = token - row * WIN_LON
    down = jnp.where(row >= HALF_LAT, 1, 0)
    across = jnp.where(col >= HALF_LON, 1, 0)
    slot = (
        (2 * down + across) * QP
        + level * (HALF_LAT * HALF_LON)
        + (row - down * HALF_LAT) * HALF_LON
        + (col - across * HALF_LON)
    )
    place = lax.broadcasted_iota(jnp.int32, (WP, WIN_TOK), 0)
    return jnp.where(slot == place, 1.0, 0.0).astype(BF16)


def halved(heads):
    return heads % 8 == 4


def row_groups(head_counts):
    groups = []
    at = 0
    for heads in head_counts:
        count = padded(heads) // 8
        for g in range(count):
            groups.append((at + g * 8, 2 if halved(heads) and g == count - 1 else 1))
        at += padded(heads)
    return groups


def bias_kernel(*refs, picks, fresh):
    if fresh:
        index_ref, *table_refs, out_ref, index, table, left = refs
    else:
        index, *table_refs, out_ref, table, left = refs
    rows = table.shape[0]
    bias_len = table_refs[0].shape[-1]
    groups = row_groups([t.shape[0] for t in table_refs])

    @pl.when(pl.program_id(0) == 0)
    def _():
        if fresh:
            spread = window_order()
            plain = index_ref[...]
            high = (plain >> 4).astype(F32).astype(BF16)
            low = (plain & 15).astype(F32).astype(BF16)

            def moved(part):
                return dot_t(dot(spread, part).astype(BF16), spread).astype(jnp.int32)

            spot = lax.broadcasted_iota(jnp.int32, (WP, WP), 1) % QP
            index[...] = jnp.where(spot < QUAD, moved(high) * 16 + moved(low), bias_len)
        table[...] = jnp.full(table.shape, MASKED, F32)
        at = 0
        for table_ref, block in zip(table_refs, picks):
            heads = table_ref.shape[0]
            for h in range(heads):
                line = table_ref[h, block : block + 1, :] * LOG2E
                table[at + h : at + h + 1, :bias_len] = line
                if halved(heads) and h >= heads - 4:
                    table[at + h + 4 : at + h + 5, : bias_len - 256] = line[:, 256:]
            at += padded(heads)
        values = table[...]
        big = values.astype(BF16)
        small = (values - big.astype(F32)).astype(BF16)
        for n, part in enumerate((big, small)):
            left[:, n * 256 : (n + 1) * 256] = jnp.concatenate(
                [
                    part[row : row + 8, i * 256 : (i + 1) * 256]
                    for row, stride in groups
                    for i in range(0, LO_COUNT, stride)
                ],
                axis=0,
            )

    ladder = lax.broadcasted_iota(jnp.int32, (256, 256), 0).astype(F32).astype(BF16)
    lane = lax.broadcasted_iota(jnp.int32, (8, 256), 1) // 32
    sublane = lax.broadcasted_iota(jnp.int32, (8, 256), 0)
    low_half = lax.broadcasted_iota(jnp.int32, (8, 256), 0) // 4
    span = out_ref.shape[1] // rows
    for group in range(span // 8):
        first = pl.multiple_of(pl.program_id(0) * span + group * 8, 8)
        count = min(8, QUAD - group * 8)
        entries = index[pl.ds(first, 8), :]
        rest = jnp.concatenate([entries[:, 128:]] * 8, axis=1)
        rest = jnp.sum(jnp.where(lane == sublane, rest, 0).astype(F32), axis=0, keepdims=True)
        pieces = [
            jnp.concatenate([entries[j : j + 1, :128], entries[j + 1 : j + 2, :128]], axis=1)
            for j in range(0, count, 2)
        ] + [rest.astype(jnp.int32)]
        for t, entry in enumerate(pieces):
            near = (entry & 255).astype(F32).astype(BF16)
            far = entry >> 8
            chosen = jnp.where(ladder == near, jnp.ones((), BF16), jnp.zeros((), BF16))
            found = dot(left[...], jnp.concatenate([chosen, chosen], axis=0))
            shifted_far = far - low_half
            unit = 0
            for row, stride in groups:
                part = found[unit : unit + 8]
                unit += 8
                for i in range(stride, LO_COUNT, stride):
                    here = (far if stride == 1 else shifted_far) == i
                    part = jnp.where(here, found[unit : unit + 8], part)
                    unit += 8
                if stride == 2:
                    part = jnp.where((far & 1) == 0, part, pltpu.roll(part, 4, 0))
                at = row * span + group * 8
                if t < len(pieces) - 1:
                    for j in range(2):
                        out_ref[0, pl.ds(at + 2 * t + j, 8, stride=span), :] = (
                            part[:, j * 128 : (j + 1) * 128]
                        )
                else:
                    for j in range(count):
                        moved_part = part[:, j // 4 * 128 : (j // 4 + 1) * 128]
                        if j % 4:
                            moved_part = pltpu.roll(moved_part, 128 - 32 * (j % 4), 1)
                        out_ref[1, pl.ds(at + j, 8, stride=span), :] = moved_part
        for row, _ in groups:
            for j in range(count, 8):
                for half in range(2):
                    out_ref[half, pl.ds(row * span + group * 8 + j, 8, stride=span), :] = (
                        jnp.zeros((8, 128), F32)
                    )


def bias_of(picks, order, vmem, fresh=False, span=QP):
    tables = [t.transpose(1, 0, 2) for t, _ in picks]
    if fresh:
        order, tables = in_hbm(order), [in_hbm(t) for t in tables]
    rows = sum(padded(t.shape[0]) for t in tables)
    units = sum(-(-LO_COUNT // stride) for _, stride in row_groups([t.shape[0] for t in tables]))
    flops = 2 * WP * 256 * WP * units * 8 * 4
    steps = WP // span
    out_shape = [jax.ShapeDtypeStruct((2, steps * rows * span, 128), F32)]
    out_specs = [pl.BlockSpec((2, rows * span, 128), lambda i: (0, i, 0))]
    if fresh:
        out_shape.append(jax.ShapeDtypeStruct((WP, WP), jnp.int32))
        out_specs.append(pl.BlockSpec((WP, WP), lambda i: (0, 0)))
    out = pl.pallas_call(
        functools.partial(bias_kernel, picks=tuple(b for _, b in picks), fresh=fresh),
        out_shape=out_shape,
        grid=(steps,),
        in_specs=[pl.BlockSpec(memory_space=pltpu.VMEM)] * (1 + len(tables)),
        out_specs=out_specs,
        scratch_shapes=[
            pltpu.VMEM((rows, LO_COUNT * 256), F32),
            pltpu.VMEM((units * 8, 512), BF16),
        ],
        compiler_params=pltpu.CompilerParams(vmem_limit_bytes=vmem << 20),
        cost_estimate=pl.CostEstimate(flops=2 * flops, bytes_accessed=1 << 20, transcendentals=0),
        name="bias_table",
    )(order, *tables)
    return [out[0].reshape(2, steps, rows, span, 128)] + list(out[1:])


class Fetched:
    def __init__(self, copies):
        self.copies = copies
        for group in copies:
            for copy in group:
                copy.start()

    def wait(self, *numbers):
        for n in numbers:
            for copy in self.copies[n]:
                copy.wait()


def first_kernel(
    fields_ref, land_ref, embed_ref, order_ref, of_row_ref, of_col_ref, gains_ref,
    bias, triple_ref, project_ref, widen_ref, narrow_ref, out_ref, top_ref, bottom_ref, context,
):
    channels = fields_ref.shape[1]
    land = land_ref[...].astype(F32).astype(BF16)
    on_row = dot(of_row_ref[...], land)
    on_land = jnp.sum(on_row * of_col_ref[...].astype(F32), axis=-1, keepdims=True)
    rows = out_ref.shape[0]
    start = dot(sent_to(order_ref, rows), fields_ref[...]) + on_land * embed_ref[...]
    x = start.astype(BF16).astype(F32)
    normed = norm(x, gains_ref[0, 0:1]).astype(BF16)
    triple = dot(normed, triple_ref[0]).astype(BF16)
    inner = top_ref.shape[0]
    for a in range(rows // inner // 2):
        for b in range(inner // QP // 2):
            top = 2 * a * inner + 2 * b * QP
            below = top + inner
            window = jnp.concatenate(
                [triple[top : top + 2 * QP], triple[below : below + 2 * QP]], axis=0
            )
            mixed = attend(
                window[:, :channels],
                window[:, channels : 2 * channels],
                window[:, 2 * channels :],
                bias, [0], None,
            ).astype(BF16)
            context[top : top + 2 * QP] = mixed[: 2 * QP]
            context[below : below + 2 * QP] = mixed[2 * QP :]
    done = finish(
        x, context[...], gains_ref[0, 1:2], project_ref[0], widen_ref[0], narrow_ref[0]
    )
    out_ref[...] = done
    top_ref[...] = done[:inner]
    bottom_ref[...] = done[rows - inner :]


def shifted_block(
    own_ref, north_ref, south_ref, west_ref, east_ref, gains_ref, fetched,
    bias, w_triple, w_project, w_widen, w_narrow, query, key, value, context,
):
    channels = own_ref.shape[1]
    across = north_ref.shape[0] // QP
    down = own_ref.shape[0] // QP // across
    line = (across + 2) * QP
    inner = across * QP
    pieces = []
    for i in range(down + 2):
        if i == 0:
            middle = north_ref[...]
        elif i == down + 1:
            middle = south_ref[...]
        else:
            middle = own_ref[(i - 1) * inner : i * inner]
        pieces += [
            west_ref[i * QP : (i + 1) * QP].astype(F32),
            middle.astype(F32),
            east_ref[i * QP : (i + 1) * QP].astype(F32),
        ]
    normed = norm(jnp.concatenate(pieces, axis=0), gains_ref[1, 0:1]).astype(BF16)
    fetched.wait(0)
    query[...] = dot(normed[line : (down + 1) * line], w_triple[:, :channels])
    both = dot(normed, w_triple[:, channels:]).astype(BF16)
    key[...] = both[:, :channels]
    value[...] = both[:, channels:]
    lane = lax.broadcasted_iota(jnp.int32, (1, WP), 1)
    place = lax.axis_index("lat")
    on_top = jnp.where(place == 0, MASKED, 0.0).astype(F32)
    on_bottom = jnp.where(place == lax.axis_size("lat") - 1, MASKED, 0.0).astype(F32)
    for wa in range(down // 2 + 1):
        mask = None
        if wa == 0:
            mask = jnp.where(lane < 2 * QP, on_top, 0.0)
        elif wa == down // 2:
            mask = jnp.where(lane < 2 * QP, 0.0, on_bottom)
        for wb in range(across // 2 + 1):
            at = [(2 * wa + r) * line + 2 * wb * QP for r in range(2)]
            k = jnp.concatenate([key[s : s + 2 * QP] for s in at], axis=0)
            v = jnp.concatenate([value[s : s + 2 * QP] for s in at], axis=0)
            rows = [r for r in range(2) if 0 < 2 * wa + r < down + 1]
            cols = [c for c in range(2) if 0 < 2 * wb + c < across + 1]
            size = len(cols) * QP
            qs = [
                query[
                    (2 * wa + r - 1) * line + (2 * wb + cols[0]) * QP :
                    (2 * wa + r - 1) * line + (2 * wb + cols[0]) * QP + size
                ]
                for r in rows
            ]
            out = attend(
                jnp.concatenate(qs, axis=0).astype(BF16), k, v, bias,
                [(2 * r + cols[0]) * QP for r in rows], mask,
            )
            for n, r in enumerate(rows):
                to = ((2 * wa + r - 1) * across + 2 * wb + cols[0] - 1) * QP
                context[to : to + size] = out[n * size : (n + 1) * size]
    fetched.wait(1, 2, 3)
    return finish(
        own_ref[...].astype(F32), context[...].astype(BF16), gains_ref[1, 1:2],
        w_project[...], w_widen[...], w_narrow[...],
    )


def block_copies(pairs, block, sems, at):
    return [
        [pltpu.make_async_copy(source.at[block], target, sems.at[at + n])]
        for n, (source, target) in enumerate(pairs)
    ]


def middle_kernel(
    own_ref, north_ref, south_ref, west_ref, east_ref, gains_ref, merge_gain_ref,
    coarse_gains_ref, merge_order_ref, bias, c_bias, triple_ref, project_ref, widen_ref, narrow_ref,
    merge_weight_hbm, c_triple_hbm, c_project_hbm, c_widen_hbm, c_narrow_hbm,
    parts_ref, coarse_ref, top_ref, bottom_ref,
    query, key, value, context, merge_weight, c_triple, c_project, c_widen, c_narrow, sems,
):
    fetched = Fetched(
        [[]] * 4
        + [[pltpu.make_async_copy(merge_weight_hbm, merge_weight, sems.at[4])]]
        + block_copies(
            [(c_triple_hbm, c_triple), (c_project_hbm, c_project),
             (c_widen_hbm, c_widen), (c_narrow_hbm, c_narrow)], 0, sems, 5,
        )
    )
    w_triple, w_project, w_widen, w_narrow = (
        ref.at[1] for ref in (triple_ref, project_ref, widen_ref, narrow_ref)
    )
    skip = shifted_block(
        own_ref, north_ref, south_ref, west_ref, east_ref, gains_ref, fetched,
        bias, w_triple, w_project, w_widen, w_narrow, query, key, value, context,
    )
    channels = own_ref.shape[1]
    grouped = dot(sent_to(merge_order_ref, skip.shape[0]), skip)
    parts_ref[...] = grouped.astype(BF16)
    parts = [grouped[i * WP : (i + 1) * WP] for i in range(4)]
    width = 4 * channels
    mean = sum(jnp.sum(p, axis=-1, keepdims=True) for p in parts) / width
    parts = [p - mean for p in parts]
    variance = sum(jnp.sum(p * p, axis=-1, keepdims=True) for p in parts) / width
    factor = lax.rsqrt(variance + 1e-05)
    merge_gain = merge_gain_ref[...].reshape(1, width)
    fetched.wait(4)
    coarse = jnp.zeros((WP, merge_weight.shape[1]), F32)
    for i, p in enumerate(parts):
        gain = merge_gain[:, i * channels : (i + 1) * channels]
        merged = (p * factor * gain).astype(BF16)
        coarse = coarse + dot(merged, merge_weight[i * channels : (i + 1) * channels])
    x = coarse.astype(BF16).astype(F32)
    wide = x.shape[1]
    normed = norm(x, coarse_gains_ref[0, 0:1]).astype(BF16)
    fetched.wait(5)
    triple = dot(normed, c_triple[...]).astype(BF16)
    mixed = attend(
        triple[:, :wide], triple[:, wide : 2 * wide], triple[:, 2 * wide :], c_bias, [0], None
    ).astype(BF16)
    fetched.wait(6, 7, 8)
    done = finish(
        x, mixed, coarse_gains_ref[0, 1:2], c_project[...], c_widen[...], c_narrow[...]
    )
    coarse_ref[...] = done
    inner = top_ref.shape[0]
    top_ref[...] = done[:inner]
    bottom_ref[...] = done[WP - inner :]


def last_kernel(
    own_ref, north_ref, south_ref, west_ref, east_ref, gains_ref, parts_ref, expand_gain_ref,
    expand_order_ref, bias, triple_ref, project_ref, widen_ref, narrow_ref, expand_weight_ref,
    out_ref,
    query, key, value, context,
):
    fetched = Fetched([[]] * 4)
    w_triple, w_project, w_widen, w_narrow = (
        ref.at[1] for ref in (triple_ref, project_ref, widen_ref, narrow_ref)
    )
    deep = shifted_block(
        own_ref, north_ref, south_ref, west_ref, east_ref, gains_ref, fetched,
        bias, w_triple, w_project, w_widen, w_narrow, query, key, value, context,
    )
    channels = parts_ref.shape[1]
    widened = dot(deep, expand_weight_ref[...])
    outs = []
    for i in range(4):
        shuffled = widened[:, i * channels : (i + 1) * channels]
        skip = parts_ref[i * WP : (i + 1) * WP].astype(F32)
        outs.append((skip + norm(shuffled, expand_gain_ref[...])).astype(BF16))
    moves = sent_to(expand_order_ref, out_ref.shape[0])
    out_ref[...] = dot(moves, jnp.concatenate(outs, axis=0)).astype(BF16)


WHOLE = pl.BlockSpec(memory_space=pltpu.VMEM)
APART = pl.BlockSpec(memory_space=pltpu.HBM)


def in_hbm(array):
    return pltpu.with_memory_space_constraint(array, pltpu.HBM)


def weight_scratch(weights):
    return [pltpu.VMEM(w.shape[1:], BF16) for w in weights]


def halo(own, top, bottom, beside=None):
    rows, cols, _, channels = own.shape
    top = top.reshape(own.shape[1:])
    bottom = bottom.reshape(own.shape[1:])
    lat = lax.axis_size("lat")
    lon = lax.axis_size(LON)
    down = [(i, (i + 1) % lat) for i in range(lat)]
    up = [((i + 1) % lat, i) for i in range(lat)]
    east = [(i, (i + 1) % lon) for i in range(lon)]
    west = [((i + 1) % lon, i) for i in range(lon)]
    north = lax.ppermute(bottom, "lat", down)
    south = lax.ppermute(top, "lat", up)
    if beside is not None:
        north, south, beside = lax.optimization_barrier((north, south, beside))

    def side(c):
        return jnp.concatenate([north[c : c + 1], own[:, c], south[c : c + 1]], axis=0)

    from_west = lax.ppermute(side(cols - 1), LON, east)
    from_east = lax.ppermute(side(0), LON, west)
    halos = [v.reshape(-1, channels) for v in (own, north, south, from_west, from_east)]
    return halos if beside is None else (halos, beside)


def shifted_scratch(rows, cols, channels):
    line = (cols + 2) * QP
    return [
        pltpu.VMEM((rows * line, channels), F32),
        pltpu.VMEM(((rows + 2) * line, channels), BF16),
        pltpu.VMEM(((rows + 2) * line, channels), BF16),
        pltpu.VMEM((rows * cols * QP, channels), F32),
    ]


def on_device(
    fields, land_sea, land_embed, bias_index, fine_bias, fine_gains, fine_query_key_value,
    fine_project, fine_widen, fine_narrow, merge_gain, merge_weight, coarse_bias, coarse_gains,
    coarse_query_key_value, coarse_project, coarse_widen, coarse_narrow, expand_weight, expand_gain,
):
    _, rows, cols, channels = fields.shape
    quad_rows, quad_cols = rows // HALF_LAT, cols // HALF_LON
    tokens = quad_rows * quad_cols * QP
    wide = merge_weight.shape[1]
    order, of_row, of_col = fine_tables(rows, cols)
    bias_first, ordered = bias_of([(fine_bias, 0)], bias_index, 16, fresh=True)
    (bias_second,) = bias_of([(fine_bias, 1)], ordered, 16)
    (bias_third,) = bias_of([(coarse_bias, 0)], ordered, 16)
    (bias_last,) = bias_of([(coarse_bias, 1)], ordered, 16)
    fine_weights = (
        fine_query_key_value, fine_project, fine_widen, fine_narrow.transpose(0, 2, 1)
    )
    coarse_weights = (coarse_query_key_value, coarse_project, coarse_widen, coarse_narrow)
    dma = pltpu.SemaphoreType.DMA
    line = quad_cols * QP

    first, top, bottom = pl.pallas_call(
        first_kernel,
        out_shape=[
            jax.ShapeDtypeStruct((tokens, channels), BF16),
            jax.ShapeDtypeStruct((line, channels), BF16),
            jax.ShapeDtypeStruct((line, channels), BF16),
        ],
        in_specs=[WHOLE] * 12,
        out_specs=[WHOLE] * 3,
        scratch_shapes=[pltpu.VMEM((tokens, channels), BF16)],
        compiler_params=pltpu.CompilerParams(vmem_limit_bytes=20 << 20),
        name="fine_plain",
    )(
        fields.reshape(-1, channels), land_sea, land_embed[None], order, of_row, of_col,
        fine_gains, bias_first, *fine_weights,
    )

    halos, bias_second = halo(
        first.reshape(quad_rows, quad_cols, QP, channels), top, bottom, bias_second
    )
    parts, coarse, top, bottom = pl.pallas_call(
        middle_kernel,
        out_shape=[
            jax.ShapeDtypeStruct((tokens, channels), BF16),
            jax.ShapeDtypeStruct((tokens // 4, wide), BF16),
            jax.ShapeDtypeStruct((line // 2, wide), BF16),
            jax.ShapeDtypeStruct((line // 2, wide), BF16),
        ],
        in_specs=[WHOLE] * 15 + [APART] * 5,
        out_specs=[WHOLE] * 4,
        scratch_shapes=shifted_scratch(quad_rows, quad_cols, channels)
        + [pltpu.VMEM(merge_weight.shape, BF16)]
        + weight_scratch(coarse_weights) + [dma((9,))],
        compiler_params=pltpu.CompilerParams(vmem_limit_bytes=36 << 20),
        name="fine_shifted_coarse_plain",
    )(
        *halos, fine_gains, merge_gain, coarse_gains,
        merge_table(rows, cols), bias_second, bias_third,
        *fine_weights, in_hbm(merge_weight),
        *[in_hbm(w) for w in coarse_weights],
    )

    out = pl.pallas_call(
        last_kernel,
        out_shape=jax.ShapeDtypeStruct((LEVELS * rows * cols, channels), BF16),
        in_specs=[WHOLE] * 15,
        out_specs=WHOLE,
        scratch_shapes=shifted_scratch(quad_rows // 2, quad_cols // 2, wide),
        compiler_params=pltpu.CompilerParams(vmem_limit_bytes=28 << 20),
        name="coarse_shifted_expand",
    )(
        *halo(coarse.reshape(quad_rows // 2, quad_cols // 2, QP, wide), top, bottom),
        coarse_gains, parts, expand_gain[None], expand_table(rows, cols),
        bias_last, *coarse_weights, expand_weight,
    )
    return out.reshape(fields.shape)


def solution(mesh):
    grid = P(None, "lat", LON, None)
    return jax.shard_map(
        on_device,
        mesh=mesh,
        in_specs=(grid, P("lat", LON)) + (P(),) * 18,
        out_specs=grid,
        check_vma=False,
    )
```
